128 devices in a mesh: depth: 16 (over y, z_lo, core), azim: 8 (over z_hi, x).
Axes of the slice: x: 4, y: 4, z: 4 (z_hi: 2, z_lo: 2; z = z_hi * 2 + z_lo), core: 2. Of those that a mesh axis runs over, the one named last changes fastest.
Arguments:
- fluid_pos: float32 [2, 16, 32, 128], P(None, 'depth', 'azim'), may hold values from 0 to 1
- fluid_vel: float32 [2, 16, 32, 128], P(None, 'depth', 'azim'), may hold values from -4 to 4
- fluid_mass: float32 [16, 32, 128], P('depth', 'azim'), may hold values from 0.015 to 0.04
- cell_count: int32 [16, 32], P('depth', 'azim'), may hold values from 16 to 128
- nb_list: int32 [24, 16, 32, 128], P(None, 'depth', 'azim'), may hold values from 0 to 1151, as said below
- iface_dest: int32 [128, 512, 1], P(('depth', 'azim')), may hold values from 0 to 127; in each aligned block of 512 rows (0 to 511, 512 to 1023, ..., all dimensions but the last counted through in order) at most 10 rows name the same one
- iface_shell: int32 [128, 512], P(('depth', 'azim')), may hold values from 0 to 15
- soil_stress: float32 [4, 2048, 128], P(None, ('depth', 'azim')), may hold values from -6 to 6
- soil_rate: float32 [3, 2048, 128], P(None, ('depth', 'azim')), may hold values from -4 to 4
- soil_couple: float32 [3, 2048, 128], P(None, ('depth', 'azim')), may hold values from -30 to 30
Outputs:
- pos_out: float32 [2, 16, 32, 128], P(None, 'depth', 'azim')
- vel_out: float32 [2, 16, 32, 128], P(None, 'depth', 'azim')
- rho_out: float32 [16, 32, 128], P('depth', 'azim')
- stress_out: float32 [4, 2048, 128], P(None, ('depth', 'azim'))
The draws below stay inside these ranges and needn't reach their ends.
Inputs may be any that keep to these rules, and one draw needn't show every extreme that they name: A cell's live particles fill its slots 0 to cell_count - 1. `nb_list`: entry nb * 128 + s names slot s of the cell at offset (nb // 3 - 1, nb % 3 - 1) in (depth, azimuth) cells, never the particle itself; entries may repeat or name empty slots. `iface_dest`: among the 512 interface slots of one device at most 10 name the same owner.
All inputs are finite; a program needn't handle non-finite values.
Results may differ from the reference program's by a relative error of at most 0.0003.
Values sent between devices are 32-bit elements; how exact they have to be, the bound alone decides.
No kernel may reach another device: no remote copies, remote signals or barrier semaphores. Data moves between devices by JAX's collectives and lax.ppermute only.
A program may use at most 64 MiB of HBM per device.

```python
import math
import jax
import jax.numpy as jnp
import numpy as np
from jax import lax

S = 128
CD = 1
CA = 4
NB = 24
FSTEPS = 2
SH_DEV = 16
PS = 128
ND = 16
NA = 32
IR = 512
CAP = 10
SHELLS = 2048
N_DEPTH = 16
N_AZIM = 8
DEVICES = 128


def draw_nb_list(key, part):
    key_cell, key_slot = jax.random.split(jax.random.fold_in(key, 17))
    shape = (NB, ND, NA, S)
    cell = jax.random.randint(key_cell, shape, 0, 9, dtype=jnp.int32)
    slot = jax.random.randint(key_slot, shape, 0, S, dtype=jnp.int32)
    own = jnp.arange(S, dtype=jnp.int32)[None, None, None, :]
    slot = jnp.where((cell == 4) & (slot == own), (slot + 1) % S, slot)
    return cell * S + slot


def touch_ends(entries, stream_key, least, largest):
    place = [jax.random.randint(jax.random.fold_in(stream_key, axis), (), 0, length) for axis, length in enumerate(entries.shape)]
    main_axis = entries.shape.index(max(entries.shape))
    beside = place[:main_axis] + [(place[main_axis] + 1) % entries.shape[main_axis]] + place[main_axis + 1:]
    return entries.at[tuple(place)].set(least).at[tuple(beside)].set(largest)


def shard_levels(key, dims, cuts, low, high):
    gain = 1.0
    for dim, parts in cuts:
        steps = jax.random.uniform(jax.random.fold_in(jax.random.fold_in(key, 6), dim), (parts,), jnp.float32, low / len(cuts), high / len(cuts))
        gain = gain * jnp.repeat(jnp.exp(steps), dims[dim] // parts).reshape((-1,) + (1,) * (len(dims) - 1 - dim))
    return gain


def deal_out(own_key, own, number, rows, amount, top, reach, skew):
    sequence = jax.random.permutation(own_key, amount)
    packed, usual = load_shares(amount, rows * top, reach, skew, True), load_shares(amount, rows * top, reach, skew, False)
    places = jnp.arange(amount)

    def named(tallies, turn):
        used = int((tallies > 0).sum())
        fixed = max(1, used // 4)
        moved = fixed + (places - fixed + turn * (used - fixed)) % max(1, amount - fixed)
        return jnp.zeros((amount,), jnp.int32).at[sequence[jnp.where(places < fixed, places, moved)]].set(jnp.asarray(tallies, jnp.int32))

    tallies = jnp.where(number % 4 == 0, named(packed, number // 4), named(usual, number - number // 4 - 1))
    mixed = jax.random.permutation(jax.random.fold_in(own, 3), amount)
    source_of, receiver = mixed[0:amount // 2 * 2:2], mixed[1:amount // 2 * 2:2]
    margin = jnp.minimum(tallies[source_of] - 1, reach - tallies[receiver]) // 2
    margin = jnp.where((source_of == sequence[0]) | (receiver == sequence[0]) | (tallies[receiver] == 0), 0, jnp.maximum(margin, 0))
    moved = jax.random.randint(jax.random.fold_in(own, 4), (amount // 2,), 0, 1 << 20) % (margin + 1)
    tallies = tallies.at[source_of].add(-moved).at[receiver].add(moved)
    labels = jnp.searchsorted(jnp.cumsum(tallies), jnp.arange(rows * top), side="right").astype(jnp.int32)
    listing = labels.reshape(top, rows).T
    listing = listing[jax.random.permutation(jax.random.fold_in(own, 1), rows)]
    turn = jax.random.randint(jax.random.fold_in(own, 2), (rows, 1), 0, top)
    return jnp.take_along_axis(listing, (jnp.arange(top)[None, :] + turn) % top, axis=1)


def load_shares(number_of, total, bound, skew, full):
    weights = [(1 << 20) // math.isqrt(rank ** skew) + 1 for rank in range(1, number_of + 1)]
    largest = bound if full else min(bound, max(-(-total // number_of), total * weights[0] // sum(weights)))
    least = 1 if total - largest >= number_of - 1 else 0
    counts, surplus = [largest] + [least] * (number_of - 1), total - largest - least * (number_of - 1)
    while surplus > 0:
        free = [i for i in range(1, number_of) if counts[i] < largest] or [i for i in range(1, number_of) if counts[i] < bound]
        whole, budget = sum([weights[i] for i in free]), surplus
        for i in free:
            addition = min(bound - counts[i], max(1, budget * weights[i] // whole), surplus)
            counts[i] = counts[i] + addition
            surplus = surplus - addition
    return np.array(counts)


def scatter_about(stream_key, extent, spread, limit, cuts=(), kind=jnp.bfloat16):
    level = shard_levels(stream_key, extent, cuts, -0.22, 0.18) if cuts else 1.0
    entries = jax.random.normal(stream_key, extent, jnp.float32) * spread * level
    return jnp.minimum(jnp.maximum(entries, -limit), limit).astype(kind)


def setup_inputs(seed: int = 0) -> dict:
    seeds = jax.random.split(jax.random.key(seed), 11)
    fluid_pos = jnp.clip(1.0 * jax.random.uniform(seeds[0], (2, ND, NA, S), jnp.float32) ** shard_levels(seeds[0], (2, ND, NA, S), ((1, 16), (2, 8)), -0.2, 0.2), 0.0, 1.0)
    fluid_vel = scatter_about(seeds[1], (2, ND, NA, S), 1.0, 4.0, ((1, 16), (2, 8)), jnp.float32)
    fluid_mass = jnp.clip(jnp.exp(math.log(0.04) - 0.98082925 * jax.random.uniform(seeds[2], (ND, NA, S), jnp.float32) ** shard_levels(seeds[2], (ND, NA, S), ((0, 16), (1, 8)), -0.2, 0.2)), 0.015, 0.04)
    cell_count = touch_ends(jax.random.randint(seeds[3], (ND, NA), 16, S + 1), jax.random.fold_in(seeds[3], 1), 16, S).astype(jnp.int32)
    nb_list = draw_nb_list(jax.random.fold_in(seeds[10], 71), 0)
    iface_dest_keys = jax.random.split(jax.random.fold_in(seeds[5], 1), DEVICES * IR // IR)
    iface_dest_turns = jax.random.permutation(jax.random.fold_in(seeds[5], 3), DEVICES * IR // IR)
    iface_dest = jax.vmap(lambda own, number: deal_out(jax.random.fold_in(seeds[5], 2), own, number, IR, DEVICES, 1, CAP, 2))(iface_dest_keys, iface_dest_turns).reshape((DEVICES, IR, 1))
    iface_shell = touch_ends(jax.random.randint(seeds[6], (DEVICES, IR), 0, SH_DEV), jax.random.fold_in(seeds[6], 1), 0, SH_DEV - 1).astype(jnp.int32)
    soil_stress = scatter_about(seeds[7], (4, SHELLS, PS), 1.0, 6.0, ((1, 128),), jnp.float32)
    soil_rate = scatter_about(seeds[8], (3, SHELLS, PS), 0.5, 4.0, ((1, 128),), jnp.float32)
    soil_couple = scatter_about(seeds[9], (3, SHELLS, PS), 5.0, 30.0, ((1, 128),), jnp.float32)
    return {"fluid_pos": fluid_pos, "fluid_vel": fluid_vel, "fluid_mass": fluid_mass, "cell_count": cell_count, "nb_list": nb_list, "iface_dest": iface_dest, "iface_shell": iface_shell, "soil_stress": soil_stress, "soil_rate": soil_rate, "soil_couple": soil_couple}


step_dt = 0.05
sound_sq = 1.0
visc_alpha = 0.5
soil_dt = 0.1
shear_mod = 1.0
bulk_mod = 2.0
cohesion = 1.0
friction = 0.3

def extend_grid(field):
    padded = jnp.pad(field, ((0, 0), (1, 1), (0, 0), (0, 0)))
    return jnp.concatenate([padded[:, :, -1:], padded, padded[:, :, :1]], axis=2)

def pair_index(codes, width_ext, slots):
    cell_code = codes // slots
    slot = codes - cell_code * slots
    row_off = cell_code // 3
    col_off = cell_code - row_off * 3
    cols = jnp.arange(codes.shape[1], dtype=jnp.int32)[None, :, None]
    index = (row_off * width_ext + cols + col_off) * slots + slot
    return (index, (row_off - 1).astype(jnp.float32), (col_off - 1).astype(jnp.float32))

def pair_geometry(own, near, off_r, off_c):
    dx = own[0][None] - (off_r + near[0])
    dy = own[1][None] - (off_c + near[1])
    dist = jnp.sqrt(dx * dx + dy * dy)
    tail = jnp.maximum(1.0 - dist, 0.0)
    return (dx, dy, dist, tail)

def density_row(state3, codes_row):
    slots = state3.shape[3]
    index, off_r, off_c = pair_index(codes_row, state3.shape[2], slots)
    flat = state3[:3].reshape(3, -1)
    near = jnp.take(flat, index, axis=1)
    own = state3[:3, 1, 1:-1]
    dx, dy, dist, tail = pair_geometry(own, near, off_r, off_c)
    kern = tail * tail * tail * tail * (4.0 * dist + 1.0)
    mass = own[2]
    return mass + lax.optimization_barrier(jnp.sum(near[2] * kern, axis=0)) + jnp.where(mass > 0.0, 0.0, 1.0)

def force_row(state3, press3, codes_row):
    slots = state3.shape[3]
    index, off_r, off_c = pair_index(codes_row, state3.shape[2], slots)
    near = jnp.take(state3.reshape(state3.shape[0], -1), index, axis=1)
    near_p = jnp.take(press3.reshape(press3.shape[0], -1), index, axis=1)
    own = state3[:, 1, 1:-1]
    own_p = press3[:, 1, 1:-1]
    dx, dy, dist, tail = pair_geometry(own, near, off_r, off_c)
    vdot = (own[3][None] - near[3]) * dx + (own[4][None] - near[4]) * dy
    visc = visc_alpha * jnp.maximum(-vdot, 0.0) / (dist * dist + 0.01) / (0.5 * (own_p[1][None] + near_p[1]))
    coef = near[2] * (own_p[0][None] + near_p[0] + visc) * (20.0 * tail * tail * tail)
    return jnp.stack([lax.optimization_barrier(jnp.sum(coef * dx, axis=0)), lax.optimization_barrier(jnp.sum(coef * dy, axis=0))])

def sweep_density(state_ext, codes):

    def one_row(row):
        part = lax.dynamic_slice_in_dim(state_ext, row, 3, 1)
        return density_row(part, lax.dynamic_index_in_dim(codes, row, 1, keepdims=False))
    return lax.map(one_row, jnp.arange(codes.shape[1], dtype=jnp.int32))

def sweep_force(state_ext, press_ext, codes):

    def one_row(row):
        part = lax.dynamic_slice_in_dim(state_ext, row, 3, 1)
        part_p = lax.dynamic_slice_in_dim(press_ext, row, 3, 1)
        return force_row(part, part_p, lax.dynamic_index_in_dim(codes, row, 1, keepdims=False))
    return jnp.moveaxis(lax.map(one_row, jnp.arange(codes.shape[1], dtype=jnp.int32)), 0, 1)

def soil_step(stress, rate, couple, loads):
    force_x = loads[0][:, None]
    force_y = loads[1][:, None]
    force_p = loads[2][:, None]
    force_e = loads[3][:, None]
    exx = rate[0] + couple[0] * force_x
    eyy = rate[1] + couple[1] * force_y
    exy = rate[2] + couple[2] * force_p
    ezz = -0.5 * (couple[0] + couple[1]) * force_e
    trace = exx + eyy + ezz
    sxx = stress[0] + soil_dt * (2.0 * shear_mod * (exx - trace / 3.0) + bulk_mod * trace)
    syy = stress[1] + soil_dt * (2.0 * shear_mod * (eyy - trace / 3.0) + bulk_mod * trace)
    szz = stress[2] + soil_dt * (2.0 * shear_mod * (ezz - trace / 3.0) + bulk_mod * trace)
    sxy = stress[3] + soil_dt * 2.0 * shear_mod * exy
    first = sxx + syy + szz
    mean = first / 3.0
    dxx = sxx - mean
    dyy = syy - mean
    dzz = szz - mean
    root = jnp.sqrt(0.5 * (dxx * dxx + dyy * dyy + dzz * dzz) + sxy * sxy)
    radius = jnp.maximum(cohesion - friction * first, 0.2 * cohesion)
    factor = radius / jnp.maximum(root, radius)
    return jnp.stack([mean + factor * dxx, mean + factor * dyy, mean + factor * dzz, factor * sxy])

def reference(fluid_pos, fluid_vel, fluid_mass, cell_count, nb_list, iface_dest, iface_shell, soil_stress, soil_rate, soil_couple):
    slots = fluid_pos.shape[3]
    live = (jnp.arange(slots, dtype=jnp.int32)[None, None, :] < cell_count[:, :, None]).astype(jnp.float32)
    mass = fluid_mass * live
    pos = fluid_pos
    vel = fluid_vel
    rho = mass
    press = mass
    for step in range(FSTEPS):
        state = jnp.concatenate([pos, mass[None], vel], axis=0)
        state_ext = extend_grid(state)
        rho = sweep_density(state_ext, nb_list)
        press = sound_sq * (rho - 1.0)
        qterm = press / (rho * rho)
        press_ext = extend_grid(jnp.stack([qterm, rho]))
        acc = sweep_force(state_ext, press_ext, nb_list)
        vel = vel + step_dt * acc * live[None]
        pos = pos + step_dt * vel * live[None]
    load = jnp.stack([mass * vel[0], mass * vel[1], mass * press, 0.5 * mass * (vel[0] * vel[0] + vel[1] * vel[1])])
    load = load[:, CD - 1::CD]
    load = load.reshape(4, N_DEPTH, N_AZIM, CA * slots).reshape(4, -1)
    shell_id = (iface_dest[:, :, 0] * SH_DEV + iface_shell).reshape(-1)
    shell_load = jax.ops.segment_sum(load.T, shell_id, num_segments=SHELLS).T
    stress_out = soil_step(soil_stress, soil_rate, soil_couple, shell_load)
    return (pos, vel, rho, stress_out)
```

```python
import jax
import jax.numpy as jnp
from jax import lax
from jax.experimental import pallas as pl
from jax.experimental.pallas import tpu as pltpu
from jax.sharding import PartitionSpec as P

step_dt = 0.05
sound_sq = 1.0
visc_alpha = 0.5
soil_dt = 0.1
shear_mod = 1.0
bulk_mod = 2.0
cohesion = 1.0
friction = 0.3

CELLS = 4
NB = 24
NT = 3
WIDE = 8
RING = 6
S = 128
PX, PY, PM, PVX, PVY, PL = range(6)


def pack_kernel(count, pos, vel, mass, nb, out):
    lane = lax.broadcasted_iota(jnp.int32, (1, S), 1)
    for c in range(CELLS):
        live = (lane < count[0, c]).astype(jnp.float32)
        out[8 * c + PX : 8 * c + PX + 1, :] = pos[c : c + 1, :]
        out[8 * c + PY : 8 * c + PY + 1, :] = pos[CELLS + c : CELLS + c + 1, :]
        out[8 * c + PM : 8 * c + PM + 1, :] = mass[c : c + 1, :] * live
        out[8 * c + PVX : 8 * c + PVX + 1, :] = vel[c : c + 1, :]
        out[8 * c + PVY : 8 * c + PVY + 1, :] = vel[CELLS + c : CELLS + c + 1, :]
        out[8 * c + PL : 8 * c + PL + 1, :] = live
        out[8 * c + PL + 1 : 8 * c + 8, :] = jnp.zeros((2, S), jnp.float32)
        base = 8 * CELLS + NB * c
        out[base : base + NB, :] = nb[pl.ds(c, NB, stride=CELLS), :].astype(jnp.float32)


def spread(row):
    return jnp.broadcast_to(row, (8, S))


def pick(tables, slot, masks):
    out = None
    for table, mask in zip(tables, masks):
        got = jnp.take_along_axis(table, slot, axis=1)
        out = got if out is None else jnp.where(mask, got, out)
    return out


def step_body(sign, frame, lists, pair, press):
    def number(dr, dc):
        return 3 * (1 + sign * dr) + dc + 1

    near = [(dr, dc) for dr in (-1, 0, 1) for dc in (-1, 0, 1)]

    def density(cell, carry):
        row = cell // RING
        col = cell - row * RING
        centre = ((row + 1) * WIDE + col + 1) * 8
        own = frame[pl.ds(pl.multiple_of(centre, 8), 8), :]
        own_x, own_y = spread(own[PX : PX + 1]), spread(own[PY : PY + 1])
        own_m = own[PM : PM + 1]
        xs, ys, ms = [], [], []
        for dr, dc in near:
            tile = frame[pl.ds(pl.multiple_of(centre + (dr * WIDE + dc) * 8, 8), 8), :]
            xs.append(spread(tile[PX : PX + 1] + (sign * dr).astype(jnp.float32)))
            ys.append(spread(tile[PY : PY + 1] + float(dc)))
            ms.append(spread(tile[PM : PM + 1]))
        total = jnp.zeros((8, S), jnp.float32)
        for t in range(NT):
            code = lists[pl.ds(pl.multiple_of(cell * NB + 8 * t, 8), 8), :].astype(jnp.int32)
            slot = code & (S - 1)
            which = code >> 7
            masks = [which == number(dr, dc) for dr, dc in near]
            dx = own_x - pick(xs, slot, masks)
            dy = own_y - pick(ys, slot, masks)
            mass = pick(ms, slot, masks)
            dist = jnp.sqrt(dx * dx + dy * dy)
            tail = jnp.maximum(1.0 - dist, 0.0)
            cube = tail * tail * tail
            total = total + mass * (cube * tail * (4.0 * dist + 1.0))
            base = pl.multiple_of((cell * NT + t) * 40, 8)
            pair[pl.ds(base, 8), :] = dx
            pair[pl.ds(base + 8, 8), :] = dy
            pair[pl.ds(base + 16, 8), :] = mass
            pair[pl.ds(base + 24, 8), :] = dist * dist + 0.01
            pair[pl.ds(base + 32, 8), :] = 20.0 * cube
        rho = own_m + jnp.sum(total, axis=0, keepdims=True) + jnp.where(own_m > 0.0, 0.0, 1.0)
        q = sound_sq * (rho - 1.0) / (rho * rho)
        base = pl.multiple_of(cell * 8, 8)
        press[pl.ds(base, 1), :] = q
        press[pl.ds(base + 1, 1), :] = rho
        return carry

    lax.fori_loop(0, 3 * RING, density, 0)

    def force(c, carry):
        cell = RING + 1 + c
        centre = (2 * WIDE + 2 + c) * 8
        own = frame[pl.ds(pl.multiple_of(centre, 8), 8), :]
        own_p = press[pl.ds(pl.multiple_of(cell * 8, 8), 8), :]
        own_vx, own_vy = spread(own[PVX : PVX + 1]), spread(own[PVY : PVY + 1])
        own_q, own_rho = spread(own_p[0:1]), spread(own_p[1:2])
        vxs, vys, qs, rhos = [], [], [], []
        for dr, dc in near:
            tile = frame[pl.ds(pl.multiple_of(centre + (dr * WIDE + dc) * 8, 8), 8), :]
            ptile = press[pl.ds(pl.multiple_of((cell + dr * RING + dc) * 8, 8), 8), :]
            vxs.append(spread(tile[PVX : PVX + 1]))
            vys.append(spread(tile[PVY : PVY + 1]))
            qs.append(spread(ptile[0:1]))
            rhos.append(spread(ptile[1:2]))
        ax = jnp.zeros((8, S), jnp.float32)
        ay = jnp.zeros((8, S), jnp.float32)
        for t in range(NT):
            code = lists[pl.ds(pl.multiple_of(cell * NB + 8 * t, 8), 8), :].astype(jnp.int32)
            slot = code & (S - 1)
            which = code >> 7
            masks = [which == number(dr, dc) for dr, dc in near]
            base = pl.multiple_of((cell * NT + t) * 40, 8)
            dx = pair[pl.ds(base, 8), :]
            dy = pair[pl.ds(base + 8, 8), :]
            mass = pair[pl.ds(base + 16, 8), :]
            soft = pair[pl.ds(base + 24, 8), :]
            slope = pair[pl.ds(base + 32, 8), :]
            vdot = (own_vx - pick(vxs, slot, masks)) * dx + (own_vy - pick(vys, slot, masks)) * dy
            visc = visc_alpha * jnp.maximum(-vdot, 0.0) / (soft * (0.5 * (own_rho + pick(rhos, slot, masks))))
            coef = mass * (own_q + pick(qs, slot, masks) + visc) * slope
            ax = ax + coef * dx
            ay = ay + coef * dy
        live = own[PL : PL + 1]
        vx = own[PVX : PVX + 1] + step_dt * jnp.sum(ax, axis=0, keepdims=True) * live
        vy = own[PVY : PVY + 1] + step_dt * jnp.sum(ay, axis=0, keepdims=True) * live
        x = own[PX : PX + 1] + step_dt * vx * live
        y = own[PY : PY + 1] + step_dt * vy * live
        return x, y, own[PM : PM + 1], vx, vy, live, own_p[1:2]

    return force


def first_kernel(parity, q0, q1, q2, q3, q4, out, frame, lists, pair, press):
    sign = 1 - 2 * parity[0]
    half = 8 * CELLS
    rows = {0: q0, 1: q3, -1: q4, 2: q1}
    right = half + CELLS * NB
    for r, ref in rows.items():
        base = (r + 2) * WIDE * 8
        frame[base : base + half, :] = ref[0:half, :]
        frame[base + half : base + 2 * half, :] = ref[right : right + half, :]
    frame[0 : 2 * half, :] = q2[...]
    for r in (-1, 0, 1):
        ref = rows[r]
        base = (r + 1) * RING * NB
        lists[base : base + 3 * NB, :] = ref[half + NB : half + 4 * NB, :]
        lists[base + 3 * NB : base + 6 * NB, :] = ref[right + half : right + half + 3 * NB, :]
        out[half + (r + 1) * NB : half + (r + 2) * NB, :] = ref[half + 3 * NB : half + 4 * NB, :]
    force = step_body(sign, frame, lists, pair, press)
    for c in range(CELLS):
        x, y, m, vx, vy, live, _ = force(c, 0)
        for k, v in enumerate((x, y, m, vx, vy, live)):
            out[8 * c + k : 8 * c + k + 1, :] = v
        out[8 * c + 6 : 8 * c + 8, :] = jnp.zeros((2, S), jnp.float32)


def second_kernel(parity, dest, shell, left, r0, r1, r2, r3, r4, q0, q3, q4, pos_out, vel_out, rho_out, part, frame, lists, pair, press):
    sign = 1 - 2 * parity[0]
    half = 8 * CELLS
    right = half + CELLS * NB
    for r, ref in {0: r0, 2: r1, -2: r2, 1: r3, -1: r4}.items():
        base = (r + 2) * WIDE * 8
        frame[base : base + 2 * half, :] = ref[...]
    for r, ref in {-1: q4, 0: q0, 1: q3}.items():
        base = (r + 1) * RING * NB
        lists[base : base + NB, :] = left[half + (r + 1) * NB : half + (r + 2) * NB, :]
        lists[base + NB : base + 5 * NB, :] = ref[half : half + 4 * NB, :]
        lists[base + 5 * NB : base + 6 * NB, :] = ref[right + half : right + half + NB, :]
    force = step_body(sign, frame, lists, pair, press)
    total = jnp.zeros((S, S), jnp.float32)
    devices = lax.broadcasted_iota(jnp.int32, (S, S), 0)
    shells = lax.broadcasted_iota(jnp.int32, (16, S), 0)
    for c in range(CELLS):
        x, y, m, vx, vy, live, rho = force(c, 0)
        pos_out[c : c + 1, :] = x
        pos_out[CELLS + c : CELLS + c + 1, :] = y
        vel_out[c : c + 1, :] = vx
        vel_out[CELLS + c : CELLS + c + 1, :] = vy
        rho_out[c : c + 1, :] = rho
        loads = (m * vx, m * vy, m * (sound_sq * (rho - 1.0)), 0.5 * m * (vx * vx + vy * vy))
        owner = (devices == dest[c : c + 1, :]).astype(jnp.float32)
        member = shells == shell[c : c + 1, :]
        spreads = [jnp.where(member, load, 0.0) for load in loads]
        spreads.append(jnp.zeros((S - 64, S), jnp.float32))
        total = total + lax.dot_general(
            owner,
            jnp.concatenate(spreads, axis=0),
            (((1,), (1,)), ((), ())),
            precision=lax.Precision.HIGHEST,
            preferred_element_type=jnp.float32,
        )
    part[...] = total


def soil_kernel(arrived, stress, rate, couple, out):
    total = jnp.sum(arrived[...], axis=0, keepdims=True)
    lane = lax.broadcasted_iota(jnp.int32, (16, S), 1)
    row = lax.broadcasted_iota(jnp.int32, (16, S), 0)
    force_x, force_y, force_p, force_e = [
        jnp.sum(jnp.where(lane == row + 16 * k, total, 0.0), axis=1, keepdims=True) for k in range(4)
    ]
    exx = rate[0] + couple[0] * force_x
    eyy = rate[1] + couple[1] * force_y
    exy = rate[2] + couple[2] * force_p
    ezz = -0.5 * (couple[0] + couple[1]) * force_e
    trace = exx + eyy + ezz
    sxx = stress[0] + soil_dt * (2.0 * shear_mod * (exx - trace / 3.0) + bulk_mod * trace)
    syy = stress[1] + soil_dt * (2.0 * shear_mod * (eyy - trace / 3.0) + bulk_mod * trace)
    szz = stress[2] + soil_dt * (2.0 * shear_mod * (ezz - trace / 3.0) + bulk_mod * trace)
    sxy = stress[3] + soil_dt * 2.0 * shear_mod * exy
    first = sxx + syy + szz
    mean = first / 3.0
    dxx = sxx - mean
    dyy = syy - mean
    dzz = szz - mean
    root = jnp.sqrt(0.5 * (dxx * dxx + dyy * dyy + dzz * dzz) + sxy * sxy)
    radius = jnp.maximum(cohesion - friction * first, 0.2 * cohesion)
    factor = radius / jnp.maximum(root, radius)
    out[0] = mean + factor * dxx
    out[1] = mean + factor * dyy
    out[2] = mean + factor * dzz
    out[3] = factor * sxy


def rows_of(n):
    return jax.ShapeDtypeStruct((n, S), jnp.float32)


VM = pl.BlockSpec(memory_space=pltpu.MemorySpace.VMEM)
SM = pl.BlockSpec(memory_space=pltpu.MemorySpace.SMEM)
WORK = [
    pltpu.VMEM((5 * WIDE * 8, S), jnp.float32),
    pltpu.VMEM((3 * RING * NB, S), jnp.float32),
    pltpu.VMEM((3 * RING * NT * 40, S), jnp.float32),
    pltpu.VMEM((3 * RING * 8, S), jnp.float32),
]


def local(
    fluid_pos,
    fluid_vel,
    fluid_mass,
    cell_count,
    nb_list,
    iface_dest,
    iface_shell,
    soil_stress,
    soil_rate,
    soil_couple,
):
    n_depth = lax.axis_size("depth")
    n_azim = lax.axis_size("azim")
    parity = (lax.axis_index("depth") % 2).astype(jnp.int32).reshape(1)
    toward_left = [(i, (i - 1) % n_azim) for i in range(n_azim)]
    toward_right = [(i, (i + 1) % n_azim) for i in range(n_azim)]
    pairs = [(i, i ^ 1) for i in range(n_depth)]
    far = [(i, i + 2 if i % 2 else i - 2) for i in range(n_depth)]
    far = [(i, j) for i, j in far if 0 <= j < n_depth]
    back = [(j, i) for i, j in far]
    half = 8 * CELLS

    own = pl.pallas_call(
        pack_kernel,
        out_shape=rows_of(half + CELLS * NB),
        in_specs=[SM, VM, VM, VM, VM],
        out_specs=VM,
        name="pack",
    )(
        cell_count,
        fluid_pos.reshape(2 * CELLS, S),
        fluid_vel.reshape(2 * CELLS, S),
        fluid_mass.reshape(CELLS, S),
        nb_list.reshape(NB * CELLS, S),
    )
    right = lax.ppermute(own, "azim", toward_left)
    q0 = jnp.concatenate([own, right[: half + 3 * NB]], axis=0)
    state = jnp.concatenate([own[:half], right[:half]], axis=0)
    q1 = lax.ppermute(q0, "depth", far)
    q2 = lax.ppermute(state, "depth", back)
    q3 = lax.ppermute(q0, "depth", pairs)
    q4 = lax.ppermute(q1, "depth", pairs)
    mid = pl.pallas_call(
        first_kernel,
        out_shape=rows_of(half + 3 * NB),
        in_specs=[SM] + [VM] * 5,
        out_specs=VM,
        scratch_shapes=WORK,
        name="first_step",
    )(parity, q0, q1, q2, q3, q4)

    left = lax.ppermute(mid, "azim", toward_right)
    r0 = jnp.concatenate([left[:half], mid[:half]], axis=0)
    r1 = lax.ppermute(r0, "depth", far)
    r2 = lax.ppermute(r0, "depth", back)
    r3 = lax.ppermute(r0, "depth", pairs)
    r4 = lax.ppermute(r1, "depth", pairs)
    pos, vel, rho, part = pl.pallas_call(
        second_kernel,
        out_shape=(rows_of(2 * CELLS), rows_of(2 * CELLS), rows_of(CELLS), rows_of(S)),
        in_specs=[SM] + [VM] * 11,
        out_specs=(VM, VM, VM, VM),
        scratch_shapes=WORK,
        name="second_step",
    )(parity, iface_dest.reshape(CELLS, S), iface_shell.reshape(CELLS, S), left, r0, r1, r2, r3, r4, q0, q3, q4)

    arrived = lax.all_to_all(part, ("depth", "azim"), split_axis=0, concat_axis=0, tiled=True)
    stress_out = pl.pallas_call(
        soil_kernel,
        out_shape=jax.ShapeDtypeStruct(soil_stress.shape, jnp.float32),
        in_specs=[VM] * 4,
        out_specs=VM,
        name="soil",
    )(arrived, soil_stress, soil_rate, soil_couple)
    return (
        pos.reshape(fluid_pos.shape),
        vel.reshape(fluid_vel.shape),
        rho.reshape(fluid_mass.shape),
        stress_out,
    )


def solution(mesh):
    return jax.shard_map(
        local,
        mesh=mesh,
        in_specs=(
            P(None, "depth", "azim", None),
            P(None, "depth", "azim", None),
            P("depth", "azim", None),
            P("depth", "azim"),
            P(None, "depth", "azim", None),
            P(("depth", "azim"), None, None),
            P(("depth", "azim"), None),
            P(None, ("depth", "azim"), None),
            P(None, ("depth", "azim"), None),
            P(None, ("depth", "azim"), None),
        ),
        out_specs=(
            P(None, "depth", "azim", None),
            P(None, "depth", "azim", None),
            P("depth", "azim", None),
            P(None, ("depth", "azim"), None),
        ),
        check_vma=False,
    )
```

```python
import jax
import jax.numpy as jnp
from jax import lax
from jax.experimental import pallas as pl
from jax.experimental.pallas import tpu as pltpu
from jax.sharding import PartitionSpec as P

step_dt = 0.05
sound_sq = 1.0
visc_alpha = 0.5
soil_dt = 0.1
shear_mod = 1.0
bulk_mod = 2.0
cohesion = 1.0
friction = 0.3

CELLS = 4
NB = 24
NT = 3
WIDE = 8
RING = 6
S = 128
PX, PY, PM, PVX, PVY, PL = range(6)


def pack_kernel(count, pos, vel, mass, nb, out):
    lane = lax.broadcasted_iota(jnp.int32, (1, S), 1)
    for c in range(CELLS):
        live = (lane < count[0, c]).astype(jnp.float32)
        out[NB * c : NB * c + NB, :] = nb[pl.ds(c, NB, stride=CELLS), :].astype(jnp.float32)
        base = NB * CELLS + 8 * c
        out[base + PX : base + PX + 1, :] = pos[c : c + 1, :]
        out[base + PY : base + PY + 1, :] = pos[CELLS + c : CELLS + c + 1, :]
        out[base + PM : base + PM + 1, :] = mass[c : c + 1, :] * live
        out[base + PVX : base + PVX + 1, :] = vel[c : c + 1, :]
        out[base + PVY : base + PVY + 1, :] = vel[CELLS + c : CELLS + c + 1, :]
        out[base + PL : base + PL + 1, :] = live
        out[base + PL + 1 : base + 8, :] = jnp.zeros((2, S), jnp.float32)


def spread(row):
    return jnp.broadcast_to(row, (8, S))


def pick(tables, slot, masks):
    out = None
    for table, mask in zip(tables, masks):
        got = jnp.take_along_axis(table, slot, axis=1)
        out = got if out is None else jnp.where(mask, got, out)
    return out


def step_body(sign, frame, lists, pair, press):
    near = [(dr, dc) for dr in (-1, 0, 1) for dc in (-1, 0, 1)]
    numbers = [3 * (1 + sign * dr) + dc + 1 for dr, dc in near]

    def codes(start):
        code = lists[pl.ds(start, 8), :].astype(jnp.int32)
        which = code >> 7
        return code & (S - 1), which, [which == n for n in numbers]

    def density(row, carry):
        for col in range(RING):
            centre = pl.multiple_of(row * (WIDE * 8), 8) + (WIDE + col + 1) * 8
            own_x = spread(frame[pl.ds(centre + PX, 1), :])
            own_y = spread(frame[pl.ds(centre + PY, 1), :])
            own_m = frame[pl.ds(centre + PM, 1), :]

            def table(k):
                return [spread(frame[pl.ds(centre + (dr * WIDE + dc) * 8 + k, 1), :]) for dr, dc in near]

            xs, ys, ms = table(PX), table(PY), table(PM)
            total = jnp.zeros((8, S), jnp.float32)
            for t in range(NT):
                slot, which, masks = codes(pl.multiple_of(row * (RING * NB), 8) + col * NB + 8 * t)
                third = (which * 11) >> 5
                dx = own_x - ((third - 1).astype(jnp.float32) + pick(xs, slot, masks))
                dy = own_y - ((which - 3 * third - 1).astype(jnp.float32) + pick(ys, slot, masks))
                mass = pick(ms, slot, masks)
                dist = jnp.sqrt(dx * dx + dy * dy)
                tail = jnp.maximum(1.0 - dist, 0.0)
                cube = tail * tail * tail
                total = total + mass * (cube * tail * (4.0 * dist + 1.0))
                base = pl.multiple_of(row * (RING * NT * 40), 8) + (col * NT + t) * 40
                pair[pl.ds(base, 8), :] = dx
                pair[pl.ds(base + 8, 8), :] = dy
                pair[pl.ds(base + 16, 8), :] = mass
                pair[pl.ds(base + 24, 8), :] = dist * dist + 0.01
                pair[pl.ds(base + 32, 8), :] = 20.0 * cube
            rho = own_m + jnp.sum(total, axis=0, keepdims=True) + jnp.where(own_m > 0.0, 0.0, 1.0)
            press[pl.ds(pl.multiple_of(row * (RING * 8), 8) + col * 8, 1), :] = rho
        return carry

    lax.fori_loop(0, 3, density, 0)

    def term(rho):
        return sound_sq * (rho - 1.0) / (rho * rho)

    def force(c):
        cell = RING + 1 + c
        centre = (2 * WIDE + 2 + c) * 8
        own = frame[centre : centre + 8, :]
        own_rho = press[cell * 8 : cell * 8 + 1, :]
        own_vx, own_vy = spread(own[PVX : PVX + 1]), spread(own[PVY : PVY + 1])
        own_q, own_r = spread(term(own_rho)), spread(own_rho)
        vxs, vys, rhos = [], [], []
        for dr, dc in near:
            tile = centre + (dr * WIDE + dc) * 8
            vxs.append(spread(frame[tile + PVX : tile + PVX + 1, :]))
            vys.append(spread(frame[tile + PVY : tile + PVY + 1, :]))
            tile = (cell + dr * RING + dc) * 8
            rhos.append(spread(press[tile : tile + 1, :]))
        ax = jnp.zeros((8, S), jnp.float32)
        ay = jnp.zeros((8, S), jnp.float32)
        for t in range(NT):
            slot, _, masks = codes(cell * NB + 8 * t)
            base = (cell * NT + t) * 40
            dx = pair[base : base + 8, :]
            dy = pair[base + 8 : base + 16, :]
            mass = pair[base + 16 : base + 24, :]
            soft = pair[base + 24 : base + 32, :]
            slope = pair[base + 32 : base + 40, :]
            rho = pick(rhos, slot, masks)
            vdot = (own_vx - pick(vxs, slot, masks)) * dx + (own_vy - pick(vys, slot, masks)) * dy
            visc = visc_alpha * jnp.maximum(-vdot, 0.0) / (soft * (0.5 * (own_r + rho)))
            coef = mass * (own_q + term(rho) + visc) * slope
            ax = ax + coef * dx
            ay = ay + coef * dy
        live = own[PL : PL + 1]
        vx = own[PVX : PVX + 1] + step_dt * jnp.sum(ax, axis=0, keepdims=True) * live
        vy = own[PVY : PVY + 1] + step_dt * jnp.sum(ay, axis=0, keepdims=True) * live
        x = own[PX : PX + 1] + step_dt * vx * live
        y = own[PY : PY + 1] + step_dt * vy * live
        return x, y, own[PM : PM + 1], vx, vy, live, own_rho

    return force


LISTS = NB * CELLS
STATE = 8 * CELLS
HEAD = LISTS
MORE = LISTS + 2 * STATE
BUNDLE = MORE + 3 * NB


def first_kernel(parity, q0, q1, outer, q3, out, frame, lists, pair, press):
    sign = 1 - 2 * parity[0]
    two = 2 * STATE
    frame[0:two, :] = outer[BUNDLE : BUNDLE + two, :]
    frame[two : 2 * two, :] = outer[HEAD:MORE, :]
    frame[2 * two : 3 * two, :] = q0[HEAD:MORE, :]
    frame[3 * two : 4 * two, :] = q3[HEAD:MORE, :]
    frame[4 * two : 5 * two, :] = q1[...]
    for r, ref in enumerate((outer, q0, q3)):
        base = r * RING * NB
        lists[base : base + 3 * NB, :] = ref[NB:LISTS, :]
        lists[base + 3 * NB : base + 6 * NB, :] = ref[MORE:BUNDLE, :]
        out[STATE + r * NB : STATE + (r + 1) * NB, :] = ref[LISTS - NB : LISTS, :]
    force = step_body(sign, frame, lists, pair, press)
    for c in range(CELLS):
        x, y, m, vx, vy, live, _ = force(c)
        for k, v in enumerate((x, y, m, vx, vy, live)):
            out[8 * c + k : 8 * c + k + 1, :] = v
        out[8 * c + 6 : 8 * c + 8, :] = jnp.zeros((2, S), jnp.float32)


def second_kernel(parity, dest, shell, left, r0, r1, outer, r3, q0, before, q3, pos_out, vel_out, rho_out, part, frame, lists, pair, press):
    sign = 1 - 2 * parity[0]
    two = 2 * STATE
    frame[0:two, :] = outer[two : 2 * two, :]
    frame[two : 2 * two, :] = outer[0:two, :]
    frame[2 * two : 3 * two, :] = r0[...]
    frame[3 * two : 4 * two, :] = r3[...]
    frame[4 * two : 5 * two, :] = r1[...]
    for r, ref in enumerate((before, q0, q3)):
        base = r * RING * NB
        lists[base : base + NB, :] = left[STATE + r * NB : STATE + (r + 1) * NB, :]
        lists[base + NB : base + 5 * NB, :] = ref[0:LISTS, :]
        lists[base + 5 * NB : base + 6 * NB, :] = ref[MORE : MORE + NB, :]
    force = step_body(sign, frame, lists, pair, press)
    total = jnp.zeros((S, S), jnp.float32)
    devices = lax.broadcasted_iota(jnp.int32, (S, S), 0)
    shells = lax.broadcasted_iota(jnp.int32, (16, S), 0)
    for c in range(CELLS):
        x, y, m, vx, vy, live, rho = force(c)
        pos_out[c : c + 1, :] = x
        pos_out[CELLS + c : CELLS + c + 1, :] = y
        vel_out[c : c + 1, :] = vx
        vel_out[CELLS + c : CELLS + c + 1, :] = vy
        rho_out[c : c + 1, :] = rho
        loads = (m * vx, m * vy, m * (sound_sq * (rho - 1.0)), 0.5 * m * (vx * vx + vy * vy))
        owner = (devices == dest[c : c + 1, :]).astype(jnp.float32)
        member = shells == shell[c : c + 1, :]
        spreads = [jnp.where(member, load, 0.0) for load in loads]
        spreads.append(jnp.zeros((S - 64, S), jnp.float32))
        total = total + lax.dot_general(
            owner,
            jnp.concatenate(spreads, axis=0),
            (((1,), (1,)), ((), ())),
            precision=lax.Precision.HIGHEST,
            preferred_element_type=jnp.float32,
        )
    part[...] = total


def soil_kernel(arrived, stress, rate, couple, out):
    total = jnp.sum(arrived[...], axis=0, keepdims=True)
    lane = lax.broadcasted_iota(jnp.int32, (16, S), 1)
    row = lax.broadcasted_iota(jnp.int32, (16, S), 0)
    force_x, force_y, force_p, force_e = [
        jnp.sum(jnp.where(lane == row + 16 * k, total, 0.0), axis=1, keepdims=True) for k in range(4)
    ]
    exx = rate[0] + couple[0] * force_x
    eyy = rate[1] + couple[1] * force_y
    exy = rate[2] + couple[2] * force_p
    ezz = -0.5 * (couple[0] + couple[1]) * force_e
    trace = exx + eyy + ezz
    sxx = stress[0] + soil_dt * (2.0 * shear_mod * (exx - trace / 3.0) + bulk_mod * trace)
    syy = stress[1] + soil_dt * (2.0 * shear_mod * (eyy - trace / 3.0) + bulk_mod * trace)
    szz = stress[2] + soil_dt * (2.0 * shear_mod * (ezz - trace / 3.0) + bulk_mod * trace)
    sxy = stress[3] + soil_dt * 2.0 * shear_mod * exy
    first = sxx + syy + szz
    mean = first / 3.0
    dxx = sxx - mean
    dyy = syy - mean
    dzz = szz - mean
    root = jnp.sqrt(0.5 * (dxx * dxx + dyy * dyy + dzz * dzz) + sxy * sxy)
    radius = jnp.maximum(cohesion - friction * first, 0.2 * cohesion)
    factor = radius / jnp.maximum(root, radius)
    out[0] = mean + factor * dxx
    out[1] = mean + factor * dyy
    out[2] = mean + factor * dzz
    out[3] = factor * sxy


def rows_of(n):
    return jax.ShapeDtypeStruct((n, S), jnp.float32)


VM = pl.BlockSpec(memory_space=pltpu.MemorySpace.VMEM)
SM = pl.BlockSpec(memory_space=pltpu.MemorySpace.SMEM)
WORK = [
    pltpu.VMEM((5 * WIDE * 8, S), jnp.float32),
    pltpu.VMEM((3 * RING * NB, S), jnp.float32),
    pltpu.VMEM((3 * RING * NT * 40, S), jnp.float32),
    pltpu.VMEM((3 * RING * 8, S), jnp.float32),
]


def local(
    fluid_pos,
    fluid_vel,
    fluid_mass,
    cell_count,
    nb_list,
    iface_dest,
    iface_shell,
    soil_stress,
    soil_rate,
    soil_couple,
):
    n_depth = lax.axis_size("depth")
    n_azim = lax.axis_size("azim")
    parity = (lax.axis_index("depth") % 2).astype(jnp.int32).reshape(1)
    toward_left = [(i, (i - 1) % n_azim) for i in range(n_azim)]
    toward_right = [(i, (i + 1) % n_azim) for i in range(n_azim)]
    pairs = [(i, i ^ 1) for i in range(n_depth)]
    facing = [(i, i + 1 if i % 2 else i - 1) for i in range(n_depth)]
    facing = [(i, j) for i, j in facing if 0 <= j < n_depth]

    own = pl.pallas_call(
        pack_kernel,
        out_shape=rows_of(LISTS + STATE),
        in_specs=[SM, VM, VM, VM, VM],
        out_specs=VM,
        name="pack",
    )(
        cell_count,
        fluid_pos.reshape(2 * CELLS, S),
        fluid_vel.reshape(2 * CELLS, S),
        fluid_mass.reshape(CELLS, S),
        nb_list.reshape(NB * CELLS, S),
    )
    right = lax.ppermute(own, "azim", toward_left)
    q0 = jnp.concatenate([own, right[HEAD:], right[: 3 * NB]], axis=0)
    q3 = lax.ppermute(q0, "depth", pairs)
    outer = lax.ppermute(jnp.concatenate([q0, q3[HEAD:MORE]], axis=0), "depth", facing)
    q1 = lax.ppermute(outer[HEAD:MORE], "depth", pairs)
    mid = pl.pallas_call(
        first_kernel,
        out_shape=rows_of(STATE + 3 * NB),
        in_specs=[SM] + [VM] * 4,
        out_specs=VM,
        scratch_shapes=WORK,
        name="first_step",
    )(parity, q0, q1, outer, q3)

    left = lax.ppermute(mid, "azim", toward_right)
    r0 = jnp.concatenate([left[:STATE], mid[:STATE]], axis=0)
    r3 = lax.ppermute(r0, "depth", pairs)
    beyond = lax.ppermute(jnp.concatenate([r0, r3], axis=0), "depth", facing)
    r1 = lax.ppermute(beyond[: 2 * STATE], "depth", pairs)
    pos, vel, rho, part = pl.pallas_call(
        second_kernel,
        out_shape=(rows_of(2 * CELLS), rows_of(2 * CELLS), rows_of(CELLS), rows_of(S)),
        in_specs=[SM] + [VM] * 10,
        out_specs=(VM, VM, VM, VM),
        scratch_shapes=WORK,
        name="second_step",
    )(parity, iface_dest.reshape(CELLS, S), iface_shell.reshape(CELLS, S), left, r0, r1, beyond, r3, q0, outer, q3)

    arrived = lax.all_to_all(part, ("depth", "azim"), split_axis=0, concat_axis=0, tiled=True)
    stress_out = pl.pallas_call(
        soil_kernel,
        out_shape=jax.ShapeDtypeStruct(soil_stress.shape, jnp.float32),
        in_specs=[VM] * 4,
        out_specs=VM,
        name="soil",
    )(arrived, soil_stress, soil_rate, soil_couple)
    return (
        pos.reshape(fluid_pos.shape),
        vel.reshape(fluid_vel.shape),
        rho.reshape(fluid_mass.shape),
        stress_out,
    )


def solution(mesh):
    return jax.shard_map(
        local,
        mesh=mesh,
        in_specs=(
            P(None, "depth", "azim", None),
            P(None, "depth", "azim", None),
            P("depth", "azim", None),
            P("depth", "azim"),
            P(None, "depth", "azim", None),
            P(("depth", "azim"), None, None),
            P(("depth", "azim"), None),
            P(None, ("depth", "azim"), None),
            P(None, ("depth", "azim"), None),
            P(None, ("depth", "azim"), None),
        ),
        out_specs=(
            P(None, "depth", "azim", None),
            P(None, "depth", "azim", None),
            P("depth", "azim", None),
            P(None, ("depth", "azim"), None),
        ),
        check_vma=False,
    )
```

```python
import jax
import jax.numpy as jnp
from jax import lax
from jax.experimental import pallas as pl
from jax.experimental.pallas import tpu as pltpu
from jax.sharding import PartitionSpec as P

step_dt = 0.05
sound_sq = 1.0
visc_alpha = 0.5
soil_dt = 0.1
shear_mod = 1.0
bulk_mod = 2.0
cohesion = 1.0
friction = 0.3

CELLS = 4
NB = 24
NT = 3
WIDE = 8
RING = 6
S = 128
PX, PY, PM, PVX, PVY, PL = range(6)


def pack_kernel(count, pos, vel, mass, nb, out):
    lane = lax.broadcasted_iota(jnp.int32, (1, S), 1)
    for c in range(CELLS):
        live = (lane < count[0, c]).astype(jnp.float32)
        out[NB * c : NB * c + NB, :] = nb[pl.ds(c, NB, stride=CELLS), :].astype(jnp.float32)
        base = NB * CELLS + 8 * c
        out[base + PX : base + PX + 1, :] = pos[c : c + 1, :]
        out[base + PY : base + PY + 1, :] = pos[CELLS + c : CELLS + c + 1, :]
        out[base + PM : base + PM + 1, :] = mass[c : c + 1, :] * live
        out[base + PVX : base + PVX + 1, :] = vel[c : c + 1, :]
        out[base + PVY : base + PVY + 1, :] = vel[CELLS + c : CELLS + c + 1, :]
        out[base + PL : base + PL + 1, :] = live
        out[base + PL + 1 : base + 8, :] = jnp.zeros((2, S), jnp.float32)


def spread(row):
    return jnp.broadcast_to(row, (8, S))


def pick(tables, slot, masks):
    out = None
    for table, mask in zip(tables, masks):
        got = jnp.take_along_axis(table, slot, axis=1)
        out = got if out is None else jnp.where(mask, got, out)
    return out


def step_body(sign, frame, lists, pair, press):
    near = [(dr, dc) for dr in (-1, 0, 1) for dc in (-1, 0, 1)]
    numbers = [3 * (1 + sign * dr) + dc + 1 for dr, dc in near]

    def codes(start):
        code = lists[pl.ds(start, 8), :].astype(jnp.int32)
        which = code >> 7
        return code & (S - 1), which, [which == n for n in numbers]

    def density(row, carry):
        for col in range(RING):
            centre = pl.multiple_of(row * (WIDE * 8), 8) + (WIDE + col + 1) * 8
            own_x = spread(frame[pl.ds(centre + PX, 1), :])
            own_y = spread(frame[pl.ds(centre + PY, 1), :])
            own_m = frame[pl.ds(centre + PM, 1), :]

            def table(k):
                return [spread(frame[pl.ds(centre + (dr * WIDE + dc) * 8 + k, 1), :]) for dr, dc in near]

            xs, ys, ms = table(PX), table(PY), table(PM)
            total = jnp.zeros((8, S), jnp.float32)
            for t in range(NT):
                slot, which, masks = codes(pl.multiple_of(row * (RING * NB), 8) + col * NB + 8 * t)
                third = (which * 11) >> 5
                dx = own_x - ((third - 1).astype(jnp.float32) + pick(xs, slot, masks))
                dy = own_y - ((which - 3 * third - 1).astype(jnp.float32) + pick(ys, slot, masks))
                mass = pick(ms, slot, masks)
                dist = jnp.sqrt(dx * dx + dy * dy)
                tail = jnp.maximum(1.0 - dist, 0.0)
                cube = tail * tail * tail
                total = total + mass * (cube * tail * (4.0 * dist + 1.0))
                base = pl.multiple_of(row * (RING * NT * 40), 8) + (col * NT + t) * 40
                pair[pl.ds(base, 8), :] = dx
                pair[pl.ds(base + 8, 8), :] = dy
                pair[pl.ds(base + 16, 8), :] = mass
                pair[pl.ds(base + 24, 8), :] = dist * dist + 0.01
                pair[pl.ds(base + 32, 8), :] = 20.0 * cube
            rho = own_m + jnp.sum(total, axis=0, keepdims=True) + jnp.where(own_m > 0.0, 0.0, 1.0)
            press[pl.ds(pl.multiple_of(row * (RING * 8), 8) + col * 8, 1), :] = rho
        return carry

    lax.fori_loop(0, 3, density, 0)

    def term(rho):
        return sound_sq * (rho - 1.0) / (rho * rho)

    def force(c):
        cell = RING + 1 + c
        centre = (2 * WIDE + 2 + c) * 8
        own = frame[centre : centre + 8, :]
        own_rho = press[cell * 8 : cell * 8 + 1, :]
        own_vx, own_vy = spread(own[PVX : PVX + 1]), spread(own[PVY : PVY + 1])
        own_q, own_r = spread(term(own_rho)), spread(own_rho)
        vxs, vys, rhos = [], [], []
        for dr, dc in near:
            tile = centre + (dr * WIDE + dc) * 8
            vxs.append(spread(frame[tile + PVX : tile + PVX + 1, :]))
            vys.append(spread(frame[tile + PVY : tile + PVY + 1, :]))
            tile = (cell + dr * RING + dc) * 8
            rhos.append(spread(press[tile : tile + 1, :]))
        ax = jnp.zeros((8, S), jnp.float32)
        ay = jnp.zeros((8, S), jnp.float32)
        for t in range(NT):
            slot, _, masks = codes(cell * NB + 8 * t)
            base = (cell * NT + t) * 40
            dx = pair[base : base + 8, :]
            dy = pair[base + 8 : base + 16, :]
            mass = pair[base + 16 : base + 24, :]
            soft = pair[base + 24 : base + 32, :]
            slope = pair[base + 32 : base + 40, :]
            rho = pick(rhos, slot, masks)
            vdot = (own_vx - pick(vxs, slot, masks)) * dx + (own_vy - pick(vys, slot, masks)) * dy
            visc = visc_alpha * jnp.maximum(-vdot, 0.0) / (soft * (0.5 * (own_r + rho)))
            coef = mass * (own_q + term(rho) + visc) * slope
            ax = ax + coef * dx
            ay = ay + coef * dy
        live = own[PL : PL + 1]
        vx = own[PVX : PVX + 1] + step_dt * jnp.sum(ax, axis=0, keepdims=True) * live
        vy = own[PVY : PVY + 1] + step_dt * jnp.sum(ay, axis=0, keepdims=True) * live
        x = own[PX : PX + 1] + step_dt * vx * live
        y = own[PY : PY + 1] + step_dt * vy * live
        return x, y, own[PM : PM + 1], vx, vy, live, own_rho

    return force


LISTS = NB * CELLS
STATE = 8 * CELLS
HEAD = LISTS
MORE = LISTS + 2 * STATE
BUNDLE = MORE + 3 * NB


def first_kernel(parity, q0, q1, outer, q3, out, frame, lists, pair, press):
    sign = 1 - 2 * parity[0]
    two = 2 * STATE
    frame[0:two, :] = outer[BUNDLE : BUNDLE + two, :]
    frame[two : 2 * two, :] = outer[HEAD:MORE, :]
    frame[2 * two : 3 * two, :] = q0[HEAD:MORE, :]
    frame[3 * two : 4 * two, :] = q3[HEAD:MORE, :]
    frame[4 * two : 5 * two, :] = q1[...]
    for r, ref in enumerate((outer, q0, q3)):
        base = r * RING * NB
        lists[base : base + 3 * NB, :] = ref[NB:LISTS, :]
        lists[base + 3 * NB : base + 6 * NB, :] = ref[MORE:BUNDLE, :]
        out[STATE + r * NB : STATE + (r + 1) * NB, :] = ref[LISTS - NB : LISTS, :]
    force = step_body(sign, frame, lists, pair, press)
    for c in range(CELLS):
        x, y, m, vx, vy, live, _ = force(c)
        for k, v in enumerate((x, y, m, vx, vy, live)):
            out[8 * c + k : 8 * c + k + 1, :] = v
        out[8 * c + 6 : 8 * c + 8, :] = jnp.zeros((2, S), jnp.float32)


def second_kernel(parity, dest, shell, left, r0, r1, outer, r3, q0, before, q3, pos_out, vel_out, rho_out, part, frame, lists, pair, press):
    sign = 1 - 2 * parity[0]
    two = 2 * STATE
    frame[0:two, :] = outer[two : 2 * two, :]
    frame[two : 2 * two, :] = outer[0:two, :]
    frame[2 * two : 3 * two, :] = r0[...]
    frame[3 * two : 4 * two, :] = r3[...]
    frame[4 * two : 5 * two, :] = r1[...]
    for r, ref in enumerate((before, q0, q3)):
        base = r * RING * NB
        lists[base : base + NB, :] = left[STATE + r * NB : STATE + (r + 1) * NB, :]
        lists[base + NB : base + 5 * NB, :] = ref[0:LISTS, :]
        lists[base + 5 * NB : base + 6 * NB, :] = ref[MORE : MORE + NB, :]
    force = step_body(sign, frame, lists, pair, press)
    total = jnp.zeros((S, S), jnp.float32)
    devices = lax.broadcasted_iota(jnp.int32, (S, S), 0)
    shells = lax.broadcasted_iota(jnp.int32, (16, S), 0)
    for c in range(CELLS):
        x, y, m, vx, vy, live, rho = force(c)
        pos_out[c : c + 1, :] = x
        pos_out[CELLS + c : CELLS + c + 1, :] = y
        vel_out[c : c + 1, :] = vx
        vel_out[CELLS + c : CELLS + c + 1, :] = vy
        rho_out[c : c + 1, :] = rho
        loads = (m * vx, m * vy, m * (sound_sq * (rho - 1.0)), 0.5 * m * (vx * vx + vy * vy))
        owner = (devices == dest[c : c + 1, :]).astype(jnp.float32)
        member = shells == shell[c : c + 1, :]
        spreads = [jnp.where(member, load, 0.0) for load in loads]
        spreads.append(jnp.zeros((S - 64, S), jnp.float32))
        total = total + lax.dot_general(
            owner,
            jnp.concatenate(spreads, axis=0),
            (((1,), (1,)), ((), ())),
            precision=lax.Precision.HIGHEST,
            preferred_element_type=jnp.float32,
        )
    part[...] = total


def soil_kernel(arrived, stress, rate, couple, out):
    total = jnp.sum(arrived[...], axis=0, keepdims=True)
    lane = lax.broadcasted_iota(jnp.int32, (16, S), 1)
    row = lax.broadcasted_iota(jnp.int32, (16, S), 0)
    force_x, force_y, force_p, force_e = [
        jnp.sum(jnp.where(lane == row + 16 * k, total, 0.0), axis=1, keepdims=True) for k in range(4)
    ]
    exx = rate[0] + couple[0] * force_x
    eyy = rate[1] + couple[1] * force_y
    exy = rate[2] + couple[2] * force_p
    ezz = -0.5 * (couple[0] + couple[1]) * force_e
    trace = exx + eyy + ezz
    sxx = stress[0] + soil_dt * (2.0 * shear_mod * (exx - trace / 3.0) + bulk_mod * trace)
    syy = stress[1] + soil_dt * (2.0 * shear_mod * (eyy - trace / 3.0) + bulk_mod * trace)
    szz = stress[2] + soil_dt * (2.0 * shear_mod * (ezz - trace / 3.0) + bulk_mod * trace)
    sxy = stress[3] + soil_dt * 2.0 * shear_mod * exy
    first = sxx + syy + szz
    mean = first / 3.0
    dxx = sxx - mean
    dyy = syy - mean
    dzz = szz - mean
    root = jnp.sqrt(0.5 * (dxx * dxx + dyy * dyy + dzz * dzz) + sxy * sxy)
    radius = jnp.maximum(cohesion - friction * first, 0.2 * cohesion)
    factor = radius / jnp.maximum(root, radius)
    out[0] = mean + factor * dxx
    out[1] = mean + factor * dyy
    out[2] = mean + factor * dzz
    out[3] = factor * sxy


def rows_of(n):
    return jax.ShapeDtypeStruct((n, S), jnp.float32)


def kept(n):
    return pltpu.VMEM((n, S), jnp.float32)


VM = pl.BlockSpec(memory_space=pltpu.MemorySpace.VMEM)
SM = pl.BlockSpec(memory_space=pltpu.MemorySpace.SMEM)
WORK = [
    pltpu.VMEM((5 * WIDE * 8, S), jnp.float32),
    pltpu.VMEM((3 * RING * NB, S), jnp.float32),
    pltpu.VMEM((3 * RING * NT * 40, S), jnp.float32),
    pltpu.VMEM((3 * RING * 8, S), jnp.float32),
]


def held(a):
    return pltpu.with_memory_space_constraint(a, pltpu.MemorySpace.VMEM)


def local(
    fluid_pos,
    fluid_vel,
    fluid_mass,
    cell_count,
    nb_list,
    iface_dest,
    iface_shell,
    soil_stress,
    soil_rate,
    soil_couple,
):
    n_depth = lax.axis_size("depth")
    n_azim = lax.axis_size("azim")
    parity = (lax.axis_index("depth") % 2).astype(jnp.int32).reshape(1)
    toward_left = [(i, (i - 1) % n_azim) for i in range(n_azim)]
    toward_right = [(i, (i + 1) % n_azim) for i in range(n_azim)]
    pairs = [(i, i ^ 1) for i in range(n_depth)]
    facing = [(i, i + 1 if i % 2 else i - 1) for i in range(n_depth)]
    facing = [(i, j) for i, j in facing if 0 <= j < n_depth]

    own = pl.pallas_call(
        pack_kernel,
        out_shape=kept(LISTS + STATE),
        in_specs=[SM, VM, VM, VM, VM],
        out_specs=VM,
        name="pack",
    )(
        cell_count,
        fluid_pos.reshape(2 * CELLS, S),
        fluid_vel.reshape(2 * CELLS, S),
        fluid_mass.reshape(CELLS, S),
        nb_list.reshape(NB * CELLS, S),
    )
    right = lax.ppermute(own, "azim", toward_left)
    q0 = jnp.concatenate([own, right[HEAD:], right[: 3 * NB]], axis=0)
    q3 = lax.ppermute(q0, "depth", pairs)
    outer = lax.ppermute(jnp.concatenate([q0, q3[HEAD:MORE]], axis=0), "depth", facing)
    q1 = lax.ppermute(outer[HEAD:MORE], "depth", pairs)
    mid = pl.pallas_call(
        first_kernel,
        out_shape=kept(STATE + 3 * NB),
        in_specs=[SM] + [VM] * 4,
        out_specs=VM,
        scratch_shapes=WORK,
        name="first_step",
    )(parity, *[held(a) for a in (q0, q1, outer, q3)])

    left = lax.ppermute(mid, "azim", toward_right)
    r0 = jnp.concatenate([left[:STATE], mid[:STATE]], axis=0)
    r3 = lax.ppermute(r0, "depth", pairs)
    beyond = lax.ppermute(jnp.concatenate([r0, r3], axis=0), "depth", facing)
    r1 = lax.ppermute(beyond[: 2 * STATE], "depth", pairs)
    pos, vel, rho, part = pl.pallas_call(
        second_kernel,
        out_shape=(kept(2 * CELLS), kept(2 * CELLS), kept(CELLS), kept(S)),
        in_specs=[SM] + [VM] * 10,
        out_specs=(VM, VM, VM, VM),
        scratch_shapes=WORK,
        name="second_step",
    )(parity, *[held(a) for a in (iface_dest.reshape(CELLS, S), iface_shell.reshape(CELLS, S), left, r0, r1, beyond, r3, q0, outer, q3)])

    arrived = lax.all_to_all(part, ("depth", "azim"), split_axis=0, concat_axis=0, tiled=True)
    stress_out = pl.pallas_call(
        soil_kernel,
        out_shape=jax.ShapeDtypeStruct(soil_stress.shape, jnp.float32),
        in_specs=[VM] * 4,
        out_specs=VM,
        name="soil",
    )(held(arrived), held(soil_stress), held(soil_rate), held(soil_couple))
    return (
        pos.reshape(fluid_pos.shape),
        vel.reshape(fluid_vel.shape),
        rho.reshape(fluid_mass.shape),
        stress_out,
    )


def solution(mesh):
    return jax.shard_map(
        local,
        mesh=mesh,
        in_specs=(
            P(None, "depth", "azim", None),
            P(None, "depth", "azim", None),
            P("depth", "azim", None),
            P("depth", "azim"),
            P(None, "depth", "azim", None),
            P(("depth", "azim"), None, None),
            P(("depth", "azim"), None),
            P(None, ("depth", "azim"), None),
            P(None, ("depth", "azim"), None),
            P(None, ("depth", "azim"), None),
        ),
        out_specs=(
            P(None, "depth", "azim", None),
            P(None, "depth", "azim", None),
            P("depth", "azim", None),
            P(None, ("depth", "azim"), None),
        ),
        check_vma=False,
    )
```

```python
import jax
import jax.numpy as jnp
from jax import lax
from jax.experimental import pallas as pl
from jax.experimental.pallas import tpu as pltpu
from jax.sharding import PartitionSpec as P

step_dt = 0.05
sound_sq = 1.0
visc_alpha = 0.5
soil_dt = 0.1
shear_mod = 1.0
bulk_mod = 2.0
cohesion = 1.0
friction = 0.3

CELLS = 4
NB = 24
NT = 3
WIDE = 8
RING = 6
S = 128
LISTS = NB * CELLS
PX, PY, PM, PVX, PVY, PL = range(6)
HALF = 6 * CELLS
SENT = 5 * WIDE
PLACE = 3 * WIDE
PAIR = 40
NEAR = [(dr, dc) for dr in (-1, 0, 1) for dc in (-1, 0, 1)]


def pack_kernel(count, pos, vel, mass, nb, out, last):
    lane = lax.broadcasted_iota(jnp.int32, (1, S), 1)
    out[0 : 2 * CELLS, :] = pos[...]
    out[PVX * CELLS : (PVX + 2) * CELLS, :] = vel[...]
    for c in range(CELLS):
        live = (lane < count[0, c]).astype(jnp.float32)
        out[PM * CELLS + c : PM * CELLS + c + 1, :] = mass[c : c + 1, :] * live
        out[PL * CELLS + c : PL * CELLS + c + 1, :] = live
        codes = nb[pl.ds(c, NB, stride=CELLS), :].astype(jnp.float32)
        if c < CELLS - 1:
            out[HALF + NB * c : HALF + NB * (c + 1), :] = codes
        else:
            last[...] = codes


def spread(row):
    return jnp.broadcast_to(row, (8, S))


def pick(tables, slot, masks):
    out = None
    for table, mask in zip(tables, masks):
        got = jnp.take_along_axis(table, slot, axis=1)
        out = got if out is None else jnp.where(mask, got, out)
    return out


def numbers_of(parity):
    sign = 1 - 2 * parity[0]
    return [3 * (1 + sign * dr) + dc + 1 for dr, dc in NEAR]


def decode(ref, start, numbers):
    code = ref[start : start + 8, :].astype(jnp.int32)
    which = code >> 7
    return code & (S - 1), which, [which == n for n in numbers]


def density(parity, rows, lists, rho_out, pair):
    numbers = numbers_of(parity)
    rho_out[...] = jnp.zeros((WIDE, S), jnp.float32)
    for k in range(RING):
        col = k + 1
        ref, start = rows[0]
        own_x, own_y = spread(ref[start + col : start + col + 1, :]), spread(ref[start + WIDE + col : start + WIDE + col + 1, :])
        own_m = ref[start + PM * WIDE + col : start + PM * WIDE + col + 1, :]

        def table(f):
            out = []
            for dr, dc in NEAR:
                r, base = rows[dr]
                at = base + f * WIDE + col + dc
                out.append(spread(r[at : at + 1, :]))
            return out

        xs, ys, ms = table(PX), table(PY), table(PM)
        total = jnp.zeros((8, S), jnp.float32)
        ref, start = lists[k]
        for t in range(NT):
            slot, which, masks = decode(ref, start + 8 * t, numbers)
            third = (which * 11) >> 5
            dx = own_x - ((third - 1).astype(jnp.float32) + pick(xs, slot, masks))
            dy = own_y - ((which - 3 * third - 1).astype(jnp.float32) + pick(ys, slot, masks))
            mass = pick(ms, slot, masks)
            dist = jnp.sqrt(dx * dx + dy * dy)
            tail = jnp.maximum(1.0 - dist, 0.0)
            cube = tail * tail * tail
            total = total + mass * (cube * tail * (4.0 * dist + 1.0))
            if pair is not None and 1 <= k <= CELLS:
                base = ((k - 1) * NT + t) * PAIR
                pair[base : base + 8, :] = dx
                pair[base + 8 : base + 16, :] = dy
                pair[base + 16 : base + 24, :] = mass
                pair[base + 24 : base + 32, :] = dist * dist + 0.01
                pair[base + 32 : base + 40, :] = 20.0 * cube
        rho = own_m + jnp.sum(total, axis=0, keepdims=True) + jnp.where(own_m > 0.0, 0.0, 1.0)
        rho_out[col : col + 1, :] = rho


def term(rho):
    return sound_sq * (rho - 1.0) / (rho * rho)


def force(c, numbers, frame, states, rhos, lists, pair):
    col = c + 2
    ref, start = lists

    def own(f):
        return frame[f * WIDE + col : f * WIDE + col + 1, :]

    def table(refs, f):
        return [spread(refs[dr][f * WIDE + col + dc : f * WIDE + col + dc + 1, :]) for dr, dc in NEAR]

    own_rho = rhos[0][col : col + 1, :]
    own_vx, own_vy = spread(own(PVX)), spread(own(PVY))
    own_q, own_r = spread(term(own_rho)), spread(own_rho)
    vxs, vys, rs = table(states, PVX), table(states, PVY), table(rhos, 0)
    ax = jnp.zeros((8, S), jnp.float32)
    ay = jnp.zeros((8, S), jnp.float32)
    for t in range(NT):
        slot, _, masks = decode(ref, start + 8 * t, numbers)
        base = (c * NT + t) * PAIR
        dx = pair[base : base + 8, :]
        dy = pair[base + 8 : base + 16, :]
        mass = pair[base + 16 : base + 24, :]
        soft = pair[base + 24 : base + 32, :]
        slope = pair[base + 32 : base + 40, :]
        rho = pick(rs, slot, masks)
        vdot = (own_vx - pick(vxs, slot, masks)) * dx + (own_vy - pick(vys, slot, masks)) * dy
        visc = visc_alpha * jnp.maximum(-vdot, 0.0) / (soft * (0.5 * (own_r + rho)))
        coef = mass * (own_q + term(rho) + visc) * slope
        ax = ax + coef * dx
        ay = ay + coef * dy
    live = own(PL)
    vx = own(PVX) + step_dt * jnp.sum(ax, axis=0, keepdims=True) * live
    vy = own(PVY) + step_dt * jnp.sum(ay, axis=0, keepdims=True) * live
    x = own(PX) + step_dt * vx * live
    y = own(PY) + step_dt * vy * live
    return (x, y, own(PM), vx, vy, live), own_rho


OUTER = SENT + PLACE


def middle_first_kernel(parity, frame, other, outer, send, last, right, rho, pair):
    lists = [(send, HALF + NB), (send, HALF + 2 * NB), (last, 0)] + [(right, HALF + NB * c) for c in range(3)]
    density(parity, {-1: (outer, 0), 0: (frame, 0), 1: (other, 0)}, lists, rho, pair)


def outer_first_kernel(parity, frame, outer, after, rho):
    lists = [(outer, OUTER + NB * (k + 1)) for k in range(RING)]
    density(parity, {-1: (outer, SENT), 0: (outer, 0), 1: (frame, 0)}, lists, rho, None)


def force_first_kernel(parity, frame, other, outer, rho_outer, rho_own, rho_other, send, last, right, pair, out):
    numbers = numbers_of(parity)
    lists = [(send, HALF + 2 * NB), (last, 0), (right, HALF), (right, HALF + NB)]
    for c in range(CELLS):
        fields, _ = force(
            c, numbers, frame, {-1: outer, 0: frame, 1: other}, {-1: rho_outer, 0: rho_own, 1: rho_other}, lists[c], pair
        )
        for k, v in enumerate(fields):
            out[k * CELLS + c : k * CELLS + c + 1, :] = v
    out[HALF : HALF + NB, :] = outer[OUTER + 3 * NB : OUTER + 4 * NB, :]
    out[HALF + NB : HALF + 2 * NB, :] = last[...]


def middle_second_kernel(parity, frame, other, outer, left, send, last, right, rho, pair):
    lists = [(left, HALF + NB)] + [(send, HALF + NB * c) for c in range(3)] + [(last, 0), (right, HALF)]
    density(parity, {-1: (outer, 0), 0: (frame, 0), 1: (other, 0)}, lists, rho, pair)


def outer_second_kernel(parity, frame, outer, left, before, after, rho):
    lists = [(left, HALF)] + [(before, OUTER + NB * c) for c in range(5)]
    density(parity, {-1: (outer, SENT), 0: (outer, 0), 1: (frame, 0)}, lists, rho, None)


def force_second_kernel(
    parity, dest, shell, frame, other, outer, rho_outer, rho_own, rho_other, send, last, pair, pos_out, vel_out, rho_out, part
):
    numbers = numbers_of(parity)
    lists = [(send, HALF), (send, HALF + NB), (send, HALF + 2 * NB), (last, 0)]
    total = jnp.zeros((S, S), jnp.float32)
    devices = lax.broadcasted_iota(jnp.int32, (S, S), 0)
    shells = lax.broadcasted_iota(jnp.int32, (16, S), 0)
    for c in range(CELLS):
        (x, y, m, vx, vy, live), rho = force(
            c, numbers, frame, {-1: outer, 0: frame, 1: other}, {-1: rho_outer, 0: rho_own, 1: rho_other}, lists[c], pair
        )
        pos_out[c : c + 1, :] = x
        pos_out[CELLS + c : CELLS + c + 1, :] = y
        vel_out[c : c + 1, :] = vx
        vel_out[CELLS + c : CELLS + c + 1, :] = vy
        rho_out[c : c + 1, :] = rho
        loads = (m * vx, m * vy, m * (sound_sq * (rho - 1.0)), 0.5 * m * (vx * vx + vy * vy))
        owner = (devices == dest[c : c + 1, :]).astype(jnp.bfloat16)
        member = shells == shell[c : c + 1, :]
        rest = jnp.concatenate([jnp.where(member, load, 0.0) for load in loads] + [jnp.zeros((S - 64, S), jnp.float32)], axis=0)
        for _ in range(3):
            some = rest.astype(jnp.bfloat16)
            total = total + lax.dot_general(owner, some, (((1,), (1,)), ((), ())), preferred_element_type=jnp.float32)
            rest = rest - some.astype(jnp.float32)
    part[...] = total


def soil_kernel(arrived, stress, rate, couple, out):
    total = jnp.sum(arrived[...], axis=0, keepdims=True)
    lane = lax.broadcasted_iota(jnp.int32, (16, S), 1)
    row = lax.broadcasted_iota(jnp.int32, (16, S), 0)
    force_x, force_y, force_p, force_e = [
        jnp.sum(jnp.where(lane == row + 16 * k, total, 0.0), axis=1, keepdims=True) for k in range(4)
    ]
    exx = rate[0] + couple[0] * force_x
    eyy = rate[1] + couple[1] * force_y
    exy = rate[2] + couple[2] * force_p
    ezz = -0.5 * (couple[0] + couple[1]) * force_e
    trace = exx + eyy + ezz
    sxx = stress[0] + soil_dt * (2.0 * shear_mod * (exx - trace / 3.0) + bulk_mod * trace)
    syy = stress[1] + soil_dt * (2.0 * shear_mod * (eyy - trace / 3.0) + bulk_mod * trace)
    szz = stress[2] + soil_dt * (2.0 * shear_mod * (ezz - trace / 3.0) + bulk_mod * trace)
    sxy = stress[3] + soil_dt * 2.0 * shear_mod * exy
    first = sxx + syy + szz
    mean = first / 3.0
    dxx = sxx - mean
    dyy = syy - mean
    dzz = szz - mean
    root = jnp.sqrt(0.5 * (dxx * dxx + dyy * dyy + dzz * dzz) + sxy * sxy)
    radius = jnp.maximum(cohesion - friction * first, 0.2 * cohesion)
    factor = radius / jnp.maximum(root, radius)
    out[0] = mean + factor * dxx
    out[1] = mean + factor * dyy
    out[2] = mean + factor * dzz
    out[3] = factor * sxy


def rows_of(n):
    return jax.ShapeDtypeStruct((n, S), jnp.float32)


def kept(n):
    return pltpu.VMEM((n, S), jnp.float32)


VM = pl.BlockSpec(memory_space=pltpu.MemorySpace.VMEM)
SM = pl.BlockSpec(memory_space=pltpu.MemorySpace.SMEM)


def held(a):
    return pltpu.with_memory_space_constraint(a, pltpu.MemorySpace.VMEM)


def local(
    fluid_pos,
    fluid_vel,
    fluid_mass,
    cell_count,
    nb_list,
    iface_dest,
    iface_shell,
    soil_stress,
    soil_rate,
    soil_couple,
):
    n_depth = lax.axis_size("depth")
    n_azim = lax.axis_size("azim")
    parity = (lax.axis_index("depth") % 2).astype(jnp.int32).reshape(1)
    toward_left = [(i, (i - 1) % n_azim) for i in range(n_azim)]
    toward_right = [(i, (i + 1) % n_azim) for i in range(n_azim)]
    pairs = [(i, i ^ 1) for i in range(n_depth)]
    facing = [(i, i + 1 if i % 2 else i - 1) for i in range(n_depth)]
    facing = [(i, j) for i, j in facing if 0 <= j < n_depth]

    def call(kernel, name, shapes, *args):
        return pl.pallas_call(
            kernel,
            out_shape=tuple(kept(n) for n in shapes),
            in_specs=[SM] + [VM] * len(args),
            out_specs=(VM,) * len(shapes),
            name=name,
        )(parity, *[held(a) for a in args])

    def merged(first, second):
        halves = [a[:HALF].reshape(6, CELLS, S) for a in (first, second)]
        return jnp.concatenate(halves, axis=1).reshape(6 * WIDE, S)

    def swapped(a):
        return lax.ppermute(a, "depth", pairs)

    send, last = pl.pallas_call(
        pack_kernel,
        out_shape=(kept(HALF + 3 * NB), kept(NB)),
        in_specs=[SM, VM, VM, VM, VM],
        out_specs=(VM, VM),
        name="pack",
    )(
        cell_count,
        fluid_pos.reshape(2 * CELLS, S),
        fluid_vel.reshape(2 * CELLS, S),
        fluid_mass.reshape(CELLS, S),
        nb_list.reshape(NB * CELLS, S),
    )
    right = lax.ppermute(send, "azim", toward_left)
    frame = merged(send, right)
    other = swapped(frame[:SENT])
    outer = lax.ppermute(
        jnp.concatenate([frame[:SENT], other[:PLACE], send[HALF:], last, right[HALF:]], axis=0), "depth", facing
    )
    rho_own, pair = call(
        middle_first_kernel, "middle_first", (WIDE, CELLS * NT * PAIR), frame, other, outer, send, last, right
    )
    rho_other = swapped(rho_own)
    (rho_outer,) = call(outer_first_kernel, "outer_first", (WIDE,), frame, outer, rho_own)
    (mid,) = call(
        force_first_kernel,
        "force_first",
        (HALF + 2 * NB,),
        frame, other, outer, rho_outer, rho_own, rho_other, send, last, right, pair,
    )

    left = lax.ppermute(mid, "azim", toward_right)
    frame = merged(left, mid)
    other = swapped(frame[:SENT])
    beyond = lax.ppermute(jnp.concatenate([frame[:SENT], other[:PLACE]], axis=0), "depth", facing)
    rho_own, pair = call(
        middle_second_kernel, "middle_second", (WIDE, CELLS * NT * PAIR), frame, other, beyond, left, send, last, right
    )
    rho_other = swapped(rho_own)
    (rho_outer,) = call(outer_second_kernel, "outer_second", (WIDE,), frame, beyond, left, outer, rho_own)
    pos, vel, rho, part = call(
        force_second_kernel,
        "force_second",
        (2 * CELLS, 2 * CELLS, CELLS, S),
        iface_dest.reshape(CELLS, S), iface_shell.reshape(CELLS, S),
        frame, other, beyond, rho_outer, rho_own, rho_other, send, last, pair,
    )

    arrived = lax.all_to_all(part, ("depth", "azim"), split_axis=0, concat_axis=0, tiled=True)
    stress_out = pl.pallas_call(
        soil_kernel,
        out_shape=jax.ShapeDtypeStruct(soil_stress.shape, jnp.float32),
        in_specs=[VM] * 4,
        out_specs=VM,
        name="soil",
    )(held(arrived), held(soil_stress), held(soil_rate), held(soil_couple))
    return (
        pos.reshape(fluid_pos.shape),
        vel.reshape(fluid_vel.shape),
        rho.reshape(fluid_mass.shape),
        stress_out,
    )


def solution(mesh):
    return jax.shard_map(
        local,
        mesh=mesh,
        in_specs=(
            P(None, "depth", "azim", None),
            P(None, "depth", "azim", None),
            P("depth", "azim", None),
            P("depth", "azim"),
            P(None, "depth", "azim", None),
            P(("depth", "azim"), None, None),
            P(("depth", "azim"), None),
            P(None, ("depth", "azim"), None),
            P(None, ("depth", "azim"), None),
            P(None, ("depth", "azim"), None),
        ),
        out_specs=(
            P(None, "depth", "azim", None),
            P(None, "depth", "azim", None),
            P("depth", "azim", None),
            P(None, ("depth", "azim"), None),
        ),
        check_vma=False,
    )
```

```python
import jax
import jax.numpy as jnp
from jax import lax
from jax.experimental import pallas as pl
from jax.experimental.pallas import tpu as pltpu
from jax.sharding import PartitionSpec as P

step_dt = 0.05
sound_sq = 1.0
visc_alpha = 0.5
soil_dt = 0.1
shear_mod = 1.0
bulk_mod = 2.0
cohesion = 1.0
friction = 0.3

CELLS = 4
NB = 24
NT = 3
WIDE = 8
RING = 6
S = 128
LISTS = NB * CELLS
PX, PY, PM, PVX, PVY, PL = range(6)
HALF = 6 * CELLS
SENT = 5 * WIDE
PLACE = 3 * WIDE
PAIR = 40
NEAR = [(dr, dc) for dr in (-1, 0, 1) for dc in (-1, 0, 1)]


def pack_kernel(count, pos, vel, mass, nb, dest, shell, stress, rate, couple, out, first, home, soil):
    soil[0:4] = stress[...]
    soil[4:7] = rate[...]
    soil[7:10] = couple[...]
    home[0:CELLS, :] = dest[...]
    home[CELLS : 2 * CELLS, :] = shell[...]
    lane = lax.broadcasted_iota(jnp.int32, (1, S), 1)
    out[0 : 2 * CELLS, :] = pos[...]
    out[PVX * CELLS : (PVX + 2) * CELLS, :] = vel[...]
    for c in range(CELLS):
        live = (lane < count[0, c]).astype(jnp.float32)
        out[PM * CELLS + c : PM * CELLS + c + 1, :] = mass[c : c + 1, :] * live
        out[PL * CELLS + c : PL * CELLS + c + 1, :] = live
        codes = nb[pl.ds(c, NB, stride=CELLS), :].astype(jnp.float32)
        if c:
            out[HALF + NB * (c - 1) : HALF + NB * c, :] = codes
        else:
            first[...] = codes


def spread(row):
    return jnp.broadcast_to(row, (8, S))


def pick(tables, slot, masks):
    out = None
    for table, mask in zip(tables, masks):
        got = jnp.take_along_axis(table, slot, axis=1)
        out = got if out is None else jnp.where(mask, got, out)
    return out


def numbers_of(parity):
    sign = 1 - 2 * parity[0]
    return [3 * (1 + sign * dr) + dc + 1 for dr, dc in NEAR]


def decode(ref, start, numbers):
    code = ref[start : start + 8, :].astype(jnp.int32)
    which = code >> 7
    return code & (S - 1), which, [which == n for n in numbers]


def density(parity, rows, lists, rho_out, pair):
    numbers = numbers_of(parity)
    rho_out[...] = jnp.zeros((WIDE, S), jnp.float32)
    for k in range(RING):
        col = k + 1
        ref, start = rows[0]
        own_x, own_y = spread(ref[start + col : start + col + 1, :]), spread(ref[start + WIDE + col : start + WIDE + col + 1, :])
        own_m = ref[start + PM * WIDE + col : start + PM * WIDE + col + 1, :]

        def table(f):
            out = []
            for dr, dc in NEAR:
                r, base = rows[dr]
                at = base + f * WIDE + col + dc
                out.append(spread(r[at : at + 1, :]))
            return out

        xs, ys, ms = table(PX), table(PY), table(PM)
        total = jnp.zeros((8, S), jnp.float32)
        ref, start = lists[k]
        for t in range(NT):
            slot, which, masks = decode(ref, start + 8 * t, numbers)
            third = (which * 11) >> 5
            dx = own_x - ((third - 1).astype(jnp.float32) + pick(xs, slot, masks))
            dy = own_y - ((which - 3 * third - 1).astype(jnp.float32) + pick(ys, slot, masks))
            mass = pick(ms, slot, masks)
            dist = jnp.sqrt(dx * dx + dy * dy)
            tail = jnp.maximum(1.0 - dist, 0.0)
            cube = tail * tail * tail
            total = total + mass * (cube * tail * (4.0 * dist + 1.0))
            if pair is not None and 1 <= k <= CELLS:
                base = ((k - 1) * NT + t) * PAIR
                pair[base : base + 8, :] = dx
                pair[base + 8 : base + 16, :] = dy
                pair[base + 16 : base + 24, :] = mass
                pair[base + 24 : base + 32, :] = dist * dist + 0.01
                pair[base + 32 : base + 40, :] = 20.0 * cube
        rho = own_m + jnp.sum(total, axis=0, keepdims=True) + jnp.where(own_m > 0.0, 0.0, 1.0)
        rho_out[col : col + 1, :] = rho


def term(rho):
    return sound_sq * (rho - 1.0) / (rho * rho)


def force(c, numbers, frame, states, rhos, lists, pair):
    col = c + 2
    ref, start = lists

    def own(f):
        return frame[f * WIDE + col : f * WIDE + col + 1, :]

    def table(refs, f):
        return [spread(refs[dr][f * WIDE + col + dc : f * WIDE + col + dc + 1, :]) for dr, dc in NEAR]

    own_rho = rhos[0][col : col + 1, :]
    own_vx, own_vy = spread(own(PVX)), spread(own(PVY))
    own_q, own_r = spread(term(own_rho)), spread(own_rho)
    vxs, vys, rs = table(states, PVX), table(states, PVY), table(rhos, 0)
    ax = jnp.zeros((8, S), jnp.float32)
    ay = jnp.zeros((8, S), jnp.float32)
    for t in range(NT):
        slot, _, masks = decode(ref, start + 8 * t, numbers)
        base = (c * NT + t) * PAIR
        dx = pair[base : base + 8, :]
        dy = pair[base + 8 : base + 16, :]
        mass = pair[base + 16 : base + 24, :]
        soft = pair[base + 24 : base + 32, :]
        slope = pair[base + 32 : base + 40, :]
        rho = pick(rs, slot, masks)
        vdot = (own_vx - pick(vxs, slot, masks)) * dx + (own_vy - pick(vys, slot, masks)) * dy
        visc = visc_alpha * jnp.maximum(-vdot, 0.0) / (soft * (0.5 * (own_r + rho)))
        coef = mass * (own_q + term(rho) + visc) * slope
        ax = ax + coef * dx
        ay = ay + coef * dy
    live = own(PL)
    vx = own(PVX) + step_dt * jnp.sum(ax, axis=0, keepdims=True) * live
    vy = own(PVY) + step_dt * jnp.sum(ay, axis=0, keepdims=True) * live
    x = own(PX) + step_dt * vx * live
    y = own(PY) + step_dt * vy * live
    return (x, y, own(PM), vx, vy, live), own_rho


OUTER = SENT + PLACE


def middle_first_kernel(parity, frame, other, outer, left, first, send, rho, pair):
    lists = [(left, HALF + NB * c) for c in range(3)] + [(first, 0), (send, HALF), (send, HALF + NB)]
    density(parity, {-1: (outer, 0), 0: (frame, 0), 1: (other, 0)}, lists, rho, pair)


def outer_first_kernel(parity, frame, outer, after, rho):
    lists = [(outer, OUTER + NB * k) for k in range(RING)]
    density(parity, {-1: (outer, SENT), 0: (outer, 0), 1: (frame, 0)}, lists, rho, None)


def force_first_kernel(parity, frame, other, outer, rho_outer, rho_own, rho_other, left, first, send, pair, out):
    numbers = numbers_of(parity)
    lists = [(left, HALF + NB), (left, HALF + 2 * NB), (first, 0), (send, HALF)]
    for c in range(CELLS):
        fields, _ = force(
            c, numbers, frame, {-1: outer, 0: frame, 1: other}, {-1: rho_outer, 0: rho_own, 1: rho_other}, lists[c], pair
        )
        for k, v in enumerate(fields):
            out[k * CELLS + c : k * CELLS + c + 1, :] = v
    out[HALF : HALF + NB, :] = outer[OUTER + 3 * NB : OUTER + 4 * NB, :]
    out[HALF + NB : HALF + 2 * NB, :] = first[...]


def middle_second_kernel(parity, frame, other, outer, right, left, first, send, rho, pair):
    lists = [(left, HALF + 2 * NB), (first, 0)] + [(send, HALF + NB * c) for c in range(3)] + [(right, HALF + NB)]
    density(parity, {-1: (outer, 0), 0: (frame, 0), 1: (other, 0)}, lists, rho, pair)


def outer_second_kernel(parity, frame, outer, right, before, after, rho):
    lists = [(before, OUTER + NB * (2 + c)) for c in range(5)] + [(right, HALF)]
    density(parity, {-1: (outer, SENT), 0: (outer, 0), 1: (frame, 0)}, lists, rho, None)


def force_second_kernel(
    parity, home, frame, other, outer, rho_outer, rho_own, rho_other, first, send, pair, pos_out, vel_out, rho_out, part
):
    numbers = numbers_of(parity)
    lists = [(first, 0), (send, HALF), (send, HALF + NB), (send, HALF + 2 * NB)]
    devices = lax.broadcasted_iota(jnp.int32, (S, S), 0)
    shells = lax.broadcasted_iota(jnp.int32, (16, S), 0)
    owners, shares = [], []
    for c in range(CELLS):
        (x, y, m, vx, vy, live), rho = force(
            c, numbers, frame, {-1: outer, 0: frame, 1: other}, {-1: rho_outer, 0: rho_own, 1: rho_other}, lists[c], pair
        )
        pos_out[c : c + 1, :] = x
        pos_out[CELLS + c : CELLS + c + 1, :] = y
        vel_out[c : c + 1, :] = vx
        vel_out[CELLS + c : CELLS + c + 1, :] = vy
        rho_out[c : c + 1, :] = rho
        loads = (m * vx, m * vy, m * (sound_sq * (rho - 1.0)), 0.5 * m * (vx * vx + vy * vy))
        owner = (devices == home[c : c + 1, :]).astype(jnp.bfloat16)
        member = shells == home[CELLS + c : CELLS + c + 1, :]
        rest = jnp.concatenate([jnp.where(member, load, 0.0) for load in loads], axis=0)
        for _ in range(3):
            some = rest.astype(jnp.bfloat16)
            owners.append(owner)
            shares.append(some)
            rest = rest - some.astype(jnp.float32)
    total = lax.dot_general(
        jnp.concatenate(owners, axis=1),
        jnp.concatenate(shares, axis=1),
        (((1,), (1,)), ((), ())),
        preferred_element_type=jnp.float32,
    )
    part[...] = jnp.concatenate([total, jnp.zeros((S, S - 64), jnp.float32)], axis=1)


def soil_kernel(arrived, soil, pos, vel, rho, stress_out, pos_out, vel_out, rho_out):
    pos_out[...] = pos[...]
    vel_out[...] = vel[...]
    rho_out[...] = rho[...]
    stress = [soil[k] for k in range(4)]
    rate = [soil[4 + k] for k in range(3)]
    couple = [soil[7 + k] for k in range(3)]
    total = jnp.sum(arrived[...], axis=0, keepdims=True)
    lane = lax.broadcasted_iota(jnp.int32, (16, S), 1)
    row = lax.broadcasted_iota(jnp.int32, (16, S), 0)
    force_x, force_y, force_p, force_e = [
        jnp.sum(jnp.where(lane == row + 16 * k, total, 0.0), axis=1, keepdims=True) for k in range(4)
    ]
    exx = rate[0] + couple[0] * force_x
    eyy = rate[1] + couple[1] * force_y
    exy = rate[2] + couple[2] * force_p
    ezz = -0.5 * (couple[0] + couple[1]) * force_e
    trace = exx + eyy + ezz
    sxx = stress[0] + soil_dt * (2.0 * shear_mod * (exx - trace / 3.0) + bulk_mod * trace)
    syy = stress[1] + soil_dt * (2.0 * shear_mod * (eyy - trace / 3.0) + bulk_mod * trace)
    szz = stress[2] + soil_dt * (2.0 * shear_mod * (ezz - trace / 3.0) + bulk_mod * trace)
    sxy = stress[3] + soil_dt * 2.0 * shear_mod * exy
    first = sxx + syy + szz
    mean = first / 3.0
    dxx = sxx - mean
    dyy = syy - mean
    dzz = szz - mean
    root = jnp.sqrt(0.5 * (dxx * dxx + dyy * dyy + dzz * dzz) + sxy * sxy)
    radius = jnp.maximum(cohesion - friction * first, 0.2 * cohesion)
    factor = radius / jnp.maximum(root, radius)
    stress_out[0] = mean + factor * dxx
    stress_out[1] = mean + factor * dyy
    stress_out[2] = mean + factor * dzz
    stress_out[3] = factor * sxy


def rows_of(n):
    return jax.ShapeDtypeStruct((n, S), jnp.float32)


def kept(n):
    return pltpu.VMEM((n, S), jnp.float32)


VM = pl.BlockSpec(memory_space=pltpu.MemorySpace.VMEM)
SM = pl.BlockSpec(memory_space=pltpu.MemorySpace.SMEM)


def held(a):
    return pltpu.with_memory_space_constraint(a, pltpu.MemorySpace.VMEM)


def local(
    fluid_pos,
    fluid_vel,
    fluid_mass,
    cell_count,
    nb_list,
    iface_dest,
    iface_shell,
    soil_stress,
    soil_rate,
    soil_couple,
):
    n_depth = lax.axis_size("depth")
    n_azim = lax.axis_size("azim")
    parity = (lax.axis_index("depth") % 2).astype(jnp.int32).reshape(1)
    toward_left = [(i, (i - 1) % n_azim) for i in range(n_azim)]
    toward_right = [(i, (i + 1) % n_azim) for i in range(n_azim)]
    pairs = [(i, i ^ 1) for i in range(n_depth)]
    facing = [(i, i + 1 if i % 2 else i - 1) for i in range(n_depth)]
    facing = [(i, j) for i, j in facing if 0 <= j < n_depth]

    def call(kernel, name, shapes, *args):
        return pl.pallas_call(
            kernel,
            out_shape=tuple(kept(n) for n in shapes),
            in_specs=[SM] + [VM] * len(args),
            out_specs=(VM,) * len(shapes),
            name=name,
        )(parity, *[held(a) for a in args])

    def merged(first, second):
        halves = [a[:HALF].reshape(6, CELLS, S) for a in (first, second)]
        return jnp.concatenate(halves, axis=1).reshape(6 * WIDE, S)

    def swapped(a):
        return lax.ppermute(a, "depth", pairs)

    send, first, home, soil = pl.pallas_call(
        pack_kernel,
        out_shape=(
            kept(HALF + 3 * NB),
            kept(NB),
            pltpu.VMEM((2 * CELLS, S), jnp.int32),
            pltpu.VMEM((10,) + soil_stress.shape[1:], jnp.float32),
        ),
        in_specs=[SM] + [VM] * 9,
        out_specs=(VM, VM, VM, VM),
        name="pack",
    )(
        cell_count,
        fluid_pos.reshape(2 * CELLS, S),
        fluid_vel.reshape(2 * CELLS, S),
        fluid_mass.reshape(CELLS, S),
        nb_list.reshape(NB * CELLS, S),
        iface_dest.reshape(CELLS, S),
        iface_shell.reshape(CELLS, S),
        soil_stress,
        soil_rate,
        soil_couple,
    )
    left = lax.ppermute(send, "azim", toward_right)
    frame = merged(left, send)
    other = swapped(frame[:SENT])
    outer = lax.ppermute(
        jnp.concatenate([frame[:SENT], other[:PLACE], left[HALF:], first, send[HALF:]], axis=0), "depth", facing
    )
    rho_own, pair = call(
        middle_first_kernel, "middle_first", (WIDE, CELLS * NT * PAIR), frame, other, outer, left, first, send
    )
    rho_other = swapped(rho_own)
    (rho_outer,) = call(outer_first_kernel, "outer_first", (WIDE,), frame, outer, rho_own)
    (mid,) = call(
        force_first_kernel,
        "force_first",
        (HALF + 2 * NB,),
        frame, other, outer, rho_outer, rho_own, rho_other, left, first, send, pair,
    )

    right = lax.ppermute(mid, "azim", toward_left)
    frame = merged(mid, right)
    other = swapped(frame[:SENT])
    beyond = lax.ppermute(jnp.concatenate([frame[:SENT], other[:PLACE]], axis=0), "depth", facing)
    rho_own, pair = call(
        middle_second_kernel, "middle_second", (WIDE, CELLS * NT * PAIR), frame, other, beyond, right, left, first, send
    )
    rho_other = swapped(rho_own)
    (rho_outer,) = call(outer_second_kernel, "outer_second", (WIDE,), frame, beyond, right, outer, rho_own)
    pos, vel, rho, part = call(
        force_second_kernel,
        "force_second",
        (2 * CELLS, 2 * CELLS, CELLS, S),
        home, frame, other, beyond, rho_outer, rho_own, rho_other, first, send, pair,
    )

    arrived = lax.all_to_all(part, ("depth", "azim"), split_axis=0, concat_axis=0, tiled=True)
    stress_out, pos, vel, rho = pl.pallas_call(
        soil_kernel,
        out_shape=(
            jax.ShapeDtypeStruct(soil_stress.shape, jnp.float32), rows_of(2 * CELLS), rows_of(2 * CELLS), rows_of(CELLS)
        ),
        in_specs=[VM] * 5,
        out_specs=(VM, VM, VM, VM),
        name="soil",
    )(*[held(a) for a in (arrived, soil, pos, vel, rho)])
    return (
        pos.reshape(fluid_pos.shape),
        vel.reshape(fluid_vel.shape),
        rho.reshape(fluid_mass.shape),
        stress_out,
    )


def solution(mesh):
    return jax.shard_map(
        local,
        mesh=mesh,
        in_specs=(
            P(None, "depth", "azim", None),
            P(None, "depth", "azim", None),
            P("depth", "azim", None),
            P("depth", "azim"),
            P(None, "depth", "azim", None),
            P(("depth", "azim"), None, None),
            P(("depth", "azim"), None),
            P(None, ("depth", "azim"), None),
            P(None, ("depth", "azim"), None),
            P(None, ("depth", "azim"), None),
        ),
        out_specs=(
            P(None, "depth", "azim", None),
            P(None, "depth", "azim", None),
            P("depth", "azim", None),
            P(None, ("depth", "azim"), None),
        ),
        check_vma=False,
    )
```

```python
import jax
import jax.numpy as jnp
from jax import lax
from jax.experimental import pallas as pl
from jax.experimental.pallas import tpu as pltpu
from jax.sharding import PartitionSpec as P

step_dt = 0.05
sound_sq = 1.0
visc_alpha = 0.5
soil_dt = 0.1
shear_mod = 1.0
bulk_mod = 2.0
cohesion = 1.0
friction = 0.3

CELLS = 4
NB = 24
NT = 3
WIDE = 8
RING = 6
S = 128
LISTS = NB * CELLS
PX, PY, PM, PVX, PVY, PL = range(6)
HALF = 6 * CELLS
SENT = 5 * WIDE
PLACE = 3 * WIDE
PAIR = 40
NEAR = [(dr, dc) for dr in (-1, 0, 1) for dc in (-1, 0, 1)]


def pack_kernel(count, pos, vel, mass, nb, dest, shell, stress, rate, couple, out, half, first, home, soil):
    soil[0:4] = stress[...]
    soil[4:7] = rate[...]
    soil[7:10] = couple[...]
    home[0:CELLS, :] = dest[...]
    home[CELLS : 2 * CELLS, :] = shell[...]
    lane = lax.broadcasted_iota(jnp.int32, (1, S), 1)
    out[0 : 2 * CELLS, :] = pos[...]
    out[PVX * CELLS : (PVX + 2) * CELLS, :] = vel[...]
    half[0 : 2 * CELLS, :] = pos[...]
    half[PVX * CELLS : (PVX + 2) * CELLS, :] = vel[...]
    for c in range(CELLS):
        live = (lane < count[0, c]).astype(jnp.float32)
        out[PM * CELLS + c : PM * CELLS + c + 1, :] = mass[c : c + 1, :] * live
        out[PL * CELLS + c : PL * CELLS + c + 1, :] = live
        codes = nb[pl.ds(c, NB, stride=CELLS), :].astype(jnp.float32)
        half[PM * CELLS + c : PM * CELLS + c + 1, :] = mass[c : c + 1, :] * live
        half[PL * CELLS + c : PL * CELLS + c + 1, :] = live
        if c:
            out[HALF + NB * (c - 1) : HALF + NB * c, :] = codes
        else:
            first[...] = codes


def spread(row):
    return jnp.broadcast_to(row, (8, S))


def pick(tables, slot, masks):
    out = None
    for table, mask in zip(tables, masks):
        got = jnp.take_along_axis(table, slot, axis=1)
        out = got if out is None else jnp.where(mask, got, out)
    return out


def numbers_of(parity):
    sign = 1 - 2 * parity[0]
    return [3 * (1 + sign * dr) + dc + 1 for dr, dc in NEAR]


def decode(ref, start, numbers):
    code = ref[start : start + 8, :].astype(jnp.int32)
    which = code >> 7
    return code & (S - 1), which, [which == n for n in numbers]


def density(parity, rows, lists, rho_out, pair):
    numbers = numbers_of(parity)
    rho_out[...] = jnp.zeros((WIDE, S), jnp.float32)
    for k in range(RING):
        col = k + 1
        ref, start = rows[0]
        own_x, own_y = spread(ref[start + col : start + col + 1, :]), spread(ref[start + WIDE + col : start + WIDE + col + 1, :])
        own_m = ref[start + PM * WIDE + col : start + PM * WIDE + col + 1, :]

        def table(f):
            out = []
            for dr, dc in NEAR:
                r, base = rows[dr]
                at = base + f * WIDE + col + dc
                out.append(spread(r[at : at + 1, :]))
            return out

        xs, ys, ms = table(PX), table(PY), table(PM)
        total = jnp.zeros((8, S), jnp.float32)
        ref, start = lists[k]
        for t in range(NT):
            slot, which, masks = decode(ref, start + 8 * t, numbers)
            third = (which * 11) >> 5
            dx = own_x - ((third - 1).astype(jnp.float32) + pick(xs, slot, masks))
            dy = own_y - ((which - 3 * third - 1).astype(jnp.float32) + pick(ys, slot, masks))
            mass = pick(ms, slot, masks)
            dist = jnp.sqrt(dx * dx + dy * dy)
            tail = jnp.maximum(1.0 - dist, 0.0)
            cube = tail * tail * tail
            total = total + mass * (cube * tail * (4.0 * dist + 1.0))
            if pair is not None and 1 <= k <= CELLS:
                base = ((k - 1) * NT + t) * PAIR
                pair[base : base + 8, :] = dx
                pair[base + 8 : base + 16, :] = dy
                pair[base + 16 : base + 24, :] = mass
                pair[base + 24 : base + 32, :] = dist * dist + 0.01
                pair[base + 32 : base + 40, :] = 20.0 * cube
        rho = own_m + jnp.sum(total, axis=0, keepdims=True) + jnp.where(own_m > 0.0, 0.0, 1.0)
        rho_out[col : col + 1, :] = rho


def term(rho):
    return sound_sq * (rho - 1.0) / (rho * rho)


def force(c, numbers, frame, states, rhos, lists, pair):
    col = c + 2
    ref, start = lists

    def own(f):
        return frame[f * WIDE + col : f * WIDE + col + 1, :]

    def table(refs, f):
        return [spread(refs[dr][f * WIDE + col + dc : f * WIDE + col + dc + 1, :]) for dr, dc in NEAR]

    own_rho = rhos[0][col : col + 1, :]
    own_vx, own_vy = spread(own(PVX)), spread(own(PVY))
    own_q, own_r = spread(term(own_rho)), spread(own_rho)
    vxs, vys, rs = table(states, PVX), table(states, PVY), table(rhos, 0)
    ax = jnp.zeros((8, S), jnp.float32)
    ay = jnp.zeros((8, S), jnp.float32)
    for t in range(NT):
        slot, _, masks = decode(ref, start + 8 * t, numbers)
        base = (c * NT + t) * PAIR
        dx = pair[base : base + 8, :]
        dy = pair[base + 8 : base + 16, :]
        mass = pair[base + 16 : base + 24, :]
        soft = pair[base + 24 : base + 32, :]
        slope = pair[base + 32 : base + 40, :]
        rho = pick(rs, slot, masks)
        vdot = (own_vx - pick(vxs, slot, masks)) * dx + (own_vy - pick(vys, slot, masks)) * dy
        visc = visc_alpha * jnp.maximum(-vdot, 0.0) / (soft * (0.5 * (own_r + rho)))
        coef = mass * (own_q + term(rho) + visc) * slope
        ax = ax + coef * dx
        ay = ay + coef * dy
    live = own(PL)
    vx = own(PVX) + step_dt * jnp.sum(ax, axis=0, keepdims=True) * live
    vy = own(PVY) + step_dt * jnp.sum(ay, axis=0, keepdims=True) * live
    x = own(PX) + step_dt * vx * live
    y = own(PY) + step_dt * vy * live
    return (x, y, own(PM), vx, vy, live), own_rho


OUTER = SENT + PLACE


def middle_first_kernel(parity, frame, other, outer, left, first, send, rho, pair):
    lists = [(left, HALF + NB * c) for c in range(3)] + [(first, 0), (send, HALF), (send, HALF + NB)]
    density(parity, {-1: (outer, 0), 0: (frame, 0), 1: (other, 0)}, lists, rho, pair)


def outer_first_kernel(parity, frame, outer, after, rho):
    lists = [(outer, OUTER + NB * k) for k in range(RING)]
    density(parity, {-1: (outer, SENT), 0: (outer, 0), 1: (frame, 0)}, lists, rho, None)


def force_first_kernel(parity, frame, other, outer, rho_outer, rho_own, rho_other, left, first, send, pair, out, half):
    numbers = numbers_of(parity)
    lists = [(left, HALF + NB), (left, HALF + 2 * NB), (first, 0), (send, HALF)]
    for c in range(CELLS):
        fields, _ = force(
            c, numbers, frame, {-1: outer, 0: frame, 1: other}, {-1: rho_outer, 0: rho_own, 1: rho_other}, lists[c], pair
        )
        for k, v in enumerate(fields):
            out[k * CELLS + c : k * CELLS + c + 1, :] = v
            half[k * CELLS + c : k * CELLS + c + 1, :] = v
    out[HALF : HALF + NB, :] = outer[OUTER + 3 * NB : OUTER + 4 * NB, :]
    out[HALF + NB : HALF + 2 * NB, :] = first[...]


def middle_second_kernel(parity, frame, other, outer, right, left, first, send, rho, pair):
    lists = [(left, HALF + 2 * NB), (first, 0)] + [(send, HALF + NB * c) for c in range(3)] + [(right, HALF + NB)]
    density(parity, {-1: (outer, 0), 0: (frame, 0), 1: (other, 0)}, lists, rho, pair)


def outer_second_kernel(parity, frame, outer, right, before, after, rho):
    lists = [(before, OUTER + NB * (2 + c)) for c in range(5)] + [(right, HALF)]
    density(parity, {-1: (outer, SENT), 0: (outer, 0), 1: (frame, 0)}, lists, rho, None)


def force_second_kernel(
    parity, home, frame, other, outer, rho_outer, rho_own, rho_other, first, send, pair, pos_out, vel_out, rho_out, part
):
    numbers = numbers_of(parity)
    lists = [(first, 0), (send, HALF), (send, HALF + NB), (send, HALF + 2 * NB)]
    devices = lax.broadcasted_iota(jnp.int32, (S, S), 0)
    shells = lax.broadcasted_iota(jnp.int32, (16, S), 0)
    owners, shares = [], []
    for c in range(CELLS):
        (x, y, m, vx, vy, live), rho = force(
            c, numbers, frame, {-1: outer, 0: frame, 1: other}, {-1: rho_outer, 0: rho_own, 1: rho_other}, lists[c], pair
        )
        pos_out[c : c + 1, :] = x
        pos_out[CELLS + c : CELLS + c + 1, :] = y
        vel_out[c : c + 1, :] = vx
        vel_out[CELLS + c : CELLS + c + 1, :] = vy
        rho_out[c : c + 1, :] = rho
        loads = (m * vx, m * vy, m * (sound_sq * (rho - 1.0)), 0.5 * m * (vx * vx + vy * vy))
        owner = (devices == home[c : c + 1, :]).astype(jnp.bfloat16)
        member = shells == home[CELLS + c : CELLS + c + 1, :]
        rest = jnp.concatenate([jnp.where(member, load, 0.0) for load in loads], axis=0)
        for _ in range(3):
            some = rest.astype(jnp.bfloat16)
            owners.append(owner)
            shares.append(some)
            rest = rest - some.astype(jnp.float32)
    total = lax.dot_general(
        jnp.concatenate(owners, axis=1),
        jnp.concatenate(shares, axis=1),
        (((1,), (1,)), ((), ())),
        preferred_element_type=jnp.float32,
    )
    part[...] = jnp.concatenate([total, jnp.zeros((S, S - 64), jnp.float32)], axis=1)


def soil_kernel(arrived, soil, pos, vel, rho, stress_out, pos_out, vel_out, rho_out):
    pos_out[...] = pos[...]
    vel_out[...] = vel[...]
    rho_out[...] = rho[...]
    stress = [soil[k] for k in range(4)]
    rate = [soil[4 + k] for k in range(3)]
    couple = [soil[7 + k] for k in range(3)]
    total = jnp.sum(arrived[...], axis=0, keepdims=True)
    lane = lax.broadcasted_iota(jnp.int32, (16, S), 1)
    row = lax.broadcasted_iota(jnp.int32, (16, S), 0)
    force_x, force_y, force_p, force_e = [
        jnp.sum(jnp.where(lane == row + 16 * k, total, 0.0), axis=1, keepdims=True) for k in range(4)
    ]
    exx = rate[0] + couple[0] * force_x
    eyy = rate[1] + couple[1] * force_y
    exy = rate[2] + couple[2] * force_p
    ezz = -0.5 * (couple[0] + couple[1]) * force_e
    trace = exx + eyy + ezz
    sxx = stress[0] + soil_dt * (2.0 * shear_mod * (exx - trace / 3.0) + bulk_mod * trace)
    syy = stress[1] + soil_dt * (2.0 * shear_mod * (eyy - trace / 3.0) + bulk_mod * trace)
    szz = stress[2] + soil_dt * (2.0 * shear_mod * (ezz - trace / 3.0) + bulk_mod * trace)
    sxy = stress[3] + soil_dt * 2.0 * shear_mod * exy
    first = sxx + syy + szz
    mean = first / 3.0
    dxx = sxx - mean
    dyy = syy - mean
    dzz = szz - mean
    root = jnp.sqrt(0.5 * (dxx * dxx + dyy * dyy + dzz * dzz) + sxy * sxy)
    radius = jnp.maximum(cohesion - friction * first, 0.2 * cohesion)
    factor = radius / jnp.maximum(root, radius)
    stress_out[0] = mean + factor * dxx
    stress_out[1] = mean + factor * dyy
    stress_out[2] = mean + factor * dzz
    stress_out[3] = factor * sxy


def rows_of(n):
    return jax.ShapeDtypeStruct((n, S), jnp.float32)


def kept(n):
    return pltpu.VMEM((n, S), jnp.float32)


VM = pl.BlockSpec(memory_space=pltpu.MemorySpace.VMEM)
SM = pl.BlockSpec(memory_space=pltpu.MemorySpace.SMEM)


def held(a):
    return pltpu.with_memory_space_constraint(a, pltpu.MemorySpace.VMEM)


def local(
    fluid_pos,
    fluid_vel,
    fluid_mass,
    cell_count,
    nb_list,
    iface_dest,
    iface_shell,
    soil_stress,
    soil_rate,
    soil_couple,
):
    n_depth = lax.axis_size("depth")
    n_azim = lax.axis_size("azim")
    parity = (lax.axis_index("depth") % 2).astype(jnp.int32).reshape(1)
    toward_left = [(i, (i - 1) % n_azim) for i in range(n_azim)]
    toward_right = [(i, (i + 1) % n_azim) for i in range(n_azim)]
    pairs = [(i, i ^ 1) for i in range(n_depth)]
    facing = [(i, i + 1 if i % 2 else i - 1) for i in range(n_depth)]
    facing = [(i, j) for i, j in facing if 0 <= j < n_depth]

    def call(kernel, name, shapes, *args):
        return pl.pallas_call(
            kernel,
            out_shape=tuple(kept(n) for n in shapes),
            in_specs=[SM] + [VM] * len(args),
            out_specs=(VM,) * len(shapes),
            name=name,
        )(parity, *[held(a) for a in args])

    def merged(first, second):
        halves = [a[:HALF].reshape(6, CELLS, S) for a in (first, second)]
        return jnp.concatenate(halves, axis=1).reshape(6 * WIDE, S)

    def crossing(step):
        return [
            (r * n_azim + c, (r ^ 1) * n_azim + (c + step) % n_azim) for r in range(n_depth) for c in range(n_azim)
        ]

    def swapped(a):
        return lax.ppermute(a, "depth", pairs)

    send, half, first, home, soil = pl.pallas_call(
        pack_kernel,
        out_shape=(
            kept(HALF + 3 * NB),
            kept(HALF),
            kept(NB),
            pltpu.VMEM((2 * CELLS, S), jnp.int32),
            pltpu.VMEM((10,) + soil_stress.shape[1:], jnp.float32),
        ),
        in_specs=[SM] + [VM] * 9,
        out_specs=(VM,) * 5,
        name="pack",
    )(
        cell_count,
        fluid_pos.reshape(2 * CELLS, S),
        fluid_vel.reshape(2 * CELLS, S),
        fluid_mass.reshape(CELLS, S),
        nb_list.reshape(NB * CELLS, S),
        iface_dest.reshape(CELLS, S),
        iface_shell.reshape(CELLS, S),
        soil_stress,
        soil_rate,
        soil_couple,
    )
    left = lax.ppermute(send, "azim", toward_right)
    across = lax.ppermute(half, ("depth", "azim"), crossing(1))
    beside = swapped(half)
    left, across, beside = lax.optimization_barrier((left, across, beside))
    frame = merged(left, send)
    other = merged(across, beside)
    outer = lax.ppermute(
        jnp.concatenate([frame[:SENT], other[:PLACE], left[HALF:], first, send[HALF:]], axis=0), "depth", facing
    )
    rho_own, pair = call(
        middle_first_kernel, "middle_first", (WIDE, CELLS * NT * PAIR), frame, other, outer, left, first, send
    )
    rho_other = swapped(rho_own)
    (rho_outer,) = call(outer_first_kernel, "outer_first", (WIDE,), frame, outer, rho_own)
    mid, half = call(
        force_first_kernel,
        "force_first",
        (HALF + 2 * NB, HALF),
        frame, other, outer, rho_outer, rho_own, rho_other, left, first, send, pair,
    )

    right = lax.ppermute(mid, "azim", toward_left)
    across = lax.ppermute(half, ("depth", "azim"), crossing(-1))
    beside = swapped(half)
    right, across, beside = lax.optimization_barrier((right, across, beside))
    frame = merged(mid, right)
    other = merged(beside, across)
    beyond = lax.ppermute(jnp.concatenate([frame[:SENT], other[:PLACE]], axis=0), "depth", facing)
    rho_own, pair = call(
        middle_second_kernel, "middle_second", (WIDE, CELLS * NT * PAIR), frame, other, beyond, right, left, first, send
    )
    rho_other = swapped(rho_own)
    (rho_outer,) = call(outer_second_kernel, "outer_second", (WIDE,), frame, beyond, right, outer, rho_own)
    pos, vel, rho, part = call(
        force_second_kernel,
        "force_second",
        (2 * CELLS, 2 * CELLS, CELLS, S),
        home, frame, other, beyond, rho_outer, rho_own, rho_other, first, send, pair,
    )

    arrived = lax.all_to_all(part, ("depth", "azim"), split_axis=0, concat_axis=0, tiled=True)
    stress_out, pos, vel, rho = pl.pallas_call(
        soil_kernel,
        out_shape=(
            jax.ShapeDtypeStruct(soil_stress.shape, jnp.float32), rows_of(2 * CELLS), rows_of(2 * CELLS), rows_of(CELLS)
        ),
        in_specs=[VM] * 5,
        out_specs=(VM, VM, VM, VM),
        name="soil",
    )(*[held(a) for a in (arrived, soil, pos, vel, rho)])
    return (
        pos.reshape(fluid_pos.shape),
        vel.reshape(fluid_vel.shape),
        rho.reshape(fluid_mass.shape),
        stress_out,
    )


def solution(mesh):
    return jax.shard_map(
        local,
        mesh=mesh,
        in_specs=(
            P(None, "depth", "azim", None),
            P(None, "depth", "azim", None),
            P("depth", "azim", None),
            P("depth", "azim"),
            P(None, "depth", "azim", None),
            P(("depth", "azim"), None, None),
            P(("depth", "azim"), None),
            P(None, ("depth", "azim"), None),
            P(None, ("depth", "azim"), None),
            P(None, ("depth", "azim"), None),
        ),
        out_specs=(
            P(None, "depth", "azim", None),
            P(None, "depth", "azim", None),
            P("depth", "azim", None),
            P(None, ("depth", "azim"), None),
        ),
        check_vma=False,
    )
```

```python
import jax
import jax.numpy as jnp
from jax import lax
from jax.experimental import pallas as pl
from jax.experimental.pallas import tpu as pltpu
from jax.sharding import PartitionSpec as P

step_dt = 0.05
sound_sq = 1.0
visc_alpha = 0.5
soil_dt = 0.1
shear_mod = 1.0
bulk_mod = 2.0
cohesion = 1.0
friction = 0.3

CELLS = 4
NB = 24
NT = 3
WIDE = 8
RING = 6
S = 128
LISTS = NB * CELLS
PX, PY, PM, PVX, PVY, PL = range(6)
HALF = 6 * CELLS
SENT = 5 * WIDE
PLACE = 3 * WIDE
PAIR = 32
EARLY = 24
NEAR = [(dr, dc) for dr in (-1, 0, 1) for dc in (-1, 0, 1)]


def pack_kernel(count, pos, vel, mass, nb, dest, shell, stress, rate, couple, out, half, first, home, soil):
    soil[0:4] = stress[...]
    soil[4:7] = rate[...]
    soil[7:10] = couple[...]
    home[0:CELLS, :] = dest[...]
    home[CELLS : 2 * CELLS, :] = shell[...]
    lane = lax.broadcasted_iota(jnp.int32, (1, S), 1)
    out[0 : 2 * CELLS, :] = pos[...]
    out[PVX * CELLS : (PVX + 2) * CELLS, :] = vel[...]
    half[0 : 2 * CELLS, :] = pos[...]
    half[PVX * CELLS : (PVX + 2) * CELLS, :] = vel[...]
    for c in range(CELLS):
        live = (lane < count[0, c]).astype(jnp.float32)
        out[PM * CELLS + c : PM * CELLS + c + 1, :] = mass[c : c + 1, :] * live
        out[PL * CELLS + c : PL * CELLS + c + 1, :] = live
        codes = nb[pl.ds(c, NB, stride=CELLS), :].astype(jnp.float32)
        half[PM * CELLS + c : PM * CELLS + c + 1, :] = mass[c : c + 1, :] * live
        half[PL * CELLS + c : PL * CELLS + c + 1, :] = live
        if c:
            out[HALF + NB * (c - 1) : HALF + NB * c, :] = codes
        else:
            first[...] = codes


def spread(row):
    return jnp.broadcast_to(row, (8, S))


def pick(tables, slot, masks, out=None):
    for table, mask in zip(tables, masks):
        got = jnp.take_along_axis(table, slot, axis=1)
        out = got if out is None else jnp.where(mask, got, out)
    return out


def numbers_of(parity):
    sign = 1 - 2 * parity[0]
    return [3 * (1 + sign * dr) + dc + 1 for dr, dc in NEAR]


def decode(ref, start, numbers):
    code = ref[start : start + 8, :].astype(jnp.int32)
    which = code >> 7
    return code & (S - 1), which, [which == n for n in numbers]


def early(parity, rows, lists, out):
    numbers = numbers_of(parity)[3:]
    for k in range(RING):
        ref, start = lists[k]
        for t in range(NT):
            slot, _, masks = decode(ref, start + 8 * t, numbers)
            for f in (PX, PY, PM):
                tables = []
                for dr, dc in NEAR[3:]:
                    at = f * WIDE + k + 1 + dc
                    tables.append(spread(rows[dr][at : at + 1, :]))
                base = (k * NT + t) * EARLY + 8 * f
                out[base : base + 8, :] = pick(tables, slot, masks)


def density(parity, rows, lists, rho_out, pair=None, gathered=None):
    near = NEAR if gathered is None else NEAR[:3]
    numbers = numbers_of(parity)[: len(near)]
    rho_out[...] = jnp.zeros((WIDE, S), jnp.float32)
    for k in range(RING):
        col = k + 1
        ref, start = rows[0]
        own_x, own_y = spread(ref[start + col : start + col + 1, :]), spread(ref[start + WIDE + col : start + WIDE + col + 1, :])
        own_m = ref[start + PM * WIDE + col : start + PM * WIDE + col + 1, :]

        def table(f):
            out = []
            for dr, dc in near:
                r, base = rows[dr]
                at = base + f * WIDE + col + dc
                out.append(spread(r[at : at + 1, :]))
            return out

        xs, ys, ms = table(PX), table(PY), table(PM)
        total = jnp.zeros((8, S), jnp.float32)
        ref, start = lists[k]
        for t in range(NT):
            slot, which, masks = decode(ref, start + 8 * t, numbers)
            third = (which * 11) >> 5
            before = [None] * 3
            if gathered is not None:
                base = (k * NT + t) * EARLY
                before = [gathered[base + 8 * f : base + 8 * f + 8, :] for f in range(3)]
            dx = own_x - ((third - 1).astype(jnp.float32) + pick(xs, slot, masks, before[0]))
            dy = own_y - ((which - 3 * third - 1).astype(jnp.float32) + pick(ys, slot, masks, before[1]))
            mass = pick(ms, slot, masks, before[2])
            dist = jnp.sqrt(dx * dx + dy * dy)
            tail = jnp.maximum(1.0 - dist, 0.0)
            cube = tail * tail * tail
            total = total + mass * (cube * tail * (4.0 * dist + 1.0))
            if pair is not None and 1 <= k <= CELLS:
                base = ((k - 1) * NT + t) * PAIR
                pair[base : base + 8, :] = dx
                pair[base + 8 : base + 16, :] = dy
                pair[base + 16 : base + 24, :] = dist * dist + 0.01
                pair[base + 24 : base + 32, :] = mass * (20.0 * cube)
        rho = own_m + jnp.sum(total, axis=0, keepdims=True) + jnp.where(own_m > 0.0, 0.0, 1.0)
        rho_out[col : col + 1, :] = rho


def term(rho):
    return sound_sq * (rho - 1.0) / (rho * rho)


def drag(parity, frame, states, lists, pair, out):
    numbers = numbers_of(parity)
    for c in range(CELLS):
        col = c + 2
        ref, start = lists[c]

        def table(f):
            return [spread(states[dr][f * WIDE + col + dc : f * WIDE + col + dc + 1, :]) for dr, dc in NEAR]

        own_vx = spread(frame[PVX * WIDE + col : PVX * WIDE + col + 1, :])
        own_vy = spread(frame[PVY * WIDE + col : PVY * WIDE + col + 1, :])
        vxs, vys = table(PVX), table(PVY)
        for t in range(NT):
            slot, _, masks = decode(ref, start + 8 * t, numbers)
            base = (c * NT + t) * PAIR
            dx = pair[base : base + 8, :]
            dy = pair[base + 8 : base + 16, :]
            vdot = (own_vx - pick(vxs, slot, masks)) * dx + (own_vy - pick(vys, slot, masks)) * dy
            base = (c * NT + t) * 8
            out[base : base + 8, :] = visc_alpha * jnp.maximum(-vdot, 0.0) / pair[4 * base + 16 : 4 * base + 24, :]


def force(c, numbers, frame, rhos, lists, pair, dragged):
    col = c + 2
    ref, start = lists

    def own(f):
        return frame[f * WIDE + col : f * WIDE + col + 1, :]

    own_rho = rhos[0][col : col + 1, :]
    own_q, own_r = spread(term(own_rho)), spread(own_rho)
    tables = [spread(rhos[dr][col + dc : col + dc + 1, :]) for dr, dc in NEAR]
    ax = jnp.zeros((8, S), jnp.float32)
    ay = jnp.zeros((8, S), jnp.float32)
    for t in range(NT):
        slot, _, masks = decode(ref, start + 8 * t, numbers)
        base = (c * NT + t) * PAIR
        rho = pick(tables, slot, masks)
        visc = dragged[base // 4 : base // 4 + 8, :] / (0.5 * (own_r + rho))
        coef = (own_q + term(rho) + visc) * pair[base + 24 : base + 32, :]
        ax = ax + coef * pair[base : base + 8, :]
        ay = ay + coef * pair[base + 8 : base + 16, :]
    live = own(PL)
    vx = own(PVX) + step_dt * jnp.sum(ax, axis=0, keepdims=True) * live
    vy = own(PVY) + step_dt * jnp.sum(ay, axis=0, keepdims=True) * live
    x = own(PX) + step_dt * vx * live
    y = own(PY) + step_dt * vy * live
    return (x, y, own(PM), vx, vy, live), own_rho


OUTER = SENT + PLACE


def lists_first(left, first, send):
    return [(left, HALF + NB * c) for c in range(3)] + [(first, 0), (send, HALF), (send, HALF + NB)]


def early_first_kernel(parity, frame, other, left, first, send, out):
    early(parity, {0: frame, 1: other}, lists_first(left, first, send), out)


def middle_first_kernel(parity, frame, outer, left, first, send, gathered, rho, pair):
    density(parity, {-1: (outer, 0), 0: (frame, 0)}, lists_first(left, first, send), rho, pair, gathered)


def outer_first_kernel(parity, frame, other, outer, left, first, send, pair, after, rho, dragged):
    lists = [(outer, OUTER + NB * k) for k in range(RING)]
    density(parity, {-1: (outer, SENT), 0: (outer, 0), 1: (frame, 0)}, lists, rho)
    drag(parity, frame, {-1: outer, 0: frame, 1: other}, lists_first(left, first, send)[1:], pair, dragged)


def force_first_kernel(parity, frame, outer, rho_outer, rho_own, rho_other, left, first, send, pair, dragged, out, half):
    numbers = numbers_of(parity)
    lists = lists_first(left, first, send)[1:]
    for c in range(CELLS):
        fields, _ = force(
            c, numbers, frame, {-1: rho_outer, 0: rho_own, 1: rho_other}, lists[c], pair, dragged
        )
        for k, v in enumerate(fields):
            out[k * CELLS + c : k * CELLS + c + 1, :] = v
            half[k * CELLS + c : k * CELLS + c + 1, :] = v
    out[HALF : HALF + NB, :] = outer[OUTER + 3 * NB : OUTER + 4 * NB, :]
    out[HALF + NB : HALF + 2 * NB, :] = first[...]


def lists_second(right, left, first, send):
    return [(left, HALF + 2 * NB), (first, 0)] + [(send, HALF + NB * c) for c in range(3)] + [(right, HALF + NB)]


def early_second_kernel(parity, frame, other, right, left, first, send, out):
    early(parity, {0: frame, 1: other}, lists_second(right, left, first, send), out)


def middle_second_kernel(parity, frame, outer, right, left, first, send, gathered, rho, pair):
    density(parity, {-1: (outer, 0), 0: (frame, 0)}, lists_second(right, left, first, send), rho, pair, gathered)


def outer_second_kernel(parity, frame, other, outer, right, before, first, send, pair, after, rho, dragged):
    lists = [(before, OUTER + NB * (2 + c)) for c in range(5)] + [(right, HALF)]
    density(parity, {-1: (outer, SENT), 0: (outer, 0), 1: (frame, 0)}, lists, rho)
    lists = [(first, 0)] + [(send, HALF + NB * c) for c in range(3)]
    drag(parity, frame, {-1: outer, 0: frame, 1: other}, lists, pair, dragged)


def force_second_kernel(
    parity, home, frame, rho_outer, rho_own, rho_other, first, send, pair, dragged, pos_out, vel_out, rho_out, part
):
    numbers = numbers_of(parity)
    lists = [(first, 0), (send, HALF), (send, HALF + NB), (send, HALF + 2 * NB)]
    devices = lax.broadcasted_iota(jnp.int32, (S, S), 0)
    shells = lax.broadcasted_iota(jnp.int32, (16, S), 0)
    owners, shares = [], []
    for c in range(CELLS):
        (x, y, m, vx, vy, live), rho = force(
            c, numbers, frame, {-1: rho_outer, 0: rho_own, 1: rho_other}, lists[c], pair, dragged
        )
        pos_out[c : c + 1, :] = x
        pos_out[CELLS + c : CELLS + c + 1, :] = y
        vel_out[c : c + 1, :] = vx
        vel_out[CELLS + c : CELLS + c + 1, :] = vy
        rho_out[c : c + 1, :] = rho
        loads = (m * vx, m * vy, m * (sound_sq * (rho - 1.0)), 0.5 * m * (vx * vx + vy * vy))
        owner = (devices == home[c : c + 1, :]).astype(jnp.bfloat16)
        member = shells == home[CELLS + c : CELLS + c + 1, :]
        rest = jnp.concatenate([jnp.where(member, load, 0.0) for load in loads], axis=0)
        for _ in range(3):
            some = rest.astype(jnp.bfloat16)
            owners.append(owner)
            shares.append(some)
            rest = rest - some.astype(jnp.float32)
    total = lax.dot_general(
        jnp.concatenate(owners, axis=1),
        jnp.concatenate(shares, axis=1),
        (((1,), (1,)), ((), ())),
        preferred_element_type=jnp.float32,
    )
    part[...] = jnp.concatenate([total, jnp.zeros((S, S - 64), jnp.float32)], axis=1)


def soil_kernel(arrived, soil, pos, vel, rho, stress_out, pos_out, vel_out, rho_out):
    pos_out[...] = pos[...]
    vel_out[...] = vel[...]
    rho_out[...] = rho[...]
    stress = [soil[k] for k in range(4)]
    rate = [soil[4 + k] for k in range(3)]
    couple = [soil[7 + k] for k in range(3)]
    total = jnp.sum(arrived[...], axis=0, keepdims=True)
    lane = lax.broadcasted_iota(jnp.int32, (16, S), 1)
    row = lax.broadcasted_iota(jnp.int32, (16, S), 0)
    force_x, force_y, force_p, force_e = [
        jnp.sum(jnp.where(lane == row + 16 * k, total, 0.0), axis=1, keepdims=True) for k in range(4)
    ]
    exx = rate[0] + couple[0] * force_x
    eyy = rate[1] + couple[1] * force_y
    exy = rate[2] + couple[2] * force_p
    ezz = -0.5 * (couple[0] + couple[1]) * force_e
    trace = exx + eyy + ezz
    sxx = stress[0] + soil_dt * (2.0 * shear_mod * (exx - trace / 3.0) + bulk_mod * trace)
    syy = stress[1] + soil_dt * (2.0 * shear_mod * (eyy - trace / 3.0) + bulk_mod * trace)
    szz = stress[2] + soil_dt * (2.0 * shear_mod * (ezz - trace / 3.0) + bulk_mod * trace)
    sxy = stress[3] + soil_dt * 2.0 * shear_mod * exy
    first = sxx + syy + szz
    mean = first / 3.0
    dxx = sxx - mean
    dyy = syy - mean
    dzz = szz - mean
    root = jnp.sqrt(0.5 * (dxx * dxx + dyy * dyy + dzz * dzz) + sxy * sxy)
    radius = jnp.maximum(cohesion - friction * first, 0.2 * cohesion)
    factor = radius / jnp.maximum(root, radius)
    stress_out[0] = mean + factor * dxx
    stress_out[1] = mean + factor * dyy
    stress_out[2] = mean + factor * dzz
    stress_out[3] = factor * sxy


def rows_of(n):
    return jax.ShapeDtypeStruct((n, S), jnp.float32)


def kept(n):
    return pltpu.VMEM((n, S), jnp.float32)


VM = pl.BlockSpec(memory_space=pltpu.MemorySpace.VMEM)
SM = pl.BlockSpec(memory_space=pltpu.MemorySpace.SMEM)


def held(a):
    return pltpu.with_memory_space_constraint(a, pltpu.MemorySpace.VMEM)


def local(
    fluid_pos,
    fluid_vel,
    fluid_mass,
    cell_count,
    nb_list,
    iface_dest,
    iface_shell,
    soil_stress,
    soil_rate,
    soil_couple,
):
    n_depth = lax.axis_size("depth")
    n_azim = lax.axis_size("azim")
    parity = (lax.axis_index("depth") % 2).astype(jnp.int32).reshape(1)
    toward_left = [(i, (i - 1) % n_azim) for i in range(n_azim)]
    toward_right = [(i, (i + 1) % n_azim) for i in range(n_azim)]
    pairs = [(i, i ^ 1) for i in range(n_depth)]
    facing = [(i, i + 1 if i % 2 else i - 1) for i in range(n_depth)]
    facing = [(i, j) for i, j in facing if 0 <= j < n_depth]

    def call(kernel, name, shapes, *args):
        return pl.pallas_call(
            kernel,
            out_shape=tuple(kept(n) for n in shapes),
            in_specs=[SM] + [VM] * len(args),
            out_specs=(VM,) * len(shapes),
            name=name,
        )(parity, *[held(a) for a in args])

    def merged(first, second):
        halves = [a[:HALF].reshape(6, CELLS, S) for a in (first, second)]
        return jnp.concatenate(halves, axis=1).reshape(6 * WIDE, S)

    def crossing(step):
        return [
            (r * n_azim + c, (r ^ 1) * n_azim + (c + step) % n_azim) for r in range(n_depth) for c in range(n_azim)
        ]

    def swapped(a):
        return lax.ppermute(a, "depth", pairs)

    send, half, first, home, soil = pl.pallas_call(
        pack_kernel,
        out_shape=(
            kept(HALF + 3 * NB),
            kept(HALF),
            kept(NB),
            pltpu.VMEM((2 * CELLS, S), jnp.int32),
            pltpu.VMEM((10,) + soil_stress.shape[1:], jnp.float32),
        ),
        in_specs=[SM] + [VM] * 9,
        out_specs=(VM,) * 5,
        name="pack",
    )(
        cell_count,
        fluid_pos.reshape(2 * CELLS, S),
        fluid_vel.reshape(2 * CELLS, S),
        fluid_mass.reshape(CELLS, S),
        nb_list.reshape(NB * CELLS, S),
        iface_dest.reshape(CELLS, S),
        iface_shell.reshape(CELLS, S),
        soil_stress,
        soil_rate,
        soil_couple,
    )
    left = lax.ppermute(send, "azim", toward_right)
    across = lax.ppermute(half, ("depth", "azim"), crossing(1))
    beside = swapped(half)
    left, across, beside = lax.optimization_barrier((left, across, beside))
    frame = merged(left, send)
    other = merged(across, beside)
    outer = lax.ppermute(
        jnp.concatenate([frame[:SENT], other[:PLACE], left[HALF:], first, send[HALF:]], axis=0), "depth", facing
    )
    tiles = CELLS * NT
    (gathered,) = call(
        early_first_kernel, "early_first", (RING * NT * EARLY,), frame, other, left, first, send
    )
    rho_own, pair = call(
        middle_first_kernel, "middle_first", (WIDE, tiles * PAIR), frame, outer, left, first, send, gathered
    )
    rho_other = swapped(rho_own)
    rho_outer, dragged = call(
        outer_first_kernel, "outer_first", (WIDE, tiles * 8), frame, other, outer, left, first, send, pair, rho_own
    )
    mid, half = call(
        force_first_kernel,
        "force_first",
        (HALF + 2 * NB, HALF),
        frame, outer, rho_outer, rho_own, rho_other, left, first, send, pair, dragged,
    )

    right = lax.ppermute(mid, "azim", toward_left)
    across = lax.ppermute(half, ("depth", "azim"), crossing(-1))
    beside = swapped(half)
    right, across, beside = lax.optimization_barrier((right, across, beside))
    frame = merged(mid, right)
    other = merged(beside, across)
    beyond = lax.ppermute(jnp.concatenate([frame[:SENT], other[:PLACE]], axis=0), "depth", facing)
    (gathered,) = call(
        early_second_kernel, "early_second", (RING * NT * EARLY,), frame, other, right, left, first, send
    )
    rho_own, pair = call(
        middle_second_kernel, "middle_second", (WIDE, tiles * PAIR), frame, beyond, right, left, first, send, gathered
    )
    rho_other = swapped(rho_own)
    rho_outer, dragged = call(
        outer_second_kernel,
        "outer_second",
        (WIDE, tiles * 8),
        frame, other, beyond, right, outer, first, send, pair, rho_own,
    )
    pos, vel, rho, part = call(
        force_second_kernel,
        "force_second",
        (2 * CELLS, 2 * CELLS, CELLS, S),
        home, frame, rho_outer, rho_own, rho_other, first, send, pair, dragged,
    )

    arrived = lax.all_to_all(part, ("depth", "azim"), split_axis=0, concat_axis=0, tiled=True)
    stress_out, pos, vel, rho = pl.pallas_call(
        soil_kernel,
        out_shape=(
            jax.ShapeDtypeStruct(soil_stress.shape, jnp.float32), rows_of(2 * CELLS), rows_of(2 * CELLS), rows_of(CELLS)
        ),
        in_specs=[VM] * 5,
        out_specs=(VM, VM, VM, VM),
        name="soil",
    )(*[held(a) for a in (arrived, soil, pos, vel, rho)])
    return (
        pos.reshape(fluid_pos.shape),
        vel.reshape(fluid_vel.shape),
        rho.reshape(fluid_mass.shape),
        stress_out,
    )


def solution(mesh):
    return jax.shard_map(
        local,
        mesh=mesh,
        in_specs=(
            P(None, "depth", "azim", None),
            P(None, "depth", "azim", None),
            P("depth", "azim", None),
            P("depth", "azim"),
            P(None, "depth", "azim", None),
            P(("depth", "azim"), None, None),
            P(("depth", "azim"), None),
            P(None, ("depth", "azim"), None),
            P(None, ("depth", "azim"), None),
            P(None, ("depth", "azim"), None),
        ),
        out_specs=(
            P(None, "depth", "azim", None),
            P(None, "depth", "azim", None),
            P("depth", "azim", None),
            P(None, ("depth", "azim"), None),
        ),
        check_vma=False,
    )
```

```python
import jax
import jax.numpy as jnp
from jax import lax
from jax.experimental import pallas as pl
from jax.experimental.pallas import tpu as pltpu
from jax.sharding import PartitionSpec as P

step_dt = 0.05
sound_sq = 1.0
visc_alpha = 0.5
soil_dt = 0.1
shear_mod = 1.0
bulk_mod = 2.0
cohesion = 1.0
friction = 0.3

CELLS = 4
NB = 24
NT = 3
WIDE = 8
RING = 6
S = 128
LISTS = NB * CELLS
PX, PY, PM, PVX, PVY, PL = range(6)
HALF = 6 * CELLS
SENT = 5 * WIDE
PLACE = 3 * WIDE
PAIR = 32
EARLY = 24
NEAR = [(dr, dc) for dr in (-1, 0, 1) for dc in (-1, 0, 1)]


def pack_kernel(count, pos, vel, mass, nb, dest, shell, stress, rate, couple, out, half, first, home, soil):
    soil[0:4] = stress[...]
    soil[4:7] = rate[...]
    soil[7:10] = couple[...]
    home[0:CELLS, :] = dest[...]
    home[CELLS : 2 * CELLS, :] = shell[...]
    lane = lax.broadcasted_iota(jnp.int32, (1, S), 1)
    out[0 : 2 * CELLS, :] = pos[...]
    out[PVX * CELLS : (PVX + 2) * CELLS, :] = vel[...]
    half[0 : 2 * CELLS, :] = pos[...]
    half[PVX * CELLS : (PVX + 2) * CELLS, :] = vel[...]
    for c in range(CELLS):
        live = (lane < count[0, c]).astype(jnp.float32)
        out[PM * CELLS + c : PM * CELLS + c + 1, :] = mass[c : c + 1, :] * live
        out[PL * CELLS + c : PL * CELLS + c + 1, :] = live
        codes = nb[pl.ds(c, NB, stride=CELLS), :].astype(jnp.float32)
        half[PM * CELLS + c : PM * CELLS + c + 1, :] = mass[c : c + 1, :] * live
        half[PL * CELLS + c : PL * CELLS + c + 1, :] = live
        if c:
            out[HALF + NB * (c - 1) : HALF + NB * c, :] = codes
        else:
            first[...] = codes


def spread(row):
    return jnp.broadcast_to(row, (8, S))


def pick(tables, slot, masks, out=None):
    for table, mask in zip(tables, masks):
        got = jnp.take_along_axis(table, slot, axis=1)
        out = got if out is None else jnp.where(mask, got, out)
    return out


def numbers_of(parity):
    sign = 1 - 2 * parity[0]
    return [3 * (1 + sign * dr) + dc + 1 for dr, dc in NEAR]


def decode(ref, start, numbers):
    code = ref[start : start + 8, :].astype(jnp.int32)
    which = code >> 7
    return code & (S - 1), which, [which == n for n in numbers]


def early(parity, rows, lists, out):
    numbers = numbers_of(parity)[3:]
    for k in range(RING):
        ref, start = lists[k]
        for t in range(NT):
            slot, _, masks = decode(ref, start + 8 * t, numbers)
            for f in (PX, PY, PM):
                tables = []
                for dr, dc in NEAR[3:]:
                    at = f * WIDE + k + 1 + dc
                    tables.append(spread(rows[dr][at : at + 1, :]))
                base = (k * NT + t) * EARLY + 8 * f
                out[base : base + 8, :] = pick(tables, slot, masks)


def density(parity, rows, lists, rho_out, pair=None, gathered=None):
    near = NEAR if gathered is None else NEAR[:3]
    numbers = numbers_of(parity)[: len(near)]
    rho_out[...] = jnp.zeros((WIDE, S), jnp.float32)
    for k in range(RING):
        col = k + 1
        ref, start = rows[0]
        own_x, own_y = spread(ref[start + col : start + col + 1, :]), spread(ref[start + WIDE + col : start + WIDE + col + 1, :])
        own_m = ref[start + PM * WIDE + col : start + PM * WIDE + col + 1, :]

        def table(f):
            out = []
            for dr, dc in near:
                r, base = rows[dr]
                at = base + f * WIDE + col + dc
                out.append(spread(r[at : at + 1, :]))
            return out

        xs, ys, ms = table(PX), table(PY), table(PM)
        total = jnp.zeros((8, S), jnp.float32)
        ref, start = lists[k]
        for t in range(NT):
            slot, which, masks = decode(ref, start + 8 * t, numbers)
            third = (which * 11) >> 5
            before = [None] * 3
            if gathered is not None:
                base = (k * NT + t) * EARLY
                before = [gathered[base + 8 * f : base + 8 * f + 8, :] for f in range(3)]
            dx = own_x - ((third - 1).astype(jnp.float32) + pick(xs, slot, masks, before[0]))
            dy = own_y - ((which - 3 * third - 1).astype(jnp.float32) + pick(ys, slot, masks, before[1]))
            mass = pick(ms, slot, masks, before[2])
            dist = jnp.sqrt(dx * dx + dy * dy)
            tail = jnp.maximum(1.0 - dist, 0.0)
            cube = tail * tail * tail
            total = total + mass * (cube * tail * (4.0 * dist + 1.0))
            if pair is not None and 1 <= k <= CELLS:
                base = ((k - 1) * NT + t) * PAIR
                pair[base : base + 8, :] = dx
                pair[base + 8 : base + 16, :] = dy
                pair[base + 16 : base + 24, :] = dist * dist + 0.01
                pair[base + 24 : base + 32, :] = mass * (20.0 * cube)
        rho = own_m + jnp.sum(total, axis=0, keepdims=True) + jnp.where(own_m > 0.0, 0.0, 1.0)
        rho_out[col : col + 1, :] = rho


def term(rho):
    return sound_sq * (rho - 1.0) / (rho * rho)


def drag(parity, frame, states, lists, pair, out):
    numbers = numbers_of(parity)
    for c in range(CELLS):
        col = c + 2
        ref, start = lists[c]

        def table(f):
            return [spread(states[dr][f * WIDE + col + dc : f * WIDE + col + dc + 1, :]) for dr, dc in NEAR]

        own_vx = spread(frame[PVX * WIDE + col : PVX * WIDE + col + 1, :])
        own_vy = spread(frame[PVY * WIDE + col : PVY * WIDE + col + 1, :])
        vxs, vys = table(PVX), table(PVY)
        for t in range(NT):
            slot, _, masks = decode(ref, start + 8 * t, numbers)
            base = (c * NT + t) * PAIR
            dx = pair[base : base + 8, :]
            dy = pair[base + 8 : base + 16, :]
            vdot = (own_vx - pick(vxs, slot, masks)) * dx + (own_vy - pick(vys, slot, masks)) * dy
            base = (c * NT + t) * 8
            out[base : base + 8, :] = visc_alpha * jnp.maximum(-vdot, 0.0) / pair[4 * base + 16 : 4 * base + 24, :]


def force(c, numbers, frame, rhos, lists, pair, dragged):
    col = c + 2
    ref, start = lists

    def own(f):
        return frame[f * WIDE + col : f * WIDE + col + 1, :]

    own_rho = rhos[0][col : col + 1, :]
    own_q, own_r = spread(term(own_rho)), spread(own_rho)
    tables = [spread(rhos[dr][col + dc : col + dc + 1, :]) for dr, dc in NEAR]
    ax = jnp.zeros((8, S), jnp.float32)
    ay = jnp.zeros((8, S), jnp.float32)
    for t in range(NT):
        slot, _, masks = decode(ref, start + 8 * t, numbers)
        base = (c * NT + t) * PAIR
        rho = pick(tables, slot, masks)
        visc = dragged[base // 4 : base // 4 + 8, :] / (0.5 * (own_r + rho))
        coef = (own_q + term(rho) + visc) * pair[base + 24 : base + 32, :]
        ax = ax + coef * pair[base : base + 8, :]
        ay = ay + coef * pair[base + 8 : base + 16, :]
    live = own(PL)
    vx = own(PVX) + step_dt * jnp.sum(ax, axis=0, keepdims=True) * live
    vy = own(PVY) + step_dt * jnp.sum(ay, axis=0, keepdims=True) * live
    x = own(PX) + step_dt * vx * live
    y = own(PY) + step_dt * vy * live
    return (x, y, own(PM), vx, vy, live), own_rho


OUTER = SENT + PLACE


def lists_first(left, first, send):
    return [(left, HALF + NB * c) for c in range(3)] + [(first, 0), (send, HALF), (send, HALF + NB)]


def early_first_kernel(parity, frame, other, left, first, send, out):
    early(parity, {0: frame, 1: other}, lists_first(left, first, send), out)


def middle_first_kernel(parity, frame, outer, left, first, send, gathered, rho, pair):
    density(parity, {-1: (outer, 0), 0: (frame, 0)}, lists_first(left, first, send), rho, pair, gathered)


def outer_first_kernel(parity, frame, other, outer, left, first, send, pair, after, rho, dragged):
    lists = [(outer, OUTER + NB * k) for k in range(RING)]
    density(parity, {-1: (outer, SENT), 0: (outer, 0), 1: (frame, 0)}, lists, rho)
    drag(parity, frame, {-1: outer, 0: frame, 1: other}, lists_first(left, first, send)[1:], pair, dragged)


def force_first_kernel(parity, frame, outer, rho_outer, rho_own, rho_other, left, first, send, pair, dragged, out, half):
    numbers = numbers_of(parity)
    lists = lists_first(left, first, send)[1:]
    for c in range(CELLS):
        fields, _ = force(
            c, numbers, frame, {-1: rho_outer, 0: rho_own, 1: rho_other}, lists[c], pair, dragged
        )
        for k, v in enumerate(fields):
            out[k * CELLS + c : k * CELLS + c + 1, :] = v
            half[k * CELLS + c : k * CELLS + c + 1, :] = v
    out[HALF : HALF + NB, :] = outer[OUTER + 3 * NB : OUTER + 4 * NB, :]
    out[HALF + NB : HALF + 2 * NB, :] = first[...]


def lists_second(right, left, first, send):
    return [(left, HALF + 2 * NB), (first, 0)] + [(send, HALF + NB * c) for c in range(3)] + [(right, HALF + NB)]


def early_second_kernel(parity, frame, other, right, left, first, send, out):
    early(parity, {0: frame, 1: other}, lists_second(right, left, first, send), out)


def middle_second_kernel(parity, frame, outer, right, left, first, send, gathered, rho, pair):
    density(parity, {-1: (outer, 0), 0: (frame, 0)}, lists_second(right, left, first, send), rho, pair, gathered)


def outer_second_kernel(parity, frame, other, outer, right, before, first, send, pair, after, rho, dragged):
    lists = [(before, OUTER + NB * (2 + c)) for c in range(5)] + [(right, HALF)]
    density(parity, {-1: (outer, SENT), 0: (outer, 0), 1: (frame, 0)}, lists, rho)
    lists = [(first, 0)] + [(send, HALF + NB * c) for c in range(3)]
    drag(parity, frame, {-1: outer, 0: frame, 1: other}, lists, pair, dragged)


def force_second_kernel(
    parity, home, frame, rho_outer, rho_own, rho_other, first, send, pair, dragged, pos_out, vel_out, rho_out, part
):
    numbers = numbers_of(parity)
    lists = [(first, 0), (send, HALF), (send, HALF + NB), (send, HALF + 2 * NB)]
    devices = lax.broadcasted_iota(jnp.int32, (S, S), 0)
    shells = lax.broadcasted_iota(jnp.int32, (16, S), 0)
    owners, shares = [], []
    for c in range(CELLS):
        (x, y, m, vx, vy, live), rho = force(
            c, numbers, frame, {-1: rho_outer, 0: rho_own, 1: rho_other}, lists[c], pair, dragged
        )
        pos_out[c : c + 1, :] = x
        pos_out[CELLS + c : CELLS + c + 1, :] = y
        vel_out[c : c + 1, :] = vx
        vel_out[CELLS + c : CELLS + c + 1, :] = vy
        rho_out[c : c + 1, :] = rho
        loads = (m * vx, m * vy, m * (sound_sq * (rho - 1.0)), 0.5 * m * (vx * vx + vy * vy))
        owner = (devices == home[c : c + 1, :]).astype(jnp.bfloat16)
        member = shells == home[CELLS + c : CELLS + c + 1, :]
        rest = jnp.concatenate([jnp.where(member, load, 0.0) for load in loads], axis=0)
        for _ in range(3):
            some = rest.astype(jnp.bfloat16)
            owners.append(owner)
            shares.append(some)
            rest = rest - some.astype(jnp.float32)
    total = lax.dot_general(
        jnp.concatenate(owners, axis=1),
        jnp.concatenate(shares, axis=1),
        (((1,), (1,)), ((), ())),
        preferred_element_type=jnp.float32,
    )
    part[...] = jnp.concatenate([total, jnp.zeros((S, S - 64), jnp.float32)], axis=1)


def soil_kernel(arrived, soil, pos, vel, rho, stress_out, pos_out, vel_out, rho_out):
    pos_out[...] = pos[...]
    vel_out[...] = vel[...]
    rho_out[...] = rho[...]
    stress = [soil[k] for k in range(4)]
    rate = [soil[4 + k] for k in range(3)]
    couple = [soil[7 + k] for k in range(3)]
    total = jnp.sum(arrived[...], axis=0, keepdims=True)
    lane = lax.broadcasted_iota(jnp.int32, (16, S), 1)
    row = lax.broadcasted_iota(jnp.int32, (16, S), 0)
    force_x, force_y, force_p, force_e = [
        jnp.sum(jnp.where(lane == row + 16 * k, total, 0.0), axis=1, keepdims=True) for k in range(4)
    ]
    exx = rate[0] + couple[0] * force_x
    eyy = rate[1] + couple[1] * force_y
    exy = rate[2] + couple[2] * force_p
    ezz = -0.5 * (couple[0] + couple[1]) * force_e
    trace = exx + eyy + ezz
    sxx = stress[0] + soil_dt * (2.0 * shear_mod * (exx - trace / 3.0) + bulk_mod * trace)
    syy = stress[1] + soil_dt * (2.0 * shear_mod * (eyy - trace / 3.0) + bulk_mod * trace)
    szz = stress[2] + soil_dt * (2.0 * shear_mod * (ezz - trace / 3.0) + bulk_mod * trace)
    sxy = stress[3] + soil_dt * 2.0 * shear_mod * exy
    first = sxx + syy + szz
    mean = first / 3.0
    dxx = sxx - mean
    dyy = syy - mean
    dzz = szz - mean
    root = jnp.sqrt(0.5 * (dxx * dxx + dyy * dyy + dzz * dzz) + sxy * sxy)
    radius = jnp.maximum(cohesion - friction * first, 0.2 * cohesion)
    factor = radius / jnp.maximum(root, radius)
    stress_out[0] = mean + factor * dxx
    stress_out[1] = mean + factor * dyy
    stress_out[2] = mean + factor * dzz
    stress_out[3] = factor * sxy


def rows_of(n):
    return jax.ShapeDtypeStruct((n, S), jnp.float32)


def kept(n):
    return pltpu.VMEM((n, S), jnp.float32)


VM = pl.BlockSpec(memory_space=pltpu.MemorySpace.VMEM)
SM = pl.BlockSpec(memory_space=pltpu.MemorySpace.SMEM)


def held(a):
    return pltpu.with_memory_space_constraint(a, pltpu.MemorySpace.VMEM)


def local(
    fluid_pos,
    fluid_vel,
    fluid_mass,
    cell_count,
    nb_list,
    iface_dest,
    iface_shell,
    soil_stress,
    soil_rate,
    soil_couple,
):
    n_depth = lax.axis_size("depth")
    n_azim = lax.axis_size("azim")
    parity = (lax.axis_index("depth") % 2).astype(jnp.int32).reshape(1)
    toward_left = [(i, (i - 1) % n_azim) for i in range(n_azim)]
    toward_right = [(i, (i + 1) % n_azim) for i in range(n_azim)]
    pairs = [(i, i ^ 1) for i in range(n_depth)]
    facing = [(i, i + 1 if i % 2 else i - 1) for i in range(n_depth)]
    facing = [(i, j) for i, j in facing if 0 <= j < n_depth]

    def call(kernel, name, shapes, *args):
        return pl.pallas_call(
            kernel,
            out_shape=tuple(kept(n) for n in shapes),
            in_specs=[SM] + [VM] * len(args),
            out_specs=(VM,) * len(shapes),
            name=name,
        )(parity, *[held(a) for a in args])

    def merged(first, second):
        halves = [a[:HALF].reshape(6, CELLS, S) for a in (first, second)]
        return jnp.concatenate(halves, axis=1).reshape(6 * WIDE, S)

    def crossing(step):
        return [
            (r * n_azim + c, (r ^ 1) * n_azim + (c + step) % n_azim) for r in range(n_depth) for c in range(n_azim)
        ]

    def swapped(a):
        return lax.ppermute(a, "depth", pairs)

    send, half, first, home, soil = pl.pallas_call(
        pack_kernel,
        out_shape=(
            kept(HALF + 3 * NB),
            kept(HALF),
            kept(NB),
            pltpu.VMEM((2 * CELLS, S), jnp.int32),
            pltpu.VMEM((10,) + soil_stress.shape[1:], jnp.float32),
        ),
        in_specs=[SM] + [VM] * 9,
        out_specs=(VM,) * 5,
        name="pack",
    )(
        cell_count,
        fluid_pos.reshape(2 * CELLS, S),
        fluid_vel.reshape(2 * CELLS, S),
        fluid_mass.reshape(CELLS, S),
        nb_list.reshape(NB * CELLS, S),
        iface_dest.reshape(CELLS, S),
        iface_shell.reshape(CELLS, S),
        soil_stress,
        soil_rate,
        soil_couple,
    )
    left = lax.ppermute(send, "azim", toward_right)
    across = lax.ppermute(half, ("depth", "azim"), crossing(1))
    beside = swapped(half)
    left, across = lax.optimization_barrier((left, across))
    frame = merged(left, send)
    other = merged(across, beside)
    outer = lax.ppermute(
        jnp.concatenate([frame[:SENT], other[:PLACE], left[HALF:], first, send[HALF:]], axis=0), "depth", facing
    )
    tiles = CELLS * NT
    (gathered,) = call(
        early_first_kernel, "early_first", (RING * NT * EARLY,), frame, other, left, first, send
    )
    rho_own, pair = call(
        middle_first_kernel, "middle_first", (WIDE, tiles * PAIR), frame, outer, left, first, send, gathered
    )
    rho_other = swapped(rho_own)
    rho_outer, dragged = call(
        outer_first_kernel, "outer_first", (WIDE, tiles * 8), frame, other, outer, left, first, send, pair, rho_own
    )
    mid, half = call(
        force_first_kernel,
        "force_first",
        (HALF + 2 * NB, HALF),
        frame, outer, rho_outer, rho_own, rho_other, left, first, send, pair, dragged,
    )

    right = lax.ppermute(mid, "azim", toward_left)
    across = lax.ppermute(half, ("depth", "azim"), crossing(-1))
    beside = swapped(half)
    right, across = lax.optimization_barrier((right, across))
    frame = merged(mid, right)
    other = merged(beside, across)
    beyond = lax.ppermute(jnp.concatenate([frame[:SENT], other[:PLACE]], axis=0), "depth", facing)
    (gathered,) = call(
        early_second_kernel, "early_second", (RING * NT * EARLY,), frame, other, right, left, first, send
    )
    rho_own, pair = call(
        middle_second_kernel, "middle_second", (WIDE, tiles * PAIR), frame, beyond, right, left, first, send, gathered
    )
    rho_other = swapped(rho_own)
    rho_outer, dragged = call(
        outer_second_kernel,
        "outer_second",
        (WIDE, tiles * 8),
        frame, other, beyond, right, outer, first, send, pair, rho_own,
    )
    pos, vel, rho, part = call(
        force_second_kernel,
        "force_second",
        (2 * CELLS, 2 * CELLS, CELLS, S),
        home, frame, rho_outer, rho_own, rho_other, first, send, pair, dragged,
    )

    arrived = lax.all_to_all(part, ("depth", "azim"), split_axis=0, concat_axis=0, tiled=True)
    stress_out, pos, vel, rho = pl.pallas_call(
        soil_kernel,
        out_shape=(
            jax.ShapeDtypeStruct(soil_stress.shape, jnp.float32), rows_of(2 * CELLS), rows_of(2 * CELLS), rows_of(CELLS)
        ),
        in_specs=[VM] * 5,
        out_specs=(VM, VM, VM, VM),
        name="soil",
    )(*[held(a) for a in (arrived, soil, pos, vel, rho)])
    return (
        pos.reshape(fluid_pos.shape),
        vel.reshape(fluid_vel.shape),
        rho.reshape(fluid_mass.shape),
        stress_out,
    )


def solution(mesh):
    return jax.shard_map(
        local,
        mesh=mesh,
        in_specs=(
            P(None, "depth", "azim", None),
            P(None, "depth", "azim", None),
            P("depth", "azim", None),
            P("depth", "azim"),
            P(None, "depth", "azim", None),
            P(("depth", "azim"), None, None),
            P(("depth", "azim"), None),
            P(None, ("depth", "azim"), None),
            P(None, ("depth", "azim"), None),
            P(None, ("depth", "azim"), None),
        ),
        out_specs=(
            P(None, "depth", "azim", None),
            P(None, "depth", "azim", None),
            P("depth", "azim", None),
            P(None, ("depth", "azim"), None),
        ),
        check_vma=False,
    )
```

```python
import jax
import jax.numpy as jnp
from jax import lax
from jax.experimental import pallas as pl
from jax.experimental.pallas import tpu as pltpu
from jax.sharding import PartitionSpec as P

step_dt = 0.05
sound_sq = 1.0
visc_alpha = 0.5
soil_dt = 0.1
shear_mod = 1.0
bulk_mod = 2.0
cohesion = 1.0
friction = 0.3

CELLS = 4
NB = 24
NT = 3
WIDE = 8
RING = 6
S = 128
LISTS = NB * CELLS
PX, PY, PM, PVX, PVY, PL = range(6)
HALF = 6 * CELLS
SENT = 5 * WIDE
PLACE = 3 * WIDE
PAIR = 32
EARLY = 24
NEAR = [(dr, dc) for dr in (-1, 0, 1) for dc in (-1, 0, 1)]


def pack_kernel(count, pos, vel, mass, nb, out, half, first):
    lane = lax.broadcasted_iota(jnp.int32, (1, S), 1)
    out[0 : 2 * CELLS, :] = pos[...]
    out[PVX * CELLS : (PVX + 2) * CELLS, :] = vel[...]
    half[0 : 2 * CELLS, :] = pos[...]
    half[PVX * CELLS : (PVX + 2) * CELLS, :] = vel[...]
    for c in range(CELLS):
        live = (lane < count[0, c]).astype(jnp.float32)
        out[PM * CELLS + c : PM * CELLS + c + 1, :] = mass[c : c + 1, :] * live
        out[PL * CELLS + c : PL * CELLS + c + 1, :] = live
        codes = nb[pl.ds(c, NB, stride=CELLS), :].astype(jnp.float32)
        half[PM * CELLS + c : PM * CELLS + c + 1, :] = mass[c : c + 1, :] * live
        half[PL * CELLS + c : PL * CELLS + c + 1, :] = live
        if c:
            out[HALF + NB * (c - 1) : HALF + NB * c, :] = codes
        else:
            first[...] = codes


def spread(row):
    return jnp.broadcast_to(row, (8, S))


def pick(tables, slot, masks, out=None):
    for table, mask in zip(tables, masks):
        got = jnp.take_along_axis(table, slot, axis=1)
        out = got if out is None else jnp.where(mask, got, out)
    return out


def numbers_of(parity):
    sign = 1 - 2 * parity[0]
    return [3 * (1 + sign * dr) + dc + 1 for dr, dc in NEAR]


def decode(ref, start, numbers):
    code = ref[start : start + 8, :].astype(jnp.int32)
    which = code >> 7
    return code & (S - 1), which, [which == n for n in numbers]


def early(parity, rows, lists, out):
    numbers = numbers_of(parity)[3:]
    for k in range(RING):
        ref, start = lists[k]
        for t in range(NT):
            slot, _, masks = decode(ref, start + 8 * t, numbers)
            for f in (PX, PY, PM):
                tables = []
                for dr, dc in NEAR[3:]:
                    at = f * WIDE + k + 1 + dc
                    tables.append(spread(rows[dr][at : at + 1, :]))
                base = (k * NT + t) * EARLY + 8 * f
                out[base : base + 8, :] = pick(tables, slot, masks)


def density(parity, rows, lists, rho_out, pair=None, gathered=None):
    near = NEAR if gathered is None else NEAR[:3]
    numbers = numbers_of(parity)[: len(near)]
    rho_out[...] = jnp.zeros((WIDE, S), jnp.float32)
    for k in range(RING):
        col = k + 1
        ref, start = rows[0]
        own_x, own_y = spread(ref[start + col : start + col + 1, :]), spread(ref[start + WIDE + col : start + WIDE + col + 1, :])
        own_m = ref[start + PM * WIDE + col : start + PM * WIDE + col + 1, :]

        def table(f):
            out = []
            for dr, dc in near:
                r, base = rows[dr]
                at = base + f * WIDE + col + dc
                out.append(spread(r[at : at + 1, :]))
            return out

        xs, ys, ms = table(PX), table(PY), table(PM)
        total = jnp.zeros((8, S), jnp.float32)
        ref, start = lists[k]
        for t in range(NT):
            slot, which, masks = decode(ref, start + 8 * t, numbers)
            third = (which * 11) >> 5
            before = [None] * 3
            if gathered is not None:
                base = (k * NT + t) * EARLY
                before = [gathered[base + 8 * f : base + 8 * f + 8, :] for f in range(3)]
            dx = own_x - ((third - 1).astype(jnp.float32) + pick(xs, slot, masks, before[0]))
            dy = own_y - ((which - 3 * third - 1).astype(jnp.float32) + pick(ys, slot, masks, before[1]))
            mass = pick(ms, slot, masks, before[2])
            dist = jnp.sqrt(dx * dx + dy * dy)
            tail = jnp.maximum(1.0 - dist, 0.0)
            cube = tail * tail * tail
            total = total + mass * (cube * tail * (4.0 * dist + 1.0))
            if pair is not None and 1 <= k <= CELLS:
                base = ((k - 1) * NT + t) * PAIR
                pair[base : base + 8, :] = dx
                pair[base + 8 : base + 16, :] = dy
                pair[base + 16 : base + 24, :] = dist * dist + 0.01
                pair[base + 24 : base + 32, :] = mass * (20.0 * cube)
        rho = own_m + jnp.sum(total, axis=0, keepdims=True) + jnp.where(own_m > 0.0, 0.0, 1.0)
        rho_out[col : col + 1, :] = rho


def term(rho):
    return sound_sq * (rho - 1.0) / (rho * rho)


def drag(parity, frame, states, lists, pair, out):
    numbers = numbers_of(parity)
    for c in range(CELLS):
        col = c + 2
        ref, start = lists[c]

        def table(f):
            return [spread(states[dr][f * WIDE + col + dc : f * WIDE + col + dc + 1, :]) for dr, dc in NEAR]

        own_vx = spread(frame[PVX * WIDE + col : PVX * WIDE + col + 1, :])
        own_vy = spread(frame[PVY * WIDE + col : PVY * WIDE + col + 1, :])
        vxs, vys = table(PVX), table(PVY)
        for t in range(NT):
            slot, _, masks = decode(ref, start + 8 * t, numbers)
            base = (c * NT + t) * PAIR
            dx = pair[base : base + 8, :]
            dy = pair[base + 8 : base + 16, :]
            vdot = (own_vx - pick(vxs, slot, masks)) * dx + (own_vy - pick(vys, slot, masks)) * dy
            base = (c * NT + t) * 8
            out[base : base + 8, :] = visc_alpha * jnp.maximum(-vdot, 0.0) / pair[4 * base + 16 : 4 * base + 24, :]


def force(c, numbers, frame, rhos, lists, pair, dragged):
    col = c + 2
    ref, start = lists

    def own(f):
        return frame[f * WIDE + col : f * WIDE + col + 1, :]

    own_rho = rhos[0][col : col + 1, :]
    own_q, own_r = spread(term(own_rho)), spread(own_rho)
    tables = [spread(rhos[dr][col + dc : col + dc + 1, :]) for dr, dc in NEAR]
    ax = jnp.zeros((8, S), jnp.float32)
    ay = jnp.zeros((8, S), jnp.float32)
    for t in range(NT):
        slot, _, masks = decode(ref, start + 8 * t, numbers)
        base = (c * NT + t) * PAIR
        rho = pick(tables, slot, masks)
        visc = dragged[base // 4 : base // 4 + 8, :] / (0.5 * (own_r + rho))
        coef = (own_q + term(rho) + visc) * pair[base + 24 : base + 32, :]
        ax = ax + coef * pair[base : base + 8, :]
        ay = ay + coef * pair[base + 8 : base + 16, :]
    live = own(PL)
    vx = own(PVX) + step_dt * jnp.sum(ax, axis=0, keepdims=True) * live
    vy = own(PVY) + step_dt * jnp.sum(ay, axis=0, keepdims=True) * live
    x = own(PX) + step_dt * vx * live
    y = own(PY) + step_dt * vy * live
    return (x, y, own(PM), vx, vy, live), own_rho


OUTER = SENT + PLACE


def lists_first(left, first, send):
    return [(left, HALF + NB * c) for c in range(3)] + [(first, 0), (send, HALF), (send, HALF + NB)]


def early_first_kernel(parity, frame, other, left, first, send, dest, shell, stress, rate, couple, out, home, soil):
    home[0:CELLS, :] = dest[...]
    home[CELLS : 2 * CELLS, :] = shell[...]
    soil[0:4] = stress[...]
    soil[4:7] = rate[...]
    soil[7:10] = couple[...]
    early(parity, {0: frame, 1: other}, lists_first(left, first, send), out)


def middle_first_kernel(parity, frame, outer, left, first, send, gathered, rho, pair):
    density(parity, {-1: (outer, 0), 0: (frame, 0)}, lists_first(left, first, send), rho, pair, gathered)


def outer_first_kernel(parity, frame, other, outer, left, first, send, pair, after, rho, dragged):
    lists = [(outer, OUTER + NB * k) for k in range(RING)]
    density(parity, {-1: (outer, SENT), 0: (outer, 0), 1: (frame, 0)}, lists, rho)
    drag(parity, frame, {-1: outer, 0: frame, 1: other}, lists_first(left, first, send)[1:], pair, dragged)


def force_first_kernel(parity, frame, outer, rho_outer, rho_own, rho_other, left, first, send, pair, dragged, out, half):
    numbers = numbers_of(parity)
    lists = lists_first(left, first, send)[1:]
    for c in range(CELLS):
        fields, _ = force(
            c, numbers, frame, {-1: rho_outer, 0: rho_own, 1: rho_other}, lists[c], pair, dragged
        )
        for k, v in enumerate(fields):
            out[k * CELLS + c : k * CELLS + c + 1, :] = v
            half[k * CELLS + c : k * CELLS + c + 1, :] = v
    out[HALF : HALF + NB, :] = outer[OUTER + 3 * NB : OUTER + 4 * NB, :]
    out[HALF + NB : HALF + 2 * NB, :] = first[...]


def lists_second(right, left, first, send):
    return [(left, HALF + 2 * NB), (first, 0)] + [(send, HALF + NB * c) for c in range(3)] + [(right, HALF + NB)]


def early_second_kernel(parity, frame, other, right, left, first, send, out):
    early(parity, {0: frame, 1: other}, lists_second(right, left, first, send), out)


def middle_second_kernel(parity, frame, outer, right, left, first, send, gathered, rho, pair):
    density(parity, {-1: (outer, 0), 0: (frame, 0)}, lists_second(right, left, first, send), rho, pair, gathered)


def outer_second_kernel(parity, frame, other, outer, right, before, first, send, pair, after, rho, dragged):
    lists = [(before, OUTER + NB * (2 + c)) for c in range(5)] + [(right, HALF)]
    density(parity, {-1: (outer, SENT), 0: (outer, 0), 1: (frame, 0)}, lists, rho)
    lists = [(first, 0)] + [(send, HALF + NB * c) for c in range(3)]
    drag(parity, frame, {-1: outer, 0: frame, 1: other}, lists, pair, dragged)


def force_second_kernel(
    parity, home, frame, rho_outer, rho_own, rho_other, first, send, pair, dragged, pos_out, vel_out, rho_out, part
):
    numbers = numbers_of(parity)
    lists = [(first, 0), (send, HALF), (send, HALF + NB), (send, HALF + 2 * NB)]
    devices = lax.broadcasted_iota(jnp.int32, (S, S), 0)
    shells = lax.broadcasted_iota(jnp.int32, (16, S), 0)
    owners, shares = [], []
    for c in range(CELLS):
        (x, y, m, vx, vy, live), rho = force(
            c, numbers, frame, {-1: rho_outer, 0: rho_own, 1: rho_other}, lists[c], pair, dragged
        )
        pos_out[c : c + 1, :] = x
        pos_out[CELLS + c : CELLS + c + 1, :] = y
        vel_out[c : c + 1, :] = vx
        vel_out[CELLS + c : CELLS + c + 1, :] = vy
        rho_out[c : c + 1, :] = rho
        loads = (m * vx, m * vy, m * (sound_sq * (rho - 1.0)), 0.5 * m * (vx * vx + vy * vy))
        owner = (devices == home[c : c + 1, :]).astype(jnp.bfloat16)
        member = shells == home[CELLS + c : CELLS + c + 1, :]
        rest = jnp.concatenate([jnp.where(member, load, 0.0) for load in loads], axis=0)
        for _ in range(3):
            some = rest.astype(jnp.bfloat16)
            owners.append(owner)
            shares.append(some)
            rest = rest - some.astype(jnp.float32)
    total = lax.dot_general(
        jnp.concatenate(owners, axis=1),
        jnp.concatenate(shares, axis=1),
        (((1,), (1,)), ((), ())),
        preferred_element_type=jnp.float32,
    )
    part[...] = jnp.concatenate([total, jnp.zeros((S, S - 64), jnp.float32)], axis=1)


def soil_kernel(arrived, soil, pos, vel, rho, stress_out, pos_out, vel_out, rho_out):
    pos_out[...] = pos[...]
    vel_out[...] = vel[...]
    rho_out[...] = rho[...]
    stress = [soil[k] for k in range(4)]
    rate = [soil[4 + k] for k in range(3)]
    couple = [soil[7 + k] for k in range(3)]
    total = jnp.sum(arrived[...], axis=0, keepdims=True)
    lane = lax.broadcasted_iota(jnp.int32, (16, S), 1)
    row = lax.broadcasted_iota(jnp.int32, (16, S), 0)
    force_x, force_y, force_p, force_e = [
        jnp.sum(jnp.where(lane == row + 16 * k, total, 0.0), axis=1, keepdims=True) for k in range(4)
    ]
    exx = rate[0] + couple[0] * force_x
    eyy = rate[1] + couple[1] * force_y
    exy = rate[2] + couple[2] * force_p
    ezz = -0.5 * (couple[0] + couple[1]) * force_e
    trace = exx + eyy + ezz
    sxx = stress[0] + soil_dt * (2.0 * shear_mod * (exx - trace / 3.0) + bulk_mod * trace)
    syy = stress[1] + soil_dt * (2.0 * shear_mod * (eyy - trace / 3.0) + bulk_mod * trace)
    szz = stress[2] + soil_dt * (2.0 * shear_mod * (ezz - trace / 3.0) + bulk_mod * trace)
    sxy = stress[3] + soil_dt * 2.0 * shear_mod * exy
    first = sxx + syy + szz
    mean = first / 3.0
    dxx = sxx - mean
    dyy = syy - mean
    dzz = szz - mean
    root = jnp.sqrt(0.5 * (dxx * dxx + dyy * dyy + dzz * dzz) + sxy * sxy)
    radius = jnp.maximum(cohesion - friction * first, 0.2 * cohesion)
    factor = radius / jnp.maximum(root, radius)
    stress_out[0] = mean + factor * dxx
    stress_out[1] = mean + factor * dyy
    stress_out[2] = mean + factor * dzz
    stress_out[3] = factor * sxy


def rows_of(n):
    return jax.ShapeDtypeStruct((n, S), jnp.float32)


def kept(n):
    return pltpu.VMEM((n, S), jnp.float32)


VM = pl.BlockSpec(memory_space=pltpu.MemorySpace.VMEM)
SM = pl.BlockSpec(memory_space=pltpu.MemorySpace.SMEM)


def held(a):
    return pltpu.with_memory_space_constraint(a, pltpu.MemorySpace.VMEM)


def local(
    fluid_pos,
    fluid_vel,
    fluid_mass,
    cell_count,
    nb_list,
    iface_dest,
    iface_shell,
    soil_stress,
    soil_rate,
    soil_couple,
):
    n_depth = lax.axis_size("depth")
    n_azim = lax.axis_size("azim")
    parity = (lax.axis_index("depth") % 2).astype(jnp.int32).reshape(1)
    toward_left = [(i, (i - 1) % n_azim) for i in range(n_azim)]
    toward_right = [(i, (i + 1) % n_azim) for i in range(n_azim)]
    pairs = [(i, i ^ 1) for i in range(n_depth)]
    facing = [(i, i + 1 if i % 2 else i - 1) for i in range(n_depth)]
    facing = [(i, j) for i, j in facing if 0 <= j < n_depth]

    def call(kernel, name, shapes, *args):
        return pl.pallas_call(
            kernel,
            out_shape=tuple(kept(n) for n in shapes),
            in_specs=[SM] + [VM] * len(args),
            out_specs=(VM,) * len(shapes),
            name=name,
        )(parity, *[held(a) for a in args])

    def merged(first, second):
        halves = [a[:HALF].reshape(6, CELLS, S) for a in (first, second)]
        return jnp.concatenate(halves, axis=1).reshape(6 * WIDE, S)

    def crossing(step):
        return [
            (r * n_azim + c, (r ^ 1) * n_azim + (c + step) % n_azim) for r in range(n_depth) for c in range(n_azim)
        ]

    def swapped(a):
        return lax.ppermute(a, "depth", pairs)

    send, half, first = pl.pallas_call(
        pack_kernel,
        out_shape=(
            kept(HALF + 3 * NB),
            kept(HALF),
            kept(NB),
        ),
        in_specs=[SM] + [VM] * 4,
        out_specs=(VM,) * 3,
        name="pack",
    )(
        cell_count,
        fluid_pos.reshape(2 * CELLS, S),
        fluid_vel.reshape(2 * CELLS, S),
        fluid_mass.reshape(CELLS, S),
        nb_list.reshape(NB * CELLS, S),
    )
    left = lax.ppermute(send, "azim", toward_right)
    across = lax.ppermute(half, ("depth", "azim"), crossing(1))
    beside = swapped(half)
    left, across = lax.optimization_barrier((left, across))
    frame = merged(left, send)
    other = merged(across, beside)
    outer = lax.ppermute(
        jnp.concatenate([frame[:SENT], other[:PLACE], left[HALF:], first, send[HALF:]], axis=0), "depth", facing
    )
    tiles = CELLS * NT
    later = (iface_dest.reshape(CELLS, S), iface_shell.reshape(CELLS, S), soil_stress, soil_rate, soil_couple)
    gathered, home, soil = pl.pallas_call(
        early_first_kernel,
        out_shape=(
            kept(RING * NT * EARLY),
            pltpu.VMEM((2 * CELLS, S), jnp.int32),
            pltpu.VMEM((10,) + soil_stress.shape[1:], jnp.float32),
        ),
        in_specs=[SM] + [VM] * 10,
        out_specs=(VM,) * 3,
        name="early_first",
    )(parity, *[held(a) for a in (frame, other, left, first, send)], *later)
    rho_own, pair = call(
        middle_first_kernel, "middle_first", (WIDE, tiles * PAIR), frame, outer, left, first, send, gathered
    )
    rho_other = swapped(rho_own)
    rho_outer, dragged = call(
        outer_first_kernel, "outer_first", (WIDE, tiles * 8), frame, other, outer, left, first, send, pair, rho_own
    )
    mid, half = call(
        force_first_kernel,
        "force_first",
        (HALF + 2 * NB, HALF),
        frame, outer, rho_outer, rho_own, rho_other, left, first, send, pair, dragged,
    )

    right = lax.ppermute(mid, "azim", toward_left)
    across = lax.ppermute(half, ("depth", "azim"), crossing(-1))
    beside = swapped(half)
    right, across = lax.optimization_barrier((right, across))
    frame = merged(mid, right)
    other = merged(beside, across)
    beyond = lax.ppermute(jnp.concatenate([frame[:SENT], other[:PLACE]], axis=0), "depth", facing)
    (gathered,) = call(
        early_second_kernel, "early_second", (RING * NT * EARLY,), frame, other, right, left, first, send
    )
    rho_own, pair = call(
        middle_second_kernel, "middle_second", (WIDE, tiles * PAIR), frame, beyond, right, left, first, send, gathered
    )
    rho_other = swapped(rho_own)
    rho_outer, dragged = call(
        outer_second_kernel,
        "outer_second",
        (WIDE, tiles * 8),
        frame, other, beyond, right, outer, first, send, pair, rho_own,
    )
    pos, vel, rho, part = call(
        force_second_kernel,
        "force_second",
        (2 * CELLS, 2 * CELLS, CELLS, S),
        home, frame, rho_outer, rho_own, rho_other, first, send, pair, dragged,
    )

    arrived = lax.all_to_all(part, ("depth", "azim"), split_axis=0, concat_axis=0, tiled=True)
    stress_out, pos, vel, rho = pl.pallas_call(
        soil_kernel,
        out_shape=(
            jax.ShapeDtypeStruct(soil_stress.shape, jnp.float32), rows_of(2 * CELLS), rows_of(2 * CELLS), rows_of(CELLS)
        ),
        in_specs=[VM] * 5,
        out_specs=(VM, VM, VM, VM),
        name="soil",
    )(*[held(a) for a in (arrived, soil, pos, vel, rho)])
    return (
        pos.reshape(fluid_pos.shape),
        vel.reshape(fluid_vel.shape),
        rho.reshape(fluid_mass.shape),
        stress_out,
    )


def solution(mesh):
    return jax.shard_map(
        local,
        mesh=mesh,
        in_specs=(
            P(None, "depth", "azim", None),
            P(None, "depth", "azim", None),
            P("depth", "azim", None),
            P("depth", "azim"),
            P(None, "depth", "azim", None),
            P(("depth", "azim"), None, None),
            P(("depth", "azim"), None),
            P(None, ("depth", "azim"), None),
            P(None, ("depth", "azim"), None),
            P(None, ("depth", "azim"), None),
        ),
        out_specs=(
            P(None, "depth", "azim", None),
            P(None, "depth", "azim", None),
            P("depth", "azim", None),
            P(None, ("depth", "azim"), None),
        ),
        check_vma=False,
    )
```

```python
import jax
import jax.numpy as jnp
from jax import lax
from jax.experimental import pallas as pl
from jax.experimental.pallas import tpu as pltpu
from jax.sharding import PartitionSpec as P

step_dt = 0.05
sound_sq = 1.0
visc_alpha = 0.5
soil_dt = 0.1
shear_mod = 1.0
bulk_mod = 2.0
cohesion = 1.0
friction = 0.3

CELLS = 4
NB = 24
NT = 3
WIDE = 8
RING = 6
S = 128
LISTS = NB * CELLS
PX, PY, PM, PVX, PVY, PL = range(6)
HALF = 6 * CELLS
SENT = 5 * WIDE
PLACE = 3 * WIDE
PAIR = 32
EARLY = 24
NEAR = [(dr, dc) for dr in (-1, 0, 1) for dc in (-1, 0, 1)]


def pack_kernel(count, pos, vel, mass, nb, dest, shell, stress, rate, couple, out, half, first, home, soil):
    soil[0:4] = stress[...]
    soil[4:7] = rate[...]
    soil[7:10] = couple[...]
    home[0:CELLS, :] = dest[...]
    home[CELLS : 2 * CELLS, :] = shell[...]
    lane = lax.broadcasted_iota(jnp.int32, (1, S), 1)
    out[0 : 2 * CELLS, :] = pos[...]
    out[PVX * CELLS : (PVX + 2) * CELLS, :] = vel[...]
    half[0 : 2 * CELLS, :] = pos[...]
    half[PVX * CELLS : (PVX + 2) * CELLS, :] = vel[...]
    for c in range(CELLS):
        live = (lane < count[0, c]).astype(jnp.float32)
        out[PM * CELLS + c : PM * CELLS + c + 1, :] = mass[c : c + 1, :] * live
        out[PL * CELLS + c : PL * CELLS + c + 1, :] = live
        codes = nb[pl.ds(c, NB, stride=CELLS), :].astype(jnp.float32)
        half[PM * CELLS + c : PM * CELLS + c + 1, :] = mass[c : c + 1, :] * live
        half[PL * CELLS + c : PL * CELLS + c + 1, :] = live
        if c:
            out[HALF + NB * (c - 1) : HALF + NB * c, :] = codes
        else:
            first[...] = codes


def spread(row):
    return jnp.broadcast_to(row, (8, S))


def pick(tables, slot, masks, out=None):
    for table, mask in zip(tables, masks):
        got = jnp.take_along_axis(table, slot, axis=1)
        out = got if out is None else jnp.where(mask, got, out)
    return out


def numbers_of(parity):
    sign = 1 - 2 * parity[0]
    return [3 * (1 + sign * dr) + dc + 1 for dr, dc in NEAR]


def decode(ref, start, numbers):
    code = ref[start : start + 8, :].astype(jnp.int32)
    which = code >> 7
    return code & (S - 1), which, [which == n for n in numbers]


def early(parity, rows, lists, out):
    numbers = numbers_of(parity)[3:]
    for k in range(RING):
        ref, start = lists[k]
        for t in range(NT):
            slot, _, masks = decode(ref, start + 8 * t, numbers)
            for f in (PX, PY, PM):
                tables = []
                for dr, dc in NEAR[3:]:
                    at = f * WIDE + k + 1 + dc
                    tables.append(spread(rows[dr][at : at + 1, :]))
                base = (k * NT + t) * EARLY + 8 * f
                out[base : base + 8, :] = pick(tables, slot, masks)


def density(parity, rows, lists, rho_out, pair=None, gathered=None):
    near = NEAR if gathered is None else NEAR[:3]
    numbers = numbers_of(parity)[: len(near)]
    rho_out[...] = jnp.zeros((WIDE, S), jnp.float32)
    for k in range(RING):
        col = k + 1
        ref, start = rows[0]
        own_x, own_y = spread(ref[start + col : start + col + 1, :]), spread(ref[start + WIDE + col : start + WIDE + col + 1, :])
        own_m = ref[start + PM * WIDE + col : start + PM * WIDE + col + 1, :]

        def table(f):
            out = []
            for dr, dc in near:
                r, base = rows[dr]
                at = base + f * WIDE + col + dc
                out.append(spread(r[at : at + 1, :]))
            return out

        xs, ys, ms = table(PX), table(PY), table(PM)
        total = jnp.zeros((8, S), jnp.float32)
        ref, start = lists[k]
        for t in range(NT):
            slot, which, masks = decode(ref, start + 8 * t, numbers)
            third = (which * 11) >> 5
            before = [None] * 3
            if gathered is not None:
                base = (k * NT + t) * EARLY
                before = [gathered[base + 8 * f : base + 8 * f + 8, :] for f in range(3)]
            dx = own_x - ((third - 1).astype(jnp.float32) + pick(xs, slot, masks, before[0]))
            dy = own_y - ((which - 3 * third - 1).astype(jnp.float32) + pick(ys, slot, masks, before[1]))
            mass = pick(ms, slot, masks, before[2])
            dist = jnp.sqrt(dx * dx + dy * dy)
            tail = jnp.maximum(1.0 - dist, 0.0)
            cube = tail * tail * tail
            total = total + mass * (cube * tail * (4.0 * dist + 1.0))
            if pair is not None and 1 <= k <= CELLS:
                base = ((k - 1) * NT + t) * PAIR
                pair[base : base + 8, :] = dx
                pair[base + 8 : base + 16, :] = dy
                pair[base + 16 : base + 24, :] = dist * dist + 0.01
                pair[base + 24 : base + 32, :] = mass * (20.0 * cube)
        rho = own_m + jnp.sum(total, axis=0, keepdims=True) + jnp.where(own_m > 0.0, 0.0, 1.0)
        rho_out[col : col + 1, :] = rho


def term(rho):
    return sound_sq * (rho - 1.0) / (rho * rho)


def drag(parity, frame, states, lists, pair, out):
    numbers = numbers_of(parity)
    for c in range(CELLS):
        col = c + 2
        ref, start = lists[c]

        def table(f):
            return [spread(states[dr][f * WIDE + col + dc : f * WIDE + col + dc + 1, :]) for dr, dc in NEAR]

        own_vx = spread(frame[PVX * WIDE + col : PVX * WIDE + col + 1, :])
        own_vy = spread(frame[PVY * WIDE + col : PVY * WIDE + col + 1, :])
        vxs, vys = table(PVX), table(PVY)
        for t in range(NT):
            slot, _, masks = decode(ref, start + 8 * t, numbers)
            base = (c * NT + t) * PAIR
            dx = pair[base : base + 8, :]
            dy = pair[base + 8 : base + 16, :]
            vdot = (own_vx - pick(vxs, slot, masks)) * dx + (own_vy - pick(vys, slot, masks)) * dy
            base = (c * NT + t) * 8
            out[base : base + 8, :] = visc_alpha * jnp.maximum(-vdot, 0.0) / pair[4 * base + 16 : 4 * base + 24, :]


def force(c, numbers, frame, rhos, lists, pair, dragged):
    col = c + 2
    ref, start = lists

    def own(f):
        return frame[f * WIDE + col : f * WIDE + col + 1, :]

    own_rho = rhos[0][col : col + 1, :]
    own_q, own_r = spread(term(own_rho)), spread(own_rho)
    tables = [spread(rhos[dr][col + dc : col + dc + 1, :]) for dr, dc in NEAR]
    ax = jnp.zeros((8, S), jnp.float32)
    ay = jnp.zeros((8, S), jnp.float32)
    for t in range(NT):
        slot, _, masks = decode(ref, start + 8 * t, numbers)
        base = (c * NT + t) * PAIR
        rho = pick(tables, slot, masks)
        visc = dragged[base // 4 : base // 4 + 8, :] / (0.5 * (own_r + rho))
        coef = (own_q + term(rho) + visc) * pair[base + 24 : base + 32, :]
        ax = ax + coef * pair[base : base + 8, :]
        ay = ay + coef * pair[base + 8 : base + 16, :]
    live = own(PL)
    vx = own(PVX) + step_dt * jnp.sum(ax, axis=0, keepdims=True) * live
    vy = own(PVY) + step_dt * jnp.sum(ay, axis=0, keepdims=True) * live
    x = own(PX) + step_dt * vx * live
    y = own(PY) + step_dt * vy * live
    return (x, y, own(PM), vx, vy, live), own_rho


OUTER = SENT + PLACE


def lists_first(left, first, send):
    return [(left, HALF + NB * c) for c in range(3)] + [(first, 0), (send, HALF), (send, HALF + NB)]


def early_first_kernel(parity, frame, other, left, first, send, out):
    early(parity, {0: frame, 1: other}, lists_first(left, first, send), out)


def middle_first_kernel(parity, frame, outer, left, first, send, gathered, rho, pair):
    density(parity, {-1: (outer, 0), 0: (frame, 0)}, lists_first(left, first, send), rho, pair, gathered)


def outer_first_kernel(parity, frame, other, outer, left, first, send, pair, after, rho, dragged):
    lists = [(outer, OUTER + NB * k) for k in range(RING)]
    density(parity, {-1: (outer, SENT), 0: (outer, 0), 1: (frame, 0)}, lists, rho)
    drag(parity, frame, {-1: outer, 0: frame, 1: other}, lists_first(left, first, send)[1:], pair, dragged)


def force_first_kernel(parity, frame, outer, rho_outer, rho_own, rho_other, left, first, send, pair, dragged, out, half):
    numbers = numbers_of(parity)
    lists = lists_first(left, first, send)[1:]
    for c in range(CELLS):
        fields, _ = force(
            c, numbers, frame, {-1: rho_outer, 0: rho_own, 1: rho_other}, lists[c], pair, dragged
        )
        for k, v in enumerate(fields):
            out[k * CELLS + c : k * CELLS + c + 1, :] = v
            half[k * CELLS + c : k * CELLS + c + 1, :] = v
    out[HALF : HALF + NB, :] = outer[OUTER + 3 * NB : OUTER + 4 * NB, :]
    out[HALF + NB : HALF + 2 * NB, :] = first[...]


def lists_second(right, left, first, send):
    return [(left, HALF + 2 * NB), (first, 0)] + [(send, HALF + NB * c) for c in range(3)] + [(right, HALF + NB)]


def early_second_kernel(parity, frame, other, right, left, first, send, home, out, owners):
    early(parity, {0: frame, 1: other}, lists_second(right, left, first, send), out)
    devices = lax.broadcasted_iota(jnp.int32, (S, S), 0)
    for c in range(CELLS):
        owners[:, S * c : S * (c + 1)] = (devices == home[c : c + 1, :]).astype(jnp.bfloat16)


def middle_second_kernel(parity, frame, outer, right, left, first, send, gathered, rho, pair):
    density(parity, {-1: (outer, 0), 0: (frame, 0)}, lists_second(right, left, first, send), rho, pair, gathered)


def outer_second_kernel(parity, frame, other, outer, right, before, first, send, pair, after, rho, dragged):
    lists = [(before, OUTER + NB * (2 + c)) for c in range(5)] + [(right, HALF)]
    density(parity, {-1: (outer, SENT), 0: (outer, 0), 1: (frame, 0)}, lists, rho)
    lists = [(first, 0)] + [(send, HALF + NB * c) for c in range(3)]
    drag(parity, frame, {-1: outer, 0: frame, 1: other}, lists, pair, dragged)


def force_second_kernel(
    parity, home, frame, rho_outer, rho_own, rho_other, first, send, pair, dragged, owners, pos_out, vel_out, rho_out, part
):
    numbers = numbers_of(parity)
    lists = [(first, 0), (send, HALF), (send, HALF + NB), (send, HALF + 2 * NB)]
    shells = lax.broadcasted_iota(jnp.int32, (16, S), 0)
    shares = [[], [], []]
    for c in range(CELLS):
        (x, y, m, vx, vy, live), rho = force(
            c, numbers, frame, {-1: rho_outer, 0: rho_own, 1: rho_other}, lists[c], pair, dragged
        )
        pos_out[c : c + 1, :] = x
        pos_out[CELLS + c : CELLS + c + 1, :] = y
        vel_out[c : c + 1, :] = vx
        vel_out[CELLS + c : CELLS + c + 1, :] = vy
        rho_out[c : c + 1, :] = rho
        loads = (m * vx, m * vy, m * (sound_sq * (rho - 1.0)), 0.5 * m * (vx * vx + vy * vy))
        member = shells == home[CELLS + c : CELLS + c + 1, :]
        rest = jnp.concatenate([jnp.where(member, load, 0.0) for load in loads], axis=0)
        for share in shares:
            share.append(rest.astype(jnp.bfloat16))
            rest = rest - share[-1].astype(jnp.float32)
    high, middle, low = [jnp.concatenate(share, axis=1) for share in shares]
    none = jnp.zeros_like(low)
    total = lax.dot_general(
        jnp.concatenate([owners[...], owners[...]], axis=1),
        jnp.concatenate(
            [jnp.concatenate(pair_of, axis=1) for pair_of in ((high, low), (none, none), (middle, none), (none, none))], axis=0
        ),
        (((1,), (1,)), ((), ())),
        preferred_element_type=jnp.float32,
    )
    part[...] = total[:, :S] + total[:, S:]


def soil_kernel(arrived, soil, pos, vel, rho, stress_out, pos_out, vel_out, rho_out):
    pos_out[...] = pos[...]
    vel_out[...] = vel[...]
    rho_out[...] = rho[...]
    stress = [soil[k] for k in range(4)]
    rate = [soil[4 + k] for k in range(3)]
    couple = [soil[7 + k] for k in range(3)]
    total = jnp.sum(arrived[...], axis=0, keepdims=True)
    lane = lax.broadcasted_iota(jnp.int32, (16, S), 1)
    row = lax.broadcasted_iota(jnp.int32, (16, S), 0)
    force_x, force_y, force_p, force_e = [
        jnp.sum(jnp.where(lane == row + 16 * k, total, 0.0), axis=1, keepdims=True) for k in range(4)
    ]
    exx = rate[0] + couple[0] * force_x
    eyy = rate[1] + couple[1] * force_y
    exy = rate[2] + couple[2] * force_p
    ezz = -0.5 * (couple[0] + couple[1]) * force_e
    trace = exx + eyy + ezz
    sxx = stress[0] + soil_dt * (2.0 * shear_mod * (exx - trace / 3.0) + bulk_mod * trace)
    syy = stress[1] + soil_dt * (2.0 * shear_mod * (eyy - trace / 3.0) + bulk_mod * trace)
    szz = stress[2] + soil_dt * (2.0 * shear_mod * (ezz - trace / 3.0) + bulk_mod * trace)
    sxy = stress[3] + soil_dt * 2.0 * shear_mod * exy
    first = sxx + syy + szz
    mean = first / 3.0
    dxx = sxx - mean
    dyy = syy - mean
    dzz = szz - mean
    root = jnp.sqrt(0.5 * (dxx * dxx + dyy * dyy + dzz * dzz) + sxy * sxy)
    radius = jnp.maximum(cohesion - friction * first, 0.2 * cohesion)
    factor = radius / jnp.maximum(root, radius)
    stress_out[0] = mean + factor * dxx
    stress_out[1] = mean + factor * dyy
    stress_out[2] = mean + factor * dzz
    stress_out[3] = factor * sxy


def rows_of(n):
    return jax.ShapeDtypeStruct((n, S), jnp.float32)


def kept(n):
    return pltpu.VMEM((n, S), jnp.float32)


VM = pl.BlockSpec(memory_space=pltpu.MemorySpace.VMEM)
SM = pl.BlockSpec(memory_space=pltpu.MemorySpace.SMEM)


def held(a):
    return pltpu.with_memory_space_constraint(a, pltpu.MemorySpace.VMEM)


def local(
    fluid_pos,
    fluid_vel,
    fluid_mass,
    cell_count,
    nb_list,
    iface_dest,
    iface_shell,
    soil_stress,
    soil_rate,
    soil_couple,
):
    n_depth = lax.axis_size("depth")
    n_azim = lax.axis_size("azim")
    parity = (lax.axis_index("depth") % 2).astype(jnp.int32).reshape(1)
    toward_left = [(i, (i - 1) % n_azim) for i in range(n_azim)]
    toward_right = [(i, (i + 1) % n_azim) for i in range(n_azim)]
    pairs = [(i, i ^ 1) for i in range(n_depth)]
    facing = [(i, i + 1 if i % 2 else i - 1) for i in range(n_depth)]
    facing = [(i, j) for i, j in facing if 0 <= j < n_depth]

    def call(kernel, name, shapes, *args):
        return pl.pallas_call(
            kernel,
            out_shape=tuple(kept(n) if isinstance(n, int) else n for n in shapes),
            in_specs=[SM] + [VM] * len(args),
            out_specs=(VM,) * len(shapes),
            name=name,
        )(parity, *[held(a) for a in args])

    def merged(first, second):
        halves = [a[:HALF].reshape(6, CELLS, S) for a in (first, second)]
        return jnp.concatenate(halves, axis=1).reshape(6 * WIDE, S)

    def crossing(step):
        return [
            (r * n_azim + c, (r ^ 1) * n_azim + (c + step) % n_azim) for r in range(n_depth) for c in range(n_azim)
        ]

    def swapped(a):
        return lax.ppermute(a, "depth", pairs)

    send, half, first, home, soil = pl.pallas_call(
        pack_kernel,
        out_shape=(
            kept(HALF + 3 * NB),
            kept(HALF),
            kept(NB),
            pltpu.VMEM((2 * CELLS, S), jnp.int32),
            pltpu.VMEM((10,) + soil_stress.shape[1:], jnp.float32),
        ),
        in_specs=[SM] + [VM] * 9,
        out_specs=(VM,) * 5,
        name="pack",
    )(
        cell_count,
        fluid_pos.reshape(2 * CELLS, S),
        fluid_vel.reshape(2 * CELLS, S),
        fluid_mass.reshape(CELLS, S),
        nb_list.reshape(NB * CELLS, S),
        iface_dest.reshape(CELLS, S),
        iface_shell.reshape(CELLS, S),
        soil_stress,
        soil_rate,
        soil_couple,
    )
    left = lax.ppermute(send, "azim", toward_right)
    across = lax.ppermute(half, ("depth", "azim"), crossing(1))
    beside = swapped(half)
    left, across = lax.optimization_barrier((left, across))
    frame = merged(left, send)
    other = merged(across, beside)
    outer = lax.ppermute(
        jnp.concatenate([frame[:SENT], other[:PLACE], left[HALF:], first, send[HALF:]], axis=0), "depth", facing
    )
    tiles = CELLS * NT
    (gathered,) = call(
        early_first_kernel, "early_first", (RING * NT * EARLY,), frame, other, left, first, send
    )
    rho_own, pair = call(
        middle_first_kernel, "middle_first", (WIDE, tiles * PAIR), frame, outer, left, first, send, gathered
    )
    rho_other = swapped(rho_own)
    rho_outer, dragged = call(
        outer_first_kernel, "outer_first", (WIDE, tiles * 8), frame, other, outer, left, first, send, pair, rho_own
    )
    mid, half = call(
        force_first_kernel,
        "force_first",
        (HALF + 2 * NB, HALF),
        frame, outer, rho_outer, rho_own, rho_other, left, first, send, pair, dragged,
    )

    right = lax.ppermute(mid, "azim", toward_left)
    across = lax.ppermute(half, ("depth", "azim"), crossing(-1))
    beside = swapped(half)
    right, across = lax.optimization_barrier((right, across))
    frame = merged(mid, right)
    other = merged(beside, across)
    beyond = lax.ppermute(jnp.concatenate([frame[:SENT], other[:PLACE]], axis=0), "depth", facing)
    gathered, owners = call(
        early_second_kernel,
        "early_second",
        (RING * NT * EARLY, pltpu.VMEM((S, CELLS * S), jnp.bfloat16)),
        frame, other, right, left, first, send, home,
    )
    rho_own, pair = call(
        middle_second_kernel, "middle_second", (WIDE, tiles * PAIR), frame, beyond, right, left, first, send, gathered
    )
    rho_other = swapped(rho_own)
    rho_outer, dragged = call(
        outer_second_kernel,
        "outer_second",
        (WIDE, tiles * 8),
        frame, other, beyond, right, outer, first, send, pair, rho_own,
    )
    pos, vel, rho, part = call(
        force_second_kernel,
        "force_second",
        (2 * CELLS, 2 * CELLS, CELLS, S),
        home, frame, rho_outer, rho_own, rho_other, first, send, pair, dragged, owners,
    )

    arrived = lax.all_to_all(part, ("depth", "azim"), split_axis=0, concat_axis=0, tiled=True)
    stress_out, pos, vel, rho = pl.pallas_call(
        soil_kernel,
        out_shape=(
            jax.ShapeDtypeStruct(soil_stress.shape, jnp.float32), rows_of(2 * CELLS), rows_of(2 * CELLS), rows_of(CELLS)
        ),
        in_specs=[VM] * 5,
        out_specs=(VM, VM, VM, VM),
        name="soil",
    )(*[held(a) for a in (arrived, soil, pos, vel, rho)])
    return (
        pos.reshape(fluid_pos.shape),
        vel.reshape(fluid_vel.shape),
        rho.reshape(fluid_mass.shape),
        stress_out,
    )


def solution(mesh):
    return jax.shard_map(
        local,
        mesh=mesh,
        in_specs=(
            P(None, "depth", "azim", None),
            P(None, "depth", "azim", None),
            P("depth", "azim", None),
            P("depth", "azim"),
            P(None, "depth", "azim", None),
            P(("depth", "azim"), None, None),
            P(("depth", "azim"), None),
            P(None, ("depth", "azim"), None),
            P(None, ("depth", "azim"), None),
            P(None, ("depth", "azim"), None),
        ),
        out_specs=(
            P(None, "depth", "azim", None),
            P(None, "depth", "azim", None),
            P("depth", "azim", None),
            P(None, ("depth", "azim"), None),
        ),
        check_vma=False,
    )
```

```python
import jax
import jax.numpy as jnp
from jax import lax
from jax.experimental import pallas as pl
from jax.experimental.pallas import tpu as pltpu
from jax.sharding import PartitionSpec as P

step_dt = 0.05
sound_sq = 1.0
visc_alpha = 0.5
soil_dt = 0.1
shear_mod = 1.0
bulk_mod = 2.0
cohesion = 1.0
friction = 0.3

CELLS = 4
NB = 24
NT = 3
WIDE = 8
RING = 6
S = 128
LISTS = NB * CELLS
PX, PY, PM, PVX, PVY, PL = range(6)
HALF = 6 * CELLS
SENT = 5 * WIDE
PLACE = 3 * WIDE
PAIR = 32
EARLY = 24
NEAR = [(dr, dc) for dr in (-1, 0, 1) for dc in (-1, 0, 1)]


def pack_kernel(count, pos, vel, mass, nb, out, half, first):
    lane = lax.broadcasted_iota(jnp.int32, (1, S), 1)
    out[0 : 2 * CELLS, :] = pos[...]
    out[PVX * CELLS : (PVX + 2) * CELLS, :] = vel[...]
    half[0 : 2 * CELLS, :] = pos[...]
    half[PVX * CELLS : (PVX + 2) * CELLS, :] = vel[...]
    for c in range(CELLS):
        live = (lane < count[0, c]).astype(jnp.float32)
        out[PM * CELLS + c : PM * CELLS + c + 1, :] = mass[c : c + 1, :] * live
        out[PL * CELLS + c : PL * CELLS + c + 1, :] = live
        codes = nb[pl.ds(c, NB, stride=CELLS), :].astype(jnp.float32)
        half[PM * CELLS + c : PM * CELLS + c + 1, :] = mass[c : c + 1, :] * live
        half[PL * CELLS + c : PL * CELLS + c + 1, :] = live
        if c:
            out[HALF + NB * (c - 1) : HALF + NB * c, :] = codes
        else:
            first[...] = codes


def spread(row):
    return jnp.broadcast_to(row, (8, S))


def pick(tables, slot, masks, out=None):
    for table, mask in zip(tables, masks):
        got = jnp.take_along_axis(table, slot, axis=1)
        out = got if out is None else jnp.where(mask, got, out)
    return out


def numbers_of(parity):
    sign = 1 - 2 * parity[0]
    return [3 * (1 + sign * dr) + dc + 1 for dr, dc in NEAR]


def decode(ref, start, numbers):
    code = ref[start : start + 8, :].astype(jnp.int32)
    which = code >> 7
    return code & (S - 1), which, [which == n for n in numbers]


def early(parity, rows, lists, out):
    numbers = numbers_of(parity)[3:]
    for k in range(RING):
        ref, start = lists[k]
        for t in range(NT):
            slot, _, masks = decode(ref, start + 8 * t, numbers)
            for f in (PX, PY, PM):
                tables = []
                for dr, dc in NEAR[3:]:
                    at = f * WIDE + k + 1 + dc
                    tables.append(spread(rows[dr][at : at + 1, :]))
                base = (k * NT + t) * EARLY + 8 * f
                out[base : base + 8, :] = pick(tables, slot, masks)


def density(parity, rows, lists, rho_out, pair=None, gathered=None):
    near = NEAR if gathered is None else NEAR[:3]
    numbers = numbers_of(parity)[: len(near)]
    rho_out[...] = jnp.zeros((WIDE, S), jnp.float32)
    for k in range(RING):
        col = k + 1
        ref, start = rows[0]
        own_x, own_y = spread(ref[start + col : start + col + 1, :]), spread(ref[start + WIDE + col : start + WIDE + col + 1, :])
        own_m = ref[start + PM * WIDE + col : start + PM * WIDE + col + 1, :]

        def table(f):
            out = []
            for dr, dc in near:
                r, base = rows[dr]
                at = base + f * WIDE + col + dc
                out.append(spread(r[at : at + 1, :]))
            return out

        xs, ys, ms = table(PX), table(PY), table(PM)
        total = jnp.zeros((8, S), jnp.float32)
        ref, start = lists[k]
        for t in range(NT):
            slot, which, masks = decode(ref, start + 8 * t, numbers)
            third = (which * 11) >> 5
            before = [None] * 3
            if gathered is not None:
                base = (k * NT + t) * EARLY
                before = [gathered[base + 8 * f : base + 8 * f + 8, :] for f in range(3)]
            dx = own_x - ((third - 1).astype(jnp.float32) + pick(xs, slot, masks, before[0]))
            dy = own_y - ((which - 3 * third - 1).astype(jnp.float32) + pick(ys, slot, masks, before[1]))
            mass = pick(ms, slot, masks, before[2])
            dist = jnp.sqrt(dx * dx + dy * dy)
            tail = jnp.maximum(1.0 - dist, 0.0)
            cube = tail * tail * tail
            total = total + mass * (cube * tail * (4.0 * dist + 1.0))
            if pair is not None and 1 <= k <= CELLS:
                base = ((k - 1) * NT + t) * PAIR
                pair[base : base + 8, :] = dx
                pair[base + 8 : base + 16, :] = dy
                pair[base + 16 : base + 24, :] = dist * dist + 0.01
                pair[base + 24 : base + 32, :] = mass * (20.0 * cube)
        rho = own_m + jnp.sum(total, axis=0, keepdims=True) + jnp.where(own_m > 0.0, 0.0, 1.0)
        rho_out[col : col + 1, :] = rho


def term(rho):
    return sound_sq * (rho - 1.0) / (rho * rho)


def drag(parity, frame, states, lists, pair, out):
    numbers = numbers_of(parity)
    for c in range(CELLS):
        col = c + 2
        ref, start = lists[c]

        def table(f):
            return [spread(states[dr][f * WIDE + col + dc : f * WIDE + col + dc + 1, :]) for dr, dc in NEAR]

        own_vx = spread(frame[PVX * WIDE + col : PVX * WIDE + col + 1, :])
        own_vy = spread(frame[PVY * WIDE + col : PVY * WIDE + col + 1, :])
        vxs, vys = table(PVX), table(PVY)
        for t in range(NT):
            slot, _, masks = decode(ref, start + 8 * t, numbers)
            base = (c * NT + t) * PAIR
            dx = pair[base : base + 8, :]
            dy = pair[base + 8 : base + 16, :]
            vdot = (own_vx - pick(vxs, slot, masks)) * dx + (own_vy - pick(vys, slot, masks)) * dy
            base = (c * NT + t) * 8
            out[base : base + 8, :] = visc_alpha * jnp.maximum(-vdot, 0.0) / pair[4 * base + 16 : 4 * base + 24, :]


def force(c, numbers, frame, rhos, lists, pair, dragged):
    col = c + 2
    ref, start = lists

    def own(f):
        return frame[f * WIDE + col : f * WIDE + col + 1, :]

    own_rho = rhos[0][col : col + 1, :]
    own_q, own_r = spread(term(own_rho)), spread(own_rho)
    tables = [spread(rhos[dr][col + dc : col + dc + 1, :]) for dr, dc in NEAR]
    ax = jnp.zeros((8, S), jnp.float32)
    ay = jnp.zeros((8, S), jnp.float32)
    for t in range(NT):
        slot, _, masks = decode(ref, start + 8 * t, numbers)
        base = (c * NT + t) * PAIR
        rho = pick(tables, slot, masks)
        visc = dragged[base // 4 : base // 4 + 8, :] / (0.5 * (own_r + rho))
        coef = (own_q + term(rho) + visc) * pair[base + 24 : base + 32, :]
        ax = ax + coef * pair[base : base + 8, :]
        ay = ay + coef * pair[base + 8 : base + 16, :]
    live = own(PL)
    vx = own(PVX) + step_dt * jnp.sum(ax, axis=0, keepdims=True) * live
    vy = own(PVY) + step_dt * jnp.sum(ay, axis=0, keepdims=True) * live
    x = own(PX) + step_dt * vx * live
    y = own(PY) + step_dt * vy * live
    return (x, y, own(PM), vx, vy, live), own_rho


OUTER = SENT + PLACE


def lists_first(left, first, send):
    return [(left, HALF + NB * c) for c in range(3)] + [(first, 0), (send, HALF), (send, HALF + NB)]


def early_first_kernel(parity, frame, other, left, first, send, dest, shell, stress, rate, couple, out, home, soil):
    home[0:CELLS, :] = dest[...]
    home[CELLS : 2 * CELLS, :] = shell[...]
    soil[0:4] = stress[...]
    soil[4:7] = rate[...]
    soil[7:10] = couple[...]
    early(parity, {0: frame, 1: other}, lists_first(left, first, send), out)


def middle_first_kernel(parity, frame, outer, left, first, send, gathered, rho, pair):
    density(parity, {-1: (outer, 0), 0: (frame, 0)}, lists_first(left, first, send), rho, pair, gathered)


def outer_first_kernel(parity, frame, other, outer, left, first, send, pair, after, rho, dragged):
    lists = [(outer, OUTER + NB * k) for k in range(RING)]
    density(parity, {-1: (outer, SENT), 0: (outer, 0), 1: (frame, 0)}, lists, rho)
    drag(parity, frame, {-1: outer, 0: frame, 1: other}, lists_first(left, first, send)[1:], pair, dragged)


def force_first_kernel(parity, frame, outer, rho_outer, rho_own, rho_other, left, first, send, pair, dragged, out, half):
    numbers = numbers_of(parity)
    lists = lists_first(left, first, send)[1:]
    for c in range(CELLS):
        fields, _ = force(
            c, numbers, frame, {-1: rho_outer, 0: rho_own, 1: rho_other}, lists[c], pair, dragged
        )
        for k, v in enumerate(fields):
            out[k * CELLS + c : k * CELLS + c + 1, :] = v
            half[k * CELLS + c : k * CELLS + c + 1, :] = v
    out[HALF : HALF + NB, :] = outer[OUTER + 3 * NB : OUTER + 4 * NB, :]
    out[HALF + NB : HALF + 2 * NB, :] = first[...]


def lists_second(right, left, first, send):
    return [(left, HALF + 2 * NB), (first, 0)] + [(send, HALF + NB * c) for c in range(3)] + [(right, HALF + NB)]


def early_second_kernel(parity, frame, other, right, left, first, send, home, out, owners):
    early(parity, {0: frame, 1: other}, lists_second(right, left, first, send), out)
    devices = lax.broadcasted_iota(jnp.int32, (S, S), 0)
    for c in range(CELLS):
        owners[:, S * c : S * (c + 1)] = (devices == home[c : c + 1, :]).astype(jnp.bfloat16)


def middle_second_kernel(parity, frame, outer, right, left, first, send, gathered, rho, pair):
    density(parity, {-1: (outer, 0), 0: (frame, 0)}, lists_second(right, left, first, send), rho, pair, gathered)


def outer_second_kernel(parity, frame, other, outer, right, before, first, send, pair, after, rho, dragged):
    lists = [(before, OUTER + NB * (2 + c)) for c in range(5)] + [(right, HALF)]
    density(parity, {-1: (outer, SENT), 0: (outer, 0), 1: (frame, 0)}, lists, rho)
    lists = [(first, 0)] + [(send, HALF + NB * c) for c in range(3)]
    drag(parity, frame, {-1: outer, 0: frame, 1: other}, lists, pair, dragged)


def force_second_kernel(
    parity, home, frame, rho_outer, rho_own, rho_other, first, send, pair, dragged, owners, pos_out, vel_out, rho_out, part
):
    numbers = numbers_of(parity)
    lists = [(first, 0), (send, HALF), (send, HALF + NB), (send, HALF + 2 * NB)]
    shells = lax.broadcasted_iota(jnp.int32, (16, S), 0)
    shares = [[], [], []]
    for c in range(CELLS):
        (x, y, m, vx, vy, live), rho = force(
            c, numbers, frame, {-1: rho_outer, 0: rho_own, 1: rho_other}, lists[c], pair, dragged
        )
        pos_out[c : c + 1, :] = x
        pos_out[CELLS + c : CELLS + c + 1, :] = y
        vel_out[c : c + 1, :] = vx
        vel_out[CELLS + c : CELLS + c + 1, :] = vy
        rho_out[c : c + 1, :] = rho
        loads = (m * vx, m * vy, m * (sound_sq * (rho - 1.0)), 0.5 * m * (vx * vx + vy * vy))
        member = shells == home[CELLS + c : CELLS + c + 1, :]
        rest = jnp.concatenate([jnp.where(member, load, 0.0) for load in loads], axis=0)
        for share in shares:
            share.append(rest.astype(jnp.bfloat16))
            rest = rest - share[-1].astype(jnp.float32)
    high, middle, low = [jnp.concatenate(share, axis=1) for share in shares]
    none = jnp.zeros_like(low)
    total = lax.dot_general(
        jnp.concatenate([owners[...], owners[...]], axis=1),
        jnp.concatenate(
            [jnp.concatenate(pair_of, axis=1) for pair_of in ((high, low), (none, none), (middle, none), (none, none))], axis=0
        ),
        (((1,), (1,)), ((), ())),
        preferred_element_type=jnp.float32,
    )
    part[...] = total[:, :S] + total[:, S:]


def soil_kernel(arrived, soil, pos, vel, rho, stress_out, pos_out, vel_out, rho_out):
    pos_out[...] = pos[...]
    vel_out[...] = vel[...]
    rho_out[...] = rho[...]
    stress = [soil[k] for k in range(4)]
    rate = [soil[4 + k] for k in range(3)]
    couple = [soil[7 + k] for k in range(3)]
    total = jnp.sum(arrived[...], axis=0, keepdims=True)
    lane = lax.broadcasted_iota(jnp.int32, (16, S), 1)
    row = lax.broadcasted_iota(jnp.int32, (16, S), 0)
    force_x, force_y, force_p, force_e = [
        jnp.sum(jnp.where(lane == row + 16 * k, total, 0.0), axis=1, keepdims=True) for k in range(4)
    ]
    exx = rate[0] + couple[0] * force_x
    eyy = rate[1] + couple[1] * force_y
    exy = rate[2] + couple[2] * force_p
    ezz = -0.5 * (couple[0] + couple[1]) * force_e
    trace = exx + eyy + ezz
    sxx = stress[0] + soil_dt * (2.0 * shear_mod * (exx - trace / 3.0) + bulk_mod * trace)
    syy = stress[1] + soil_dt * (2.0 * shear_mod * (eyy - trace / 3.0) + bulk_mod * trace)
    szz = stress[2] + soil_dt * (2.0 * shear_mod * (ezz - trace / 3.0) + bulk_mod * trace)
    sxy = stress[3] + soil_dt * 2.0 * shear_mod * exy
    first = sxx + syy + szz
    mean = first / 3.0
    dxx = sxx - mean
    dyy = syy - mean
    dzz = szz - mean
    root = jnp.sqrt(0.5 * (dxx * dxx + dyy * dyy + dzz * dzz) + sxy * sxy)
    radius = jnp.maximum(cohesion - friction * first, 0.2 * cohesion)
    factor = radius / jnp.maximum(root, radius)
    stress_out[0] = mean + factor * dxx
    stress_out[1] = mean + factor * dyy
    stress_out[2] = mean + factor * dzz
    stress_out[3] = factor * sxy


def rows_of(n):
    return jax.ShapeDtypeStruct((n, S), jnp.float32)


def kept(n):
    return pltpu.VMEM((n, S), jnp.float32)


VM = pl.BlockSpec(memory_space=pltpu.MemorySpace.VMEM)
SM = pl.BlockSpec(memory_space=pltpu.MemorySpace.SMEM)


def held(a):
    return pltpu.with_memory_space_constraint(a, pltpu.MemorySpace.VMEM)


def local(
    fluid_pos,
    fluid_vel,
    fluid_mass,
    cell_count,
    nb_list,
    iface_dest,
    iface_shell,
    soil_stress,
    soil_rate,
    soil_couple,
):
    n_depth = lax.axis_size("depth")
    n_azim = lax.axis_size("azim")
    parity = (lax.axis_index("depth") % 2).astype(jnp.int32).reshape(1)
    toward_left = [(i, (i - 1) % n_azim) for i in range(n_azim)]
    toward_right = [(i, (i + 1) % n_azim) for i in range(n_azim)]
    pairs = [(i, i ^ 1) for i in range(n_depth)]
    facing = [(i, i + 1 if i % 2 else i - 1) for i in range(n_depth)]
    facing = [(i, j) for i, j in facing if 0 <= j < n_depth]

    def call(kernel, name, shapes, *args):
        return pl.pallas_call(
            kernel,
            out_shape=tuple(kept(n) if isinstance(n, int) else n for n in shapes),
            in_specs=[SM] + [VM] * len(args),
            out_specs=(VM,) * len(shapes),
            name=name,
        )(parity, *[held(a) for a in args])

    def merged(first, second):
        halves = [a[:HALF].reshape(6, CELLS, S) for a in (first, second)]
        return jnp.concatenate(halves, axis=1).reshape(6 * WIDE, S)

    def crossing(step):
        return [
            (r * n_azim + c, (r ^ 1) * n_azim + (c + step) % n_azim) for r in range(n_depth) for c in range(n_azim)
        ]

    def swapped(a):
        return lax.ppermute(a, "depth", pairs)

    send, half, first = pl.pallas_call(
        pack_kernel,
        out_shape=(
            kept(HALF + 3 * NB),
            kept(HALF),
            kept(NB),
        ),
        in_specs=[SM] + [VM] * 4,
        out_specs=(VM,) * 3,
        name="pack",
    )(
        cell_count,
        fluid_pos.reshape(2 * CELLS, S),
        fluid_vel.reshape(2 * CELLS, S),
        fluid_mass.reshape(CELLS, S),
        nb_list.reshape(NB * CELLS, S),
    )
    left = lax.ppermute(send, "azim", toward_right)
    across = lax.ppermute(half, ("depth", "azim"), crossing(1))
    beside = swapped(half)
    left, across = lax.optimization_barrier((left, across))
    frame = merged(left, send)
    other = merged(across, beside)
    outer = lax.ppermute(
        jnp.concatenate([frame[:SENT], other[:PLACE], left[HALF:], first, send[HALF:]], axis=0), "depth", facing
    )
    tiles = CELLS * NT
    later = (iface_dest.reshape(CELLS, S), iface_shell.reshape(CELLS, S), soil_stress, soil_rate, soil_couple)
    gathered, home, soil = pl.pallas_call(
        early_first_kernel,
        out_shape=(
            kept(RING * NT * EARLY),
            pltpu.VMEM((2 * CELLS, S), jnp.int32),
            pltpu.VMEM((10,) + soil_stress.shape[1:], jnp.float32),
        ),
        in_specs=[SM] + [VM] * 10,
        out_specs=(VM,) * 3,
        name="early_first",
    )(parity, *[held(a) for a in (frame, other, left, first, send)], *later)
    rho_own, pair = call(
        middle_first_kernel, "middle_first", (WIDE, tiles * PAIR), frame, outer, left, first, send, gathered
    )
    rho_other = swapped(rho_own)
    rho_outer, dragged = call(
        outer_first_kernel, "outer_first", (WIDE, tiles * 8), frame, other, outer, left, first, send, pair, rho_own
    )
    mid, half = call(
        force_first_kernel,
        "force_first",
        (HALF + 2 * NB, HALF),
        frame, outer, rho_outer, rho_own, rho_other, left, first, send, pair, dragged,
    )

    right = lax.ppermute(mid, "azim", toward_left)
    across = lax.ppermute(half, ("depth", "azim"), crossing(-1))
    beside = swapped(half)
    right, across = lax.optimization_barrier((right, across))
    frame = merged(mid, right)
    other = merged(beside, across)
    beyond = lax.ppermute(jnp.concatenate([frame[:SENT], other[:PLACE]], axis=0), "depth", facing)
    gathered, owners = call(
        early_second_kernel,
        "early_second",
        (RING * NT * EARLY, pltpu.VMEM((S, CELLS * S), jnp.bfloat16)),
        frame, other, right, left, first, send, home,
    )
    rho_own, pair = call(
        middle_second_kernel, "middle_second", (WIDE, tiles * PAIR), frame, beyond, right, left, first, send, gathered
    )
    rho_other = swapped(rho_own)
    rho_outer, dragged = call(
        outer_second_kernel,
        "outer_second",
        (WIDE, tiles * 8),
        frame, other, beyond, right, outer, first, send, pair, rho_own,
    )
    pos, vel, rho, part = call(
        force_second_kernel,
        "force_second",
        (2 * CELLS, 2 * CELLS, CELLS, S),
        home, frame, rho_outer, rho_own, rho_other, first, send, pair, dragged, owners,
    )

    arrived = lax.all_to_all(part, ("depth", "azim"), split_axis=0, concat_axis=0, tiled=True)
    stress_out, pos, vel, rho = pl.pallas_call(
        soil_kernel,
        out_shape=(
            jax.ShapeDtypeStruct(soil_stress.shape, jnp.float32), rows_of(2 * CELLS), rows_of(2 * CELLS), rows_of(CELLS)
        ),
        in_specs=[VM] * 5,
        out_specs=(VM, VM, VM, VM),
        name="soil",
    )(*[held(a) for a in (arrived, soil, pos, vel, rho)])
    return (
        pos.reshape(fluid_pos.shape),
        vel.reshape(fluid_vel.shape),
        rho.reshape(fluid_mass.shape),
        stress_out,
    )


def solution(mesh):
    return jax.shard_map(
        local,
        mesh=mesh,
        in_specs=(
            P(None, "depth", "azim", None),
            P(None, "depth", "azim", None),
            P("depth", "azim", None),
            P("depth", "azim"),
            P(None, "depth", "azim", None),
            P(("depth", "azim"), None, None),
            P(("depth", "azim"), None),
            P(None, ("depth", "azim"), None),
            P(None, ("depth", "azim"), None),
            P(None, ("depth", "azim"), None),
        ),
        out_specs=(
            P(None, "depth", "azim", None),
            P(None, "depth", "azim", None),
            P("depth", "azim", None),
            P(None, ("depth", "azim"), None),
        ),
        check_vma=False,
    )
```
